512 devices in a mesh: cluster: 64 (over y, z), member: 8 (over x, core).
Axes of the slice: x: 4, y: 4, z: 16, core: 2. Of those that a mesh axis runs over, the one named last changes fastest.
Arguments:
- leaf_centers: float32 [3, 512], replicated, may hold values from 0 to 1
- source_coords: float32 [3, 65536], P(None, ('cluster', 'member')), may hold values from -1 to 1
- target_points: float32 [3, 65536], P(None, ('cluster', 'member')), may hold values from 0 to 1
- charges: float32 [8, 65536], P(None, ('cluster', 'member')), may hold values from -6 to 6
- boundary_data: float32 [8, 65536], P(None, ('cluster', 'member')), may hold values from -6 to 6
- step_sizes: float32 [8], replicated, may hold values from 0.2 to 1
- valid_count: int32 [512], P(('cluster', 'member')), may hold values from 64 to 128, as said below
- near_lists: int32 [64, 26], replicated, may hold values from 0 to 63, as said below
Outputs:
- new_charges: float32 [8, 65536], P(None, ('cluster', 'member'))
- residual: float32 [8, 65536], P(None, ('cluster', 'member'))
The draws below stay inside these ranges and needn't reach their ends.
Inputs may be any that keep to these rules, and one draw needn't show every extreme that they name: `valid_count`: some leaf has 128 live slots and some has half of 128. `near_lists`: row c names 26 different clusters, none of them c.
All inputs are finite; a program needn't handle non-finite values.
Results may differ from the reference program's by a relative error of at most 0.0003.
Values sent between devices are 32-bit elements; how exact they have to be, the bound alone decides.
No kernel may reach another device: no remote copies, remote signals or barrier semaphores. Data moves between devices by JAX's collectives and lax.ppermute only.
A program may use at most 64 MiB of HBM per device.

```python
import math
import jax
import jax.numpy as jnp
import numpy as np
from jax import lax

LEAF = 128
FIELDS = 8
PROXIES = 32
ITERS = 2
NEAR = 26
CLUSTERS = 64
LEAVES = 512
POINTS = 65536
N_CLUSTER = 64
N_MEMBER = 8


def draw_valid_count(key, part):
    counts = jax.random.randint(key, (LEAVES,), LEAF // 2, LEAF + 1)
    order = jax.random.permutation(jax.random.fold_in(key, 7), LEAVES)
    counts = counts.at[order[0]].set(LEAF)
    counts = counts.at[order[1]].set(LEAF // 2)
    return counts.astype(jnp.int32)


def draw_near_lists(key, part):
    keys = jax.random.split(jax.random.fold_in(key, 11), CLUSTERS)

    def one_row(row_key):
        return jax.random.permutation(row_key, CLUSTERS - 1)[:NEAR] + 1
    offsets = jax.vmap(one_row)(keys)
    rows = (jnp.arange(CLUSTERS)[:, None] + offsets) % CLUSTERS
    return rows.astype(jnp.int32)


def steps_of(rng, dims, cuts, least, largest):
    def one(axis_at, blocks):
        draws = jax.random.uniform(jax.random.fold_in(jax.random.fold_in(rng, 6), axis_at), (blocks,), jnp.float32, least / len(cuts), largest / len(cuts))
        return jnp.repeat(jnp.exp(draws), dims[axis_at] // blocks).reshape((-1,) + (1,) * (len(dims) - axis_at - 1))

    gain = one(*cuts[0])
    for cut in cuts[1:]:
        gain = gain * one(*cut)
    return gain


def bell_draw(stream_key, shape, scale, most, cuts=(), kind=jnp.bfloat16):
    factor_of = steps_of(stream_key, shape, cuts, -0.22, 0.18) if cuts else 1.0
    array = jax.random.normal(stream_key, shape, jnp.float32) * scale * factor_of
    return jnp.minimum(jnp.maximum(array, -most), most).astype(kind)


def setup_inputs(seed: int = 0) -> dict:
    splits = jax.random.split(jax.random.key(seed), 9)
    leaf_centers = jnp.clip(jax.random.uniform(splits[0], (3, LEAVES), jnp.float32, 0.0, 1.0), 0.0, 1.0)
    source_coords = jnp.clip(jax.random.uniform(splits[1], (3, POINTS), jnp.float32, -1.0, 1.0) * steps_of(splits[1], (3, POINTS), ((1, 512),), -0.4, 0.0), -1.0, 1.0)
    target_points = jnp.clip(1.0 * jax.random.uniform(splits[2], (3, POINTS), jnp.float32) ** steps_of(splits[2], (3, POINTS), ((1, 512),), -0.2, 0.2), 0.0, 1.0)
    charges = bell_draw(splits[3], (FIELDS, POINTS), 1.0, 6.0, ((1, 512),), jnp.float32)
    boundary_data = bell_draw(splits[4], (FIELDS, POINTS), 1.0, 6.0, ((1, 512),), jnp.float32)
    step_sizes = jnp.clip(jnp.exp(jax.random.uniform(splits[5], (FIELDS,), jnp.float32, math.log(0.2), math.log(1.0))), 0.2, 1.0)
    valid_count = draw_valid_count(jax.random.fold_in(splits[8], 71), 0)
    near_lists = draw_near_lists(jax.random.fold_in(splits[8], 71), 0)
    return dict(leaf_centers=leaf_centers, source_coords=source_coords, target_points=target_points, charges=charges, boundary_data=boundary_data, step_sizes=step_sizes, valid_count=valid_count, near_lists=near_lists)


HALF_SIDE = 0.08
SOFTENING = 0.0025

def cheby_nodes(number):
    return np.cos(np.pi * (2 * np.arange(number) + 1) / (2 * number))

def basis_line(coord, number):
    nodes = cheby_nodes(number)
    factors = []
    for first in range(number):
        factor = jnp.ones_like(coord)
        for other in range(number):
            if other != first:
                factor = factor * (coord - nodes[other]) / (nodes[first] - nodes[other])
        factors.append(factor)
    return jnp.stack(factors, 0)

def lagrange(coords):
    along_x = basis_line(coords[0], 2)
    along_y = basis_line(coords[1], 4)
    along_z = basis_line(coords[2], 4)
    joined = along_x[:, None, None, :] * along_y[None, :, None, :] * along_z[None, None, :, :]
    return joined.reshape(32, coords.shape[1])

def proxy_grid():
    grid_x, grid_y, grid_z = np.meshgrid(cheby_nodes(2), cheby_nodes(4), cheby_nodes(4), indexing='ij')
    return jnp.asarray(np.stack([grid_x.reshape(-1), grid_y.reshape(-1), grid_z.reshape(-1)], 0), jnp.float32)

def potential(targets, sources, weights):
    target_count = targets.shape[1]
    source_count = sources.shape[1]
    limit = max(128, (1 << 20) // target_count)
    src_block = math.gcd(source_count, limit)

    def advance(turn, running):
        pts = lax.dynamic_slice_in_dim(sources, turn * src_block, src_block, 1)
        wts = lax.dynamic_slice_in_dim(weights, turn * src_block, src_block, 1)
        distance = (pts[0][:, None] - targets[0][None, :]) ** 2
        distance = distance + (pts[1][:, None] - targets[1][None, :]) ** 2
        distance = distance + (pts[2][:, None] - targets[2][None, :]) ** 2
        kernel = lax.rsqrt(distance + SOFTENING)
        return running + jnp.dot(wts, kernel, precision=lax.Precision.HIGHEST, preferred_element_type=jnp.float32)
    start_value = jnp.zeros((weights.shape[0], target_count), jnp.float32)
    return lax.fori_loop(0, source_count // src_block, advance, start_value)

def reference(leaf_centers, source_coords, target_points, charges, boundary_data, step_sizes, valid_count, near_lists):
    clusters = N_CLUSTER
    members = N_MEMBER
    span = members * LEAF
    live = (jnp.arange(LEAF, dtype=jnp.int32)[None, :] < valid_count[:, None]).astype(jnp.float32).reshape(-1)
    source_points = jnp.repeat(leaf_centers, LEAF, axis=1) + HALF_SIDE * source_coords
    interp = lagrange(source_coords)
    offsets = proxy_grid()
    proxy_points = (leaf_centers[:, :, None] + HALF_SIDE * offsets[:, None, :]).reshape(3, LEAVES * PROXIES)
    proxy_cluster = (jnp.arange(LEAVES * PROXIES, dtype=jnp.int32) // (members * PROXIES)).astype(jnp.int32)
    grouped_points = source_points.reshape(3, clusters, span)
    scale = 1.0 / math.sqrt(POINTS)
    current = charges * live
    residual = current
    for turn in range(ITERS):
        stacked_a = current.reshape(FIELDS, LEAVES, LEAF)
        stacked_b = interp.reshape(PROXIES, LEAVES, LEAF)
        proxy_charges = jnp.einsum('flj,plj->flp', stacked_a, stacked_b, precision=lax.Precision.HIGHEST).reshape(FIELDS, LEAVES * PROXIES)
        grouped_charges = current.reshape(FIELDS, clusters, span)

        def per_cluster(cluster_id):
            own_row = jnp.concatenate([cluster_id[None], near_lists[cluster_id]]).astype(jnp.int32)
            targets = lax.dynamic_slice_in_dim(target_points, cluster_id * span, span, 1)
            near_pts = jnp.take(grouped_points, own_row, axis=1).reshape(3, -1)
            near_wts = jnp.take(grouped_charges, own_row, axis=1).reshape(FIELDS, -1)
            far_ok = jnp.all(proxy_cluster[:, None] != own_row[None, :], axis=1).astype(jnp.float32)
            return potential(targets, near_pts, near_wts) + potential(targets, proxy_points, proxy_charges * far_ok[None, :])
        fields_all = lax.map(per_cluster, jnp.arange(clusters, dtype=jnp.int32))
        field = jnp.transpose(fields_all, (1, 0, 2)).reshape(FIELDS, POINTS) * scale
        residual = live * (boundary_data - field)
        current = live * (current + step_sizes[:, None] * residual / (1.0 + jnp.abs(residual)))
    return (current, residual)
```

```python
import functools
import math

import jax
import jax.numpy as jnp
import numpy as np
from jax import lax
from jax.experimental import pallas as pl
from jax.experimental.pallas import tpu as pltpu
from jax.sharding import Mesh
from jax.sharding import PartitionSpec as P

HALF_SIDE = 0.08
SOFTENING = 0.0025
NY, NZ, NX, NC = 4, 16, 4, 2
MEMBERS = NX * NC
PLANE = NY * MEMBERS
NEAR = 26
DEPTH = 48
ZERO_BLOCK = NZ
FAR_A = NZ + 1
A_BLOCKS = FAR_A + 4
FAR_Q = NZ + 1
Q_BLOCKS = FAR_Q + 4 * NY
SLOTS = 32
bf16, f32 = jnp.bfloat16, jnp.float32


def cheby_nodes(number):
    return np.cos(np.pi * (2 * np.arange(number) + 1) / (2 * number))


def pick(index, values):
    out = jnp.full(index.shape, float(values[0]), f32)
    for k in range(1, len(values)):
        out = jnp.where(index == k, float(values[k]), out)
    return out


def iota(shape, dim):
    return lax.broadcasted_iota(jnp.int32, shape, dim)


def split3(v):
    h = v.astype(bf16).astype(f32)
    r = v - h
    m = r.astype(bf16).astype(f32)
    low = (r - m).astype(bf16).astype(f32)
    return h, m, low


def split2(v):
    h = v.astype(bf16)
    return h, (v - h.astype(f32)).astype(bf16)


def source_rows(pts, extra):
    row = iota(pts.shape, 0)
    s = jnp.where(row < 3, pts - 0.5, 0.0)
    norm = jnp.sum(s * s, axis=0, keepdims=True) + SOFTENING
    return jnp.where(row < 3, -2.0 * s, jnp.where(row == 3, norm, jnp.where(row == 4, 1.0, extra)))


def target_rows(pts):
    row = iota(pts.shape, 0)
    t = jnp.where(row < 3, pts - 0.5, 0.0)
    norm = jnp.sum(t * t, axis=0, keepdims=True)
    return jnp.where(row < 3, t, jnp.where(row == 3, 1.0, jnp.where(row == 4, norm, 0.0)))


def column3(a, b, c, shape):
    row = iota(shape, 0)
    return jnp.where(row == 0, a, jnp.where(row == 1, b, jnp.where(row == 2, c, 0.0)))


def prologue_kernel(leaf_ref, count_ref, centers_ref, charges_ref, coords_ref, targets_ref, zsend_ref, tsend_ref, current_ref):
    leaf = leaf_ref[0]
    shape = (8, 128)
    lane = iota(shape, 1)
    live = (lane < count_ref[0]).astype(f32)
    current = charges_ref[...] * live
    current_ref[...] = current
    u = jnp.concatenate([coords_ref[...], jnp.zeros((5, 128), f32)], 0)
    center = column3(centers_ref[0, leaf], centers_ref[1, leaf], centers_ref[2, leaf], shape)
    pts = center + HALF_SIDE * u
    shifted = jnp.concatenate([jnp.zeros((5, 128), f32), coords_ref[...]], 0)
    rows = source_rows(pts, shifted)
    for k in range(NZ):
        zsend_ref[k, 0:8] = current
        zsend_ref[k, 8:16] = rows
    trows = target_rows(jnp.concatenate([targets_ref[...], jnp.zeros((5, 128), f32)], 0))
    for k in range(PLANE):
        tsend_ref[k] = trows


def a_block(rows):
    rows = jnp.where(iota(rows.shape, 0) < 5, rows, 0.0)
    h, m, low = split3(rows)
    return jnp.concatenate([h, h, m, m, h, low], 0).T.astype(bf16)


def interp_tables():
    p = iota((32, 128), 0)
    parts = (p >> 4, (p >> 2) & 3, p & 3)
    tables = []
    for index, number in zip(parts, (2, 4, 4)):
        nodes = cheby_nodes(number)
        others = [[nodes[i] for i in range(number) if i != k] for k in range(number)]
        roots = [pick(index, [others[k][j] for k in range(number)]) for j in range(number - 1)]
        scale = pick(index, [1.0 / np.prod([nodes[k] - o for o in others[k]]) for k in range(number)])
        tables.append((roots, scale))
    return tables


def setup_kernel(pos_ref, centers_ref, near_ref, recv_ref, tgt_ref, a_ref, b_ref, ih_ref, il_ref, list_ref, cnt_ref, mask_ref):
    y, z, member = pos_ref[0], pos_ref[1], pos_ref[2]
    tables = interp_tables()
    for k in range(NZ):
        rows = recv_ref[k, 8:16]
        a_ref[k * 128 : (k + 1) * 128, :DEPTH] = a_block(rows)
        value = None
        for axis, (roots, scale) in enumerate(tables):
            u = jnp.broadcast_to(rows[5 + axis : 6 + axis], (32, 128))
            line = scale
            for root in roots:
                line = line * (u - root)
            value = line if value is None else value * line
        hi, lo = split2(value)
        ih_ref[k * 32 : (k + 1) * 32] = hi
        il_ref[k * 32 : (k + 1) * 32] = lo
    a_ref[ZERO_BLOCK * 128 : (ZERO_BLOCK + 1) * 128, :DEPTH] = a_ref[0:128, :DEPTH]
    lane = iota((8, 128), 1)
    p = lane & 31
    row = iota((8, 128), 0)
    offset = jnp.where(
        row == 0,
        pick(p >> 4, cheby_nodes(2)),
        jnp.where(row == 1, pick((p >> 2) & 3, cheby_nodes(4)), jnp.where(row == 2, pick(p & 3, cheby_nodes(4)), 0.0)),
    )
    for block in range(4):
        center = jnp.zeros((8, 128), f32)
        for k in range(4):
            leaf = (y * NZ + block * 4 + k) * MEMBERS + member
            column = column3(centers_ref[0, leaf], centers_ref[1, leaf], centers_ref[2, leaf], (8, 128))
            center = jnp.where((lane >> 5) == k, column, center)
        rows = source_rows(center + HALF_SIDE * offset, 0.0)
        a_ref[(FAR_A + block) * 128 : (FAR_A + block + 1) * 128, :DEPTH] = a_block(rows)
    for other in range(NY):
        rows = jnp.concatenate([tgt_ref[other * MEMBERS + k] for k in range(MEMBERS)], 1)
        h, m, low = split3(rows)
        b_ref[other] = jnp.concatenate([h, m, h, m, low, h], 0).astype(bf16)
    group = iota((1, 512), 1) >> 5
    for other in range(NY):
        own = (y == other).astype(jnp.int32)
        list_ref[other, 0] = z

        def visit(j, state):
            count, mask = state
            cluster = near_ref[j, other * NZ + z]
            mine = (cluster >> 4) == y
            zz = cluster & 15
            list_ref[other, count] = zz
            mask = jnp.where((group == zz) & mine, 0.0, mask)
            return count + mine.astype(jnp.int32), mask

        first = jnp.where((group == z) & (own > 0), 0.0, jnp.ones((1, 512), f32))
        count, mask = lax.fori_loop(0, NEAR, visit, (own, first))
        mask_ref[other] = jnp.broadcast_to(mask, (16, 512))
        for k in range(4):
            list_ref[other, count + k] = FAR_A + k
        for k in range(4, 8):
            list_ref[other, count + k] = ZERO_BLOCK
        cnt_ref[other] = (count + 4 + 3) // 4


def field_kernel(list_ref, cnt_ref, recv_ref, a_ref, b_ref, ih_ref, il_ref, mask_ref, out_ref, q_ref):
    far = []
    for k in range(NZ):
        hi, lo = split2(recv_ref[k, 0:8])
        q = jnp.concatenate([hi.astype(f32), lo.astype(f32)], 0).astype(bf16)
        q_ref[k] = q
        nt = (((1,), (1,)), ((), ()))
        both = lax.dot_general(q, ih_ref[k * 32 : (k + 1) * 32], nt, preferred_element_type=f32)
        both = both + lax.dot_general(q, il_ref[k * 32 : (k + 1) * 32], nt, preferred_element_type=f32)
        far.append(both[0:8] + both[8:16])
    far = jnp.concatenate(far, 1)
    hi = far.astype(bf16).astype(f32)
    far = jnp.concatenate([hi, far - hi], 0)
    q_ref[ZERO_BLOCK] = jnp.zeros((16, 128), bf16)
    for other in range(NY):
        masked = (far * mask_ref[other]).astype(bf16)
        for k in range(4):
            q_ref[FAR_Q + other * 4 + k] = masked[:, k * 128 : (k + 1) * 128]

    def per_cluster(other, carry):
        b = b_ref[other]

        def chunk(i, acc):
            blocks = [list_ref[other, i * 4 + k] for k in range(4)]
            a = jnp.concatenate([a_ref[pl.ds(pl.multiple_of(n * 128, 128), 128), :DEPTH] for n in blocks], 0)
            q = jnp.concatenate([q_ref[jnp.where(n >= FAR_A, n + other * 4, n)] for n in blocks], 1)
            square = jnp.dot(a, b, preferred_element_type=f32)
            hi, lo = split2(lax.rsqrt(square))
            acc = acc + jnp.dot(q, hi, preferred_element_type=f32)
            return acc + jnp.dot(q, lo, preferred_element_type=f32)

        acc = lax.fori_loop(0, cnt_ref[other], chunk, jnp.zeros((16, MEMBERS * 128), f32))
        total = acc[0:8] + acc[8:16]
        for k in range(MEMBERS):
            out_ref[other * MEMBERS + k] = total[:, k * 128 : (k + 1) * 128]
        return carry

    lax.fori_loop(0, NY, per_cluster, 0)


def update_kernel(scale, count_ref, steps_ref, recv_ref, boundary_ref, current_ref, new_ref, residual_ref, *zsend):
    parts = [recv_ref[k] for k in range(PLANE)]
    while len(parts) > 1:
        parts = [parts[i] + parts[i + 1] for i in range(0, len(parts), 2)]
    shape = (8, 128)
    live = (iota(shape, 1) < count_ref[0]).astype(f32)
    row = iota(shape, 0)
    steps = jnp.zeros(shape, f32)
    for k in range(8):
        steps = jnp.where(row == k, steps_ref[k], steps)
    residual = live * (boundary_ref[...] - scale * parts[0])
    new = live * (current_ref[...] + steps * residual / (1.0 + jnp.abs(residual)))
    new_ref[...] = new
    residual_ref[...] = residual
    for ref in zsend:
        for k in range(NZ):
            ref[k] = new


VM = pl.BlockSpec(memory_space=pltpu.VMEM)
SM = pl.BlockSpec(memory_space=pltpu.SMEM)


def sds(shape, dtype=f32):
    return jax.ShapeDtypeStruct(shape, dtype)


def body(leaf_centers, source_coords, target_points, charges, boundary_data, step_sizes, valid_count, near_lists):
    y, z = lax.axis_index("y"), lax.axis_index("z")
    member = lax.axis_index("x") * NC + lax.axis_index("core")
    leaf = (y * NZ + z) * MEMBERS + member
    pos = jnp.stack([y, z, member, leaf]).astype(jnp.int32)
    plane = ("y", "x", "core")
    params = pltpu.CompilerParams(vmem_limit_bytes=56 * 2**20)
    zsend, tsend, current = pl.pallas_call(
        prologue_kernel,
        out_shape=(sds((NZ, 16, 128)), sds((PLANE, 8, 128)), sds((8, 128))),
        in_specs=[SM, SM, SM, VM, VM, VM],
        out_specs=(VM, VM, VM),
        name="prologue",
    )(pos[3:], valid_count, leaf_centers, charges, source_coords, target_points)
    targets = lax.all_to_all(tsend, plane, 0, 0, tiled=True)
    recv = lax.all_to_all(zsend, "z", 0, 0, tiled=True)
    a, b, ih, il, lists, counts, mask = pl.pallas_call(
        setup_kernel,
        out_shape=(
            sds((A_BLOCKS * 128, 128), bf16),
            sds((NY, DEPTH, MEMBERS * 128), bf16),
            sds((NZ * 32, 128), bf16),
            sds((NZ * 32, 128), bf16),
            sds((NY, SLOTS), jnp.int32),
            sds((NY,), jnp.int32),
            sds((NY, 16, 512)),
        ),
        in_specs=[SM, SM, SM, VM, VM],
        out_specs=(VM, VM, VM, VM, SM, SM, VM),
        compiler_params=params,
        name="setup",
    )(pos, leaf_centers, near_lists.T, recv, targets)
    scale = 1.0 / math.sqrt(NY * NZ * MEMBERS * 128)
    residual = None
    for turn in range(2):
        sums = pl.pallas_call(
            field_kernel,
            out_shape=sds((PLANE, 8, 128)),
            in_specs=[SM, SM, VM, VM, VM, VM, VM, VM],
            out_specs=VM,
            scratch_shapes=[pltpu.VMEM((Q_BLOCKS, 16, 128), bf16)],
            compiler_params=params,
            name="field",
        )(lists, counts, recv, a, b, ih, il, mask)
        sums = lax.all_to_all(sums, plane, 0, 0, tiled=True)
        more = (sds((NZ, 8, 128)),) if turn == 0 else ()
        current, residual, *zsend = pl.pallas_call(
            functools.partial(update_kernel, scale),
            out_shape=(sds((8, 128)), sds((8, 128))) + more,
            in_specs=[SM, SM, VM, VM, VM],
            out_specs=(VM, VM) + (VM,) * len(more),
            name="update",
        )(valid_count, step_sizes, sums, boundary_data, current)
        if turn == 0:
            recv = lax.all_to_all(zsend[0], "z", 0, 0, tiled=True)
    return (current, residual)


def solution(mesh):
    grid = Mesh(mesh.devices.reshape(NY, NZ, NX, NC), ("y", "z", "x", "core"))
    split = P(None, ("y", "z", "x", "core"))
    in_specs = (P(), split, split, split, split, P(), P(("y", "z", "x", "core")), P())
    return jax.shard_map(body, mesh=grid, in_specs=in_specs, out_specs=(split, split), check_vma=False)
```

```python
import functools
import math

import jax
import jax.numpy as jnp
import numpy as np
from jax import lax
from jax.experimental import pallas as pl
from jax.experimental.pallas import tpu as pltpu
from jax.sharding import Mesh
from jax.sharding import PartitionSpec as P

HALF_SIDE = 0.08
SOFTENING = 0.0025
NY, NZ, NX, NC = 4, 16, 4, 2
MEMBERS = NX * NC
PLANE = NY * MEMBERS
NEAR = 26
DEPTH = 48
FAR = NZ
ZERO_BLOCK = FAR + 4 * NY
FAR_SLOTS = 32
CHUNK_OWNER = 80
CHUNK_SLOTS = 128
PAIRS = 17
bf16, f32 = jnp.bfloat16, jnp.float32


def cheby_nodes(number):
    return np.cos(np.pi * (2 * np.arange(number) + 1) / (2 * number))


def pick(index, values):
    out = jnp.full(index.shape, float(values[0]), f32)
    for k in range(1, len(values)):
        out = jnp.where(index == k, float(values[k]), out)
    return out


def iota(shape, dim):
    return lax.broadcasted_iota(jnp.int32, shape, dim)


def split3(v):
    h = v.astype(bf16).astype(f32)
    r = v - h
    m = r.astype(bf16).astype(f32)
    low = (r - m).astype(bf16).astype(f32)
    return h, m, low


def split2(v):
    h = v.astype(bf16)
    return h, (v - h.astype(f32)).astype(bf16)


def source_rows(pts, extra):
    row = iota(pts.shape, 0)
    s = jnp.where(row < 3, pts - 0.5, 0.0)
    norm = jnp.sum(s * s, axis=0, keepdims=True) + SOFTENING
    return jnp.where(row < 3, -2.0 * s, jnp.where(row == 3, norm, jnp.where(row == 4, 1.0, extra)))


def target_rows(pts):
    row = iota(pts.shape, 0)
    t = jnp.where(row < 3, pts - 0.5, 0.0)
    norm = jnp.sum(t * t, axis=0, keepdims=True)
    return jnp.where(row < 3, t, jnp.where(row == 3, 1.0, jnp.where(row == 4, norm, 0.0)))


def column3(a, b, c, shape):
    row = iota(shape, 0)
    return jnp.where(row == 0, a, jnp.where(row == 1, b, jnp.where(row == 2, c, 0.0)))


def here():
    member = lax.axis_index("x") * NC + lax.axis_index("core")
    return lax.axis_index("y"), lax.axis_index("z"), member


def prologue_kernel(count_ref, centers_ref, charges_ref, coords_ref, targets_ref, zsend_ref, tsend_ref, current_ref):
    y, z, member = here()
    leaf = (y * NZ + z) * MEMBERS + member
    shape = (8, 128)
    lane = iota(shape, 1)
    live = (lane < count_ref[0]).astype(f32)
    current = charges_ref[...] * live
    current_ref[...] = current
    u = jnp.concatenate([coords_ref[...], jnp.zeros((5, 128), f32)], 0)
    center = column3(centers_ref[0, leaf], centers_ref[1, leaf], centers_ref[2, leaf], shape)
    pts = center + HALF_SIDE * u
    shifted = jnp.concatenate([jnp.zeros((5, 128), f32), coords_ref[...]], 0)
    rows = source_rows(pts, shifted)
    for k in range(NZ):
        zsend_ref[k, 0:8] = current
        zsend_ref[k, 8:16] = rows
    trows = target_rows(jnp.concatenate([targets_ref[...], jnp.zeros((5, 128), f32)], 0))
    for k in range(PLANE):
        tsend_ref[k] = trows


def a_block(rows):
    rows = jnp.where(iota(rows.shape, 0) < 5, rows, 0.0)
    h, m, low = split3(rows)
    return jnp.concatenate([h, h, m, m, h, low], 0).T.astype(bf16)


def interp_tables():
    p = iota((32, 128), 0)
    parts = (p >> 4, (p >> 2) & 3, p & 3)
    tables = []
    for index, number in zip(parts, (2, 4, 4)):
        nodes = cheby_nodes(number)
        others = [[nodes[i] for i in range(number) if i != k] for k in range(number)]
        roots = [pick(index, [others[k][j] for k in range(number)]) for j in range(number - 1)]
        scale = pick(index, [1.0 / np.prod([nodes[k] - o for o in others[k]]) for k in range(number)])
        tables.append((roots, scale))
    return tables


def lists_kernel(near_ref, far_ref, chunk_ref, count_ref, mine_ref):
    y, z, _ = here()
    total = jnp.int32(0)
    for other in range(NY):
        for k in range(NZ):
            mine_ref[k] = 0
        mine_ref[z] = (y == other).astype(jnp.int32)

        def visit(j, carry):
            cluster = near_ref[j, other * NZ + z]
            slot = jnp.where((cluster >> 4) == y, cluster & 15, NZ)
            mine_ref[slot] = 1
            return carry

        lax.fori_loop(0, NEAR, visit, 0, unroll=True)
        near_count = jnp.int32(0)
        far_count = jnp.int32(0)
        for k in range(NZ):
            mine = mine_ref[k]
            chunk_ref[total + near_count] = k
            far_ref[other, far_count] = k
            near_count = near_count + mine
            far_count = far_count + 1 - mine
        for k in range(3):
            far_ref[other, far_count + k] = NZ
        far_blocks = (far_count + 3) // 4
        start = total + near_count
        for k in range(4):
            chunk_ref[start + k] = FAR + other * 4 + k
        end = start + far_blocks
        chunk_ref[end] = ZERO_BLOCK
        far_ref[other, FAR_SLOTS - 1] = far_blocks
        rounded = ((end + 1) >> 1) << 1

        def owner(k, carry):
            chunk_ref[CHUNK_OWNER + k] = other
            return carry

        lax.fori_loop(total >> 1, rounded >> 1, owner, 0)
        total = rounded
    count_ref[0] = total >> 1


def charge_blocks(recv_ref, ih_ref, il_ref, far_ref, q_ref, wide_ref):
    far = []
    nt = (((1,), (1,)), ((), ()))
    for k in range(NZ):
        hi, lo = split2(recv_ref[k, 0:8])
        q = jnp.concatenate([hi.astype(f32), lo.astype(f32)], 0).astype(bf16)
        q_ref[k] = q
        both = lax.dot_general(q, ih_ref[k * 32 : (k + 1) * 32], nt, preferred_element_type=f32)
        both = both + lax.dot_general(q, il_ref[k * 32 : (k + 1) * 32], nt, preferred_element_type=f32)
        far.append(both[0:8] + both[8:16])
    for k in range(4):
        wide = jnp.concatenate(far[4 * k : 4 * k + 4], 1)
        hi = wide.astype(bf16).astype(f32)
        wide_ref[k] = jnp.concatenate([hi, wide - hi], 0)
    wide_ref[4] = jnp.zeros((16, 128), f32)
    q_ref[ZERO_BLOCK] = jnp.zeros((16, 128), bf16)
    group = iota((16, 128), 1) >> 5
    for other in range(NY):
        for block in range(4):

            @pl.when(block < far_ref[other, FAR_SLOTS - 1])
            def _(other=other, block=block):
                out = jnp.zeros((16, 128), f32)
                for k in range(4):
                    leaf = far_ref[other, block * 4 + k]
                    moved = pltpu.roll(wide_ref[leaf >> 2], ((4 + k - leaf) & 3) * 32, 1)
                    out = jnp.where(group == k, moved, out)
                q_ref[FAR + other * 4 + block] = out.astype(bf16)


def setup_kernel(centers_ref, far_ref, recv_ref, a_ref, ih_ref, il_ref, q_ref, proxy_ref, wide_ref):
    y, _, member = here()
    tables = interp_tables()
    for k in range(NZ):
        rows = recv_ref[k, 8:16]
        a_ref[k * 128 : (k + 1) * 128, :DEPTH] = a_block(rows)
        value = None
        for axis, (roots, scale) in enumerate(tables):
            u = jnp.broadcast_to(rows[5 + axis : 6 + axis], (32, 128))
            line = scale
            for root in roots:
                line = line * (u - root)
            value = line if value is None else value * line
        hi, lo = split2(value)
        ih_ref[k * 32 : (k + 1) * 32] = hi
        il_ref[k * 32 : (k + 1) * 32] = lo
    lane = iota((8, 128), 1)
    p = lane & 31
    row = iota((8, 128), 0)
    offset = jnp.where(
        row == 0,
        pick(p >> 4, cheby_nodes(2)),
        jnp.where(row == 1, pick((p >> 2) & 3, cheby_nodes(4)), jnp.where(row == 2, pick(p & 3, cheby_nodes(4)), 0.0)),
    )
    for block in range(4):
        center = jnp.zeros((8, 128), f32)
        for k in range(4):
            leaf = (y * NZ + block * 4 + k) * MEMBERS + member
            column = column3(centers_ref[0, leaf], centers_ref[1, leaf], centers_ref[2, leaf], (8, 128))
            center = jnp.where((lane >> 5) == k, column, center)
        rows = source_rows(center + HALF_SIDE * offset, 0.0)
        proxy_ref[block * 128 : (block + 1) * 128, :DEPTH] = a_block(rows)
    proxy_ref[512:544, :DEPTH] = proxy_ref[0:32, :DEPTH]
    for other in range(NY):
        for block in range(4):

            @pl.when(block < far_ref[other, FAR_SLOTS - 1])
            def _(other=other, block=block):
                for k in range(4):
                    leaf = far_ref[other, block * 4 + k]
                    base = (FAR + other * 4 + block) * 128 + k * 32
                    a_ref[base : base + 32] = proxy_ref[pl.ds(pl.multiple_of(leaf * 32, 32), 32)]

    charge_blocks(recv_ref, ih_ref, il_ref, far_ref, q_ref, wide_ref)


def charges_of(chunk_ref, q_ref, i):
    return jnp.concatenate([q_ref[chunk_ref[2 * i + k]] for k in range(2)], 1)


def multiply(chunk_ref, q_ref, acc_ref, i, hi_ref, lo_ref, j):
    q = charges_of(chunk_ref, q_ref, i)
    rows = pl.ds(pl.multiple_of(chunk_ref[CHUNK_OWNER + i] * 16, 16), 16)
    part = jnp.dot(q, hi_ref[j], preferred_element_type=f32) + jnp.dot(q, lo_ref[j], preferred_element_type=f32)
    acc_ref[rows] = acc_ref[rows] + part


def write_sums(acc_ref, out_ref):
    for other in range(NY):
        total = acc_ref[other * 16 : other * 16 + 8] + acc_ref[other * 16 + 8 : other * 16 + 16]
        for k in range(MEMBERS):
            out_ref[other * MEMBERS + k] = total[:, k * 128 : (k + 1) * 128]


def first_kernel(chunk_ref, count_ref, tgt_ref, a_ref, q_ref, out_ref, eh_ref, el_ref, oh_ref, ol_ref, b_ref, acc_ref):
    for other in range(NY):
        rows = jnp.concatenate([tgt_ref[other * MEMBERS + k] for k in range(MEMBERS)], 1)
        h, m, low = split3(rows)
        b_ref[other] = jnp.concatenate([h, m, h, m, low, h], 0).astype(bf16)
    acc_ref[...] = jnp.zeros_like(acc_ref)
    count = count_ref[0]

    def evaluate(i, hi_ref, lo_ref, j):
        blocks = [chunk_ref[2 * i + k] for k in range(2)]
        starts = [pl.multiple_of(jnp.where(n == ZERO_BLOCK, 0, n) * 128, 128) for n in blocks]
        a = jnp.concatenate([a_ref[pl.ds(n, 128), :DEPTH] for n in starts], 0)
        square = jnp.dot(a, b_ref[chunk_ref[CHUNK_OWNER + i]], preferred_element_type=f32)
        hi, lo = split2(lax.rsqrt(square))
        hi_ref[j] = hi
        lo_ref[j] = lo

    even, odd = (eh_ref, el_ref), (oh_ref, ol_ref)
    mul = functools.partial(multiply, chunk_ref, q_ref, acc_ref)
    evaluate(0, *even, 0)

    def pair(j, carry):
        evaluate(2 * j + 1, *odd, j)
        mul(2 * j, *even, j)
        evaluate(2 * j + 2, *even, j + 1)
        mul(2 * j + 1, *odd, j)
        return carry

    pairs = (count - 1) >> 1
    lax.fori_loop(0, pairs, pair, 0)

    @pl.when((count & 1) == 0)
    def _():
        evaluate(2 * pairs + 1, *odd, pairs)
        mul(2 * pairs, *even, pairs)
        mul(2 * pairs + 1, *odd, pairs)

    @pl.when((count & 1) == 1)
    def _():
        mul(2 * pairs, *even, pairs)

    write_sums(acc_ref, out_ref)


def second_kernel(chunk_ref, count_ref, far_ref, recv_ref, ih_ref, il_ref, eh_ref, el_ref, oh_ref, ol_ref, out_ref, q_ref, wide_ref, acc_ref):
    charge_blocks(recv_ref, ih_ref, il_ref, far_ref, q_ref, wide_ref)
    acc_ref[...] = jnp.zeros_like(acc_ref)
    count = count_ref[0]
    mul = functools.partial(multiply, chunk_ref, q_ref, acc_ref)

    def pair(j, carry):
        mul(2 * j, eh_ref, el_ref, j)
        mul(2 * j + 1, oh_ref, ol_ref, j)
        return carry

    lax.fori_loop(0, count >> 1, pair, 0)

    @pl.when((count & 1) == 1)
    def _():
        mul(count - 1, eh_ref, el_ref, count >> 1)

    write_sums(acc_ref, out_ref)


def update_kernel(scale, count_ref, steps_ref, recv_ref, boundary_ref, current_ref, new_ref, residual_ref, *zsend):
    parts = [recv_ref[k] for k in range(PLANE)]
    while len(parts) > 1:
        parts = [parts[i] + parts[i + 1] for i in range(0, len(parts), 2)]
    shape = (8, 128)
    live = (iota(shape, 1) < count_ref[0]).astype(f32)
    row = iota(shape, 0)
    steps = jnp.zeros(shape, f32)
    for k in range(8):
        steps = jnp.where(row == k, steps_ref[k], steps)
    residual = live * (boundary_ref[...] - scale * parts[0])
    new = live * (current_ref[...] + steps * residual / (1.0 + jnp.abs(residual)))
    new_ref[...] = new
    residual_ref[...] = residual
    for ref in zsend:
        for k in range(NZ):
            ref[k] = new


VM = pl.BlockSpec(memory_space=pltpu.VMEM)
SM = pl.BlockSpec(memory_space=pltpu.SMEM)


def sds(shape, dtype=f32):
    return jax.ShapeDtypeStruct(shape, dtype)


def body(leaf_centers, source_coords, target_points, charges, boundary_data, step_sizes, valid_count, near_lists):
    plane = ("y", "x", "core")
    params = pltpu.CompilerParams(vmem_limit_bytes=12 * 2**20)
    small = pltpu.CompilerParams(vmem_limit_bytes=4 * 2**20)
    zsend, tsend, current = pl.pallas_call(
        prologue_kernel,
        out_shape=(sds((NZ, 16, 128)), sds((PLANE, 8, 128)), sds((8, 128))),
        in_specs=[SM, SM, VM, VM, VM],
        out_specs=(VM, VM, VM),
        compiler_params=small,
        name="prologue",
    )(valid_count, leaf_centers, charges, source_coords, target_points)
    recv = lax.all_to_all(zsend, "z", 0, 0, tiled=True)
    recv, tsend, near_lists = lax.optimization_barrier((recv, tsend, near_lists))
    targets = lax.all_to_all(tsend, plane, 0, 0, tiled=True)
    far, chunks, count = pl.pallas_call(
        lists_kernel,
        out_shape=(sds((NY, FAR_SLOTS), jnp.int32), sds((CHUNK_SLOTS,), jnp.int32), sds((1,), jnp.int32)),
        in_specs=[SM],
        out_specs=(SM, SM, SM),
        scratch_shapes=[pltpu.SMEM((NZ + 1,), jnp.int32)],
        compiler_params=small,
        cost_estimate=pl.CostEstimate(flops=10**9, bytes_accessed=4 * 10**6, transcendentals=0),
        name="lists",
    )(near_lists.T)
    a, ih, il, q = pl.pallas_call(
        setup_kernel,
        out_shape=(
            sds((ZERO_BLOCK * 128, 128), bf16),
            sds((NZ * 32, 128), bf16),
            sds((NZ * 32, 128), bf16),
            sds((ZERO_BLOCK + 1, 16, 128), bf16),
        ),
        in_specs=[SM, SM, VM],
        out_specs=(VM, VM, VM, VM),
        scratch_shapes=[pltpu.VMEM((544, 128), bf16), pltpu.VMEM((5, 16, 128), f32)],
        compiler_params=params,
        cost_estimate=pl.CostEstimate(flops=10**9, bytes_accessed=8 * 10**6, transcendentals=0),
        name="setup",
    )(leaf_centers, far, recv)
    scale = 1.0 / math.sqrt(NY * NZ * MEMBERS * 128)
    half = pltpu.VMEM((PAIRS, 256, MEMBERS * 128), bf16)
    sums, *kernels = pl.pallas_call(
        first_kernel,
        out_shape=(sds((PLANE, 8, 128)), half, half, half, half),
        in_specs=[SM, SM, VM, VM, VM],
        out_specs=(VM,) * 5,
        scratch_shapes=[pltpu.VMEM((NY, DEPTH, MEMBERS * 128), bf16), pltpu.VMEM((NY * 16, MEMBERS * 128), f32)],
        compiler_params=params,
        name="first",
    )(chunks, count, targets, a, q)

    def update(sums, more):
        return pl.pallas_call(
            functools.partial(update_kernel, scale),
            out_shape=(sds((8, 128)), sds((8, 128))) + more,
            in_specs=[SM, SM, VM, VM, VM],
            out_specs=(VM, VM) + (VM,) * len(more),
            compiler_params=small,
            name="update",
        )(valid_count, step_sizes, lax.all_to_all(sums, plane, 0, 0, tiled=True), boundary_data, current)

    current, residual, zsend = update(sums, (sds((NZ, 8, 128)),))
    recv = lax.all_to_all(zsend, "z", 0, 0, tiled=True)
    sums = pl.pallas_call(
        second_kernel,
        out_shape=sds((PLANE, 8, 128)),
        in_specs=[SM, SM, SM] + [VM] * 7,
        out_specs=VM,
        scratch_shapes=[
            pltpu.VMEM((ZERO_BLOCK + 1, 16, 128), bf16),
            pltpu.VMEM((5, 16, 128), f32),
            pltpu.VMEM((NY * 16, MEMBERS * 128), f32),
        ],
        compiler_params=params,
        name="second",
    )(chunks, count, far, recv, ih, il, *kernels)
    current, residual = update(sums, ())
    return (current, residual)


def solution(mesh):
    grid = Mesh(mesh.devices.reshape(NY, NZ, NX, NC), ("y", "z", "x", "core"))
    split = P(None, ("y", "z", "x", "core"))
    in_specs = (P(), split, split, split, split, P(), P(("y", "z", "x", "core")), P())
    return jax.shard_map(body, mesh=grid, in_specs=in_specs, out_specs=(split, split), check_vma=False)
```

```python
import functools
import math

import jax
import jax.numpy as jnp
import numpy as np
from jax import lax
from jax.experimental import pallas as pl
from jax.experimental.pallas import tpu as pltpu
from jax.sharding import Mesh
from jax.sharding import PartitionSpec as P

HALF_SIDE = 0.08
SOFTENING = 0.0025
NY, NZ, NX, NC = 4, 16, 4, 2
MEMBERS = NX * NC
PLANE = NY * MEMBERS
NEAR = 26
DEPTH = 48
FAR = NZ
ZERO_BLOCK = FAR + 4 * NY
FAR_SLOTS = 32
CHUNK_OWNER = 80
CHUNK_SLOTS = 128
PAIRS = 17
bf16, f32 = jnp.bfloat16, jnp.float32


def cheby_nodes(number):
    return np.cos(np.pi * (2 * np.arange(number) + 1) / (2 * number))


def pick(index, values):
    out = jnp.full(index.shape, float(values[0]), f32)
    for k in range(1, len(values)):
        out = jnp.where(index == k, float(values[k]), out)
    return out


def iota(shape, dim):
    return lax.broadcasted_iota(jnp.int32, shape, dim)


def split3(v):
    h = v.astype(bf16).astype(f32)
    r = v - h
    m = r.astype(bf16).astype(f32)
    low = (r - m).astype(bf16).astype(f32)
    return h, m, low


def split2(v):
    h = v.astype(bf16)
    return h, (v - h.astype(f32)).astype(bf16)


def source_rows(pts, extra):
    row = iota(pts.shape, 0)
    s = jnp.where(row < 3, pts - 0.5, 0.0)
    norm = jnp.sum(s * s, axis=0, keepdims=True) + SOFTENING
    return jnp.where(row < 3, -2.0 * s, jnp.where(row == 3, norm, jnp.where(row == 4, 1.0, extra)))


def target_rows(pts):
    row = iota(pts.shape, 0)
    t = jnp.where(row < 3, pts - 0.5, 0.0)
    norm = jnp.sum(t * t, axis=0, keepdims=True)
    return jnp.where(row < 3, t, jnp.where(row == 3, 1.0, jnp.where(row == 4, norm, 0.0)))


def column3(a, b, c, shape):
    row = iota(shape, 0)
    return jnp.where(row == 0, a, jnp.where(row == 1, b, jnp.where(row == 2, c, 0.0)))


def here():
    member = lax.axis_index("x") * NC + lax.axis_index("core")
    return lax.axis_index("y"), lax.axis_index("z"), member


def a_block(rows):
    rows = jnp.where(iota(rows.shape, 0) < 5, rows, 0.0)
    h, m, low = split3(rows)
    return jnp.concatenate([h, h, m, m, h, low], 0).T.astype(bf16)


def interp_tables():
    p = iota((32, 128), 0)
    parts = (p >> 4, (p >> 2) & 3, p & 3)
    tables = []
    for index, number in zip(parts, (2, 4, 4)):
        nodes = cheby_nodes(number)
        others = [[nodes[i] for i in range(number) if i != k] for k in range(number)]
        roots = [pick(index, [others[k][j] for k in range(number)]) for j in range(number - 1)]
        scale = pick(index, [1.0 / np.prod([nodes[k] - o for o in others[k]]) for k in range(number)])
        tables.append((roots, scale))
    return tables


def make_lists(y, z, near_ref, far_ref, chunk_ref, count_ref, mine_ref):
    total = jnp.int32(0)
    for other in range(NY):
        for k in range(NZ):
            mine_ref[k] = 0
        mine_ref[z] = (y == other).astype(jnp.int32)
        for j in range(NEAR):
            cluster = near_ref[j, other * NZ + z]
            mine_ref[jnp.where((cluster >> 4) == y, cluster & 15, NZ)] = 1
        near_count = jnp.int32(0)
        far_count = jnp.int32(0)
        for k in range(NZ):
            mine = mine_ref[k]
            chunk_ref[total + near_count] = k
            far_ref[other, far_count] = k
            near_count = near_count + mine
            far_count = far_count + 1 - mine
        for k in range(3):
            far_ref[other, far_count + k] = NZ
        far_blocks = (far_count + 3) // 4
        start = total + near_count
        for k in range(4):
            chunk_ref[start + k] = FAR + other * 4 + k
        end = start + far_blocks
        chunk_ref[end] = ZERO_BLOCK
        far_ref[other, FAR_SLOTS - 1] = far_blocks
        rounded = ((end + 1) >> 1) << 1

        def owner(k, carry):
            chunk_ref[CHUNK_OWNER + k] = other
            return carry

        lax.fori_loop(total >> 1, rounded >> 1, owner, 0)
        total = rounded
    count_ref[0] = total >> 1


def prep_kernel(
    centers_ref, near_ref, count_ref, steps_ref, charges_hbm, coords_hbm, boundary_hbm,
    zsend_ref, held_ref, far_ref, chunk_ref, chunks_ref, proxy_ref,
    mine_ref, wide_ref, coords_ref, sem,
):
    y, z, member = here()
    leaf = (y * NZ + z) * MEMBERS + member
    copies = [
        pltpu.make_async_copy(source, target, sem.at[k])
        for k, (source, target) in enumerate(((charges_hbm, held_ref.at[0]), (coords_hbm, coords_ref), (boundary_hbm, held_ref.at[1])))
    ]
    for copy in copies:
        copy.start()
    make_lists(y, z, near_ref, far_ref, chunk_ref, chunks_ref, mine_ref)
    for copy in copies:
        copy.wait()
    lane = iota((8, 128), 1)
    row = iota((8, 128), 0)
    live = (lane < count_ref[0]).astype(f32)
    current = held_ref[0] * live
    held_ref[0] = current
    steps = jnp.zeros((8, 128), f32)
    for k in range(8):
        steps = jnp.where(row == k, steps_ref[k], steps)
    held_ref[2] = steps
    held_ref[3] = live
    u = jnp.concatenate([coords_ref[...], jnp.zeros((5, 128), f32)], 0)
    center = column3(centers_ref[0, leaf], centers_ref[1, leaf], centers_ref[2, leaf], (8, 128))
    shifted = jnp.concatenate([jnp.zeros((5, 128), f32), coords_ref[...]], 0)
    rows = source_rows(center + HALF_SIDE * u, shifted)
    for k in range(NZ):
        zsend_ref[k, 0:8] = current
        zsend_ref[k, 8:16] = rows
    p = lane & 31
    offset = jnp.where(
        row == 0,
        pick(p >> 4, cheby_nodes(2)),
        jnp.where(row == 1, pick((p >> 2) & 3, cheby_nodes(4)), jnp.where(row == 2, pick(p & 3, cheby_nodes(4)), 0.0)),
    )
    for block in range(4):
        center = jnp.zeros((8, 128), f32)
        for k in range(4):
            leaf = (y * NZ + block * 4 + k) * MEMBERS + member
            column = column3(centers_ref[0, leaf], centers_ref[1, leaf], centers_ref[2, leaf], (8, 128))
            center = jnp.where((lane >> 5) == k, column, center)
        rows = source_rows(center + HALF_SIDE * offset, 0.0)
        wide_ref[block * 128 : (block + 1) * 128, :DEPTH] = a_block(rows)
    wide_ref[512:544, :DEPTH] = wide_ref[0:32, :DEPTH]
    for other in range(NY):
        for block in range(4):

            @pl.when(block < far_ref[other, FAR_SLOTS - 1])
            def _(other=other, block=block):
                for k in range(4):
                    leaf = far_ref[other, block * 4 + k]
                    base = (other * 4 + block) * 128 + k * 32
                    proxy_ref[base : base + 32] = wide_ref[pl.ds(pl.multiple_of(leaf * 32, 32), 32)]


def charge_blocks(recv_ref, ih_ref, il_ref, far_ref, q_ref, wide_ref):
    far = []
    nt = (((1,), (1,)), ((), ()))
    for k in range(NZ):
        hi, lo = split2(recv_ref[k, 0:8])
        q = jnp.concatenate([hi.astype(f32), lo.astype(f32)], 0).astype(bf16)
        q_ref[k] = q
        both = lax.dot_general(q, ih_ref[k * 32 : (k + 1) * 32], nt, preferred_element_type=f32)
        both = both + lax.dot_general(q, il_ref[k * 32 : (k + 1) * 32], nt, preferred_element_type=f32)
        far.append(both[0:8] + both[8:16])
    for k in range(4):
        wide = jnp.concatenate(far[4 * k : 4 * k + 4], 1)
        hi = wide.astype(bf16).astype(f32)
        wide_ref[k] = jnp.concatenate([hi, wide - hi], 0)
    wide_ref[4] = jnp.zeros((16, 128), f32)
    q_ref[ZERO_BLOCK] = jnp.zeros((16, 128), bf16)
    group = iota((16, 128), 1) >> 5
    for other in range(NY):
        for block in range(4):

            @pl.when(block < far_ref[other, FAR_SLOTS - 1])
            def _(other=other, block=block):
                out = jnp.zeros((16, 128), f32)
                for k in range(4):
                    leaf = far_ref[other, block * 4 + k]
                    moved = pltpu.roll(wide_ref[leaf >> 2], ((4 + k - leaf) & 3) * 32, 1)
                    out = jnp.where(group == k, moved, out)
                q_ref[FAR + other * 4 + block] = out.astype(bf16)


def setup_kernel(far_ref, recv_ref, a_ref, ih_ref, il_ref, q_ref, wide_ref):
    tables = interp_tables()
    for k in range(NZ):
        rows = recv_ref[k, 8:16]
        a_ref[k * 128 : (k + 1) * 128, :DEPTH] = a_block(rows)
        value = None
        for axis, (roots, scale) in enumerate(tables):
            u = jnp.broadcast_to(rows[5 + axis : 6 + axis], (32, 128))
            line = scale
            for root in roots:
                line = line * (u - root)
            value = line if value is None else value * line
        hi, lo = split2(value)
        ih_ref[k * 32 : (k + 1) * 32] = hi
        il_ref[k * 32 : (k + 1) * 32] = lo
    charge_blocks(recv_ref, ih_ref, il_ref, far_ref, q_ref, wide_ref)


def charges_of(chunk_ref, q_ref, i):
    return jnp.concatenate([q_ref[chunk_ref[2 * i + k]] for k in range(2)], 1)


def multiply(chunk_ref, q_ref, acc_ref, i, hi_ref, lo_ref, j):
    q = charges_of(chunk_ref, q_ref, i)
    rows = pl.ds(pl.multiple_of(chunk_ref[CHUNK_OWNER + i] * 16, 16), 16)
    part = jnp.dot(q, hi_ref[j], preferred_element_type=f32) + jnp.dot(q, lo_ref[j], preferred_element_type=f32)
    acc_ref[rows] = acc_ref[rows] + part


def write_sums(acc_ref, out_ref):
    for other in range(NY):
        total = acc_ref[other * 16 : other * 16 + 8] + acc_ref[other * 16 + 8 : other * 16 + 16]
        for k in range(MEMBERS):
            out_ref[other * MEMBERS + k] = total[:, k * 128 : (k + 1) * 128]


def first_kernel(
    chunk_ref, count_ref, far_ref, tgt_ref, recv_ref, proxy_ref, out_ref, ih_ref, il_ref, eh_ref, el_ref, oh_ref, ol_ref, a_ref, q_ref, wide_ref, b_ref, acc_ref
):
    setup_kernel(far_ref, recv_ref, a_ref, ih_ref, il_ref, q_ref, wide_ref)
    a_ref[FAR * 128 :] = proxy_ref[...]
    for other in range(NY):
        points = jnp.concatenate([tgt_ref[other * MEMBERS + k] for k in range(MEMBERS)], 1)
        h, m, low = split3(target_rows(jnp.concatenate([points, jnp.zeros((5, MEMBERS * 128), f32)], 0)))
        b_ref[other] = jnp.concatenate([h, m, h, m, low, h], 0).astype(bf16)
    acc_ref[...] = jnp.zeros_like(acc_ref)
    count = count_ref[0]

    def evaluate(i, hi_ref, lo_ref, j):
        blocks = [chunk_ref[2 * i + k] for k in range(2)]
        starts = [pl.multiple_of(jnp.where(n == ZERO_BLOCK, 0, n) * 128, 128) for n in blocks]
        a = jnp.concatenate([a_ref[pl.ds(n, 128), :DEPTH] for n in starts], 0)
        square = jnp.dot(a, b_ref[chunk_ref[CHUNK_OWNER + i]], preferred_element_type=f32)
        hi, lo = split2(lax.rsqrt(square))
        hi_ref[j] = hi
        lo_ref[j] = lo

    even, odd = (eh_ref, el_ref), (oh_ref, ol_ref)
    mul = functools.partial(multiply, chunk_ref, q_ref, acc_ref)
    evaluate(0, *even, 0)

    def pair(j, carry):
        evaluate(2 * j + 1, *odd, j)
        mul(2 * j, *even, j)
        evaluate(2 * j + 2, *even, j + 1)
        mul(2 * j + 1, *odd, j)
        return carry

    pairs = (count - 1) >> 1
    lax.fori_loop(0, pairs, pair, 0)

    @pl.when((count & 1) == 0)
    def _():
        evaluate(2 * pairs + 1, *odd, pairs)
        mul(2 * pairs, *even, pairs)
        mul(2 * pairs + 1, *odd, pairs)

    @pl.when((count & 1) == 1)
    def _():
        mul(2 * pairs, *even, pairs)

    write_sums(acc_ref, out_ref)


def second_kernel(chunk_ref, count_ref, far_ref, recv_ref, ih_ref, il_ref, eh_ref, el_ref, oh_ref, ol_ref, out_ref, q_ref, wide_ref, acc_ref):
    charge_blocks(recv_ref, ih_ref, il_ref, far_ref, q_ref, wide_ref)
    acc_ref[...] = jnp.zeros_like(acc_ref)
    count = count_ref[0]
    mul = functools.partial(multiply, chunk_ref, q_ref, acc_ref)

    def pair(j, carry):
        mul(2 * j, eh_ref, el_ref, j)
        mul(2 * j + 1, oh_ref, ol_ref, j)
        return carry

    lax.fori_loop(0, count >> 1, pair, 0)

    @pl.when((count & 1) == 1)
    def _():
        mul(count - 1, eh_ref, el_ref, count >> 1)

    write_sums(acc_ref, out_ref)


def update_kernel(scale, last, recv_ref, held_ref, *refs):
    parts = [recv_ref[k] for k in range(PLANE)]
    while len(parts) > 1:
        parts = [parts[i] + parts[i + 1] for i in range(0, len(parts), 2)]
    live = held_ref[3]
    residual = live * (held_ref[1] - scale * parts[0])
    if last:
        current_ref, new_ref, residual_ref = refs
        residual_ref[...] = residual
        current = current_ref[...]
    else:
        new_ref, zsend_ref = refs
        current = held_ref[0]
    new = live * (current + held_ref[2] * residual / (1.0 + jnp.abs(residual)))
    new_ref[...] = new
    if not last:
        for k in range(NZ):
            zsend_ref[k] = new


VM = pl.BlockSpec(memory_space=pltpu.VMEM)
SM = pl.BlockSpec(memory_space=pltpu.SMEM)
HB = pl.BlockSpec(memory_space=pltpu.HBM)


def sds(shape, dtype=f32):
    return jax.ShapeDtypeStruct(shape, dtype)


def body(leaf_centers, source_coords, target_points, charges, boundary_data, step_sizes, valid_count, near_lists):
    plane = ("y", "x", "core")
    params = pltpu.CompilerParams(vmem_limit_bytes=12 * 2**20)
    small = pltpu.CompilerParams(vmem_limit_bytes=4 * 2**20)
    targets = lax.all_to_all(jnp.broadcast_to(target_points[None], (PLANE, 3, 128)), plane, 0, 0, tiled=True)
    zsend, held, far, chunks, count, proxies = pl.pallas_call(
        prep_kernel,
        out_shape=(
            sds((NZ, 16, 128)),
            sds((4, 8, 128)),
            sds((NY, FAR_SLOTS), jnp.int32),
            sds((CHUNK_SLOTS,), jnp.int32),
            sds((1,), jnp.int32),
            sds((4 * NY * 128, 128), bf16),
        ),
        in_specs=[SM, SM, SM, SM, HB, HB, HB],
        out_specs=(VM, VM, SM, SM, SM, VM),
        scratch_shapes=[
            pltpu.SMEM((NZ + 1,), jnp.int32),
            pltpu.VMEM((544, 128), bf16),
            pltpu.VMEM((3, 128), f32),
            pltpu.SemaphoreType.DMA((3,)),
        ],
        compiler_params=small,
        cost_estimate=pl.CostEstimate(flops=10**9, bytes_accessed=12 * 10**6, transcendentals=0),
        name="prep",
    )(leaf_centers, near_lists.T, valid_count, step_sizes, charges, source_coords, boundary_data)
    zsend, targets = lax.optimization_barrier((zsend, targets))
    recv = lax.all_to_all(zsend, "z", 0, 0, tiled=True)
    scale = 1.0 / math.sqrt(NY * NZ * MEMBERS * 128)
    half = pltpu.VMEM((PAIRS, 256, MEMBERS * 128), bf16)
    interp = sds((NZ * 32, 128), bf16)
    sums, ih, il, *kernels = pl.pallas_call(
        first_kernel,
        out_shape=(sds((PLANE, 8, 128)), interp, interp, half, half, half, half),
        in_specs=[SM, SM, SM, VM, VM, VM],
        out_specs=(VM,) * 7,
        scratch_shapes=[
            pltpu.VMEM((ZERO_BLOCK * 128, 128), bf16),
            pltpu.VMEM((ZERO_BLOCK + 1, 16, 128), bf16),
            pltpu.VMEM((5, 16, 128), f32),
            pltpu.VMEM((NY, DEPTH, MEMBERS * 128), bf16),
            pltpu.VMEM((NY * 16, MEMBERS * 128), f32),
        ],
        compiler_params=params,
        name="first",
    )(chunks, count, far, targets, recv, proxies)

    def update(sums, *current):
        last = len(current) > 0
        return pl.pallas_call(
            functools.partial(update_kernel, scale, last),
            out_shape=(sds((8, 128)), sds((8, 128) if last else (NZ, 8, 128))),
            in_specs=[VM, VM] + [VM] * last,
            out_specs=(VM, VM),
            compiler_params=small,
            name="update",
        )(lax.all_to_all(sums, plane, 0, 0, tiled=True), held, *current)

    current, zsend = update(sums)
    recv = lax.all_to_all(zsend, "z", 0, 0, tiled=True)
    sums = pl.pallas_call(
        second_kernel,
        out_shape=sds((PLANE, 8, 128)),
        in_specs=[SM, SM, SM] + [VM] * 7,
        out_specs=VM,
        scratch_shapes=[
            pltpu.VMEM((ZERO_BLOCK + 1, 16, 128), bf16),
            pltpu.VMEM((5, 16, 128), f32),
            pltpu.VMEM((NY * 16, MEMBERS * 128), f32),
        ],
        compiler_params=params,
        name="second",
    )(chunks, count, far, recv, ih, il, *kernels)
    current, residual = update(sums, current)
    return (current, residual)


def solution(mesh):
    grid = Mesh(mesh.devices.reshape(NY, NZ, NX, NC), ("y", "z", "x", "core"))
    split = P(None, ("y", "z", "x", "core"))
    in_specs = (P(), split, split, split, split, P(), P(("y", "z", "x", "core")), P())
    return jax.shard_map(body, mesh=grid, in_specs=in_specs, out_specs=(split, split), check_vma=False)
```

```python
import functools
import math

import jax
import jax.numpy as jnp
import numpy as np
from jax import lax
from jax.experimental import pallas as pl
from jax.experimental.pallas import tpu as pltpu
from jax.sharding import Mesh
from jax.sharding import PartitionSpec as P

HALF_SIDE = 0.08
SOFTENING = 0.0025
NY, NZ, NX, NC = 4, 16, 4, 2
MEMBERS = NX * NC
PLANE = NY * MEMBERS
NEAR = 26
DEPTH = 48
FAR = NZ
ZERO_BLOCK = FAR + 4 * NY
FAR_SLOTS = 32
CHUNK_OWNER = 80
CHUNK_SLOTS = 128
PAIRS = 17
bf16, f32 = jnp.bfloat16, jnp.float32


def cheby_nodes(number):
    return np.cos(np.pi * (2 * np.arange(number) + 1) / (2 * number))


def pick(index, values):
    out = jnp.full(index.shape, float(values[0]), f32)
    for k in range(1, len(values)):
        out = jnp.where(index == k, float(values[k]), out)
    return out


def iota(shape, dim):
    return lax.broadcasted_iota(jnp.int32, shape, dim)


def split3(v):
    h = v.astype(bf16).astype(f32)
    r = v - h
    m = r.astype(bf16).astype(f32)
    low = (r - m).astype(bf16).astype(f32)
    return h, m, low


def split2(v):
    h = v.astype(bf16)
    return h, (v - h.astype(f32)).astype(bf16)


def source_rows(pts, extra):
    row = iota(pts.shape, 0)
    s = jnp.where(row < 3, pts - 0.5, 0.0)
    norm = jnp.sum(s * s, axis=0, keepdims=True) + SOFTENING
    return jnp.where(row < 3, -2.0 * s, jnp.where(row == 3, norm, jnp.where(row == 4, 1.0, extra)))


def target_rows(pts):
    row = iota(pts.shape, 0)
    t = jnp.where(row < 3, pts - 0.5, 0.0)
    norm = jnp.sum(t * t, axis=0, keepdims=True)
    return jnp.where(row < 3, t, jnp.where(row == 3, 1.0, jnp.where(row == 4, norm, 0.0)))


def column3(a, b, c, shape):
    row = iota(shape, 0)
    return jnp.where(row == 0, a, jnp.where(row == 1, b, jnp.where(row == 2, c, 0.0)))


def here():
    member = lax.axis_index("x") * NC + lax.axis_index("core")
    return lax.axis_index("y"), lax.axis_index("z"), member


def a_block(rows):
    rows = jnp.where(iota(rows.shape, 0) < 5, rows, 0.0)
    h, m, low = split3(rows)
    return jnp.concatenate([h, h, m, m, h, low], 0).T.astype(bf16)


def interp_tables():
    p = iota((32, 128), 0)
    parts = (p >> 4, (p >> 2) & 3, p & 3)
    tables = []
    for index, number in zip(parts, (2, 4, 4)):
        nodes = cheby_nodes(number)
        others = [[nodes[i] for i in range(number) if i != k] for k in range(number)]
        roots = [pick(index, [others[k][j] for k in range(number)]) for j in range(number - 1)]
        scale = pick(index, [1.0 / np.prod([nodes[k] - o for o in others[k]]) for k in range(number)])
        tables.append((roots, scale))
    return tables


def make_lists(y, z, near_ref, far_ref, chunk_ref, count_ref, mine_ref):
    total = jnp.int32(0)
    for other in range(NY):
        for k in range(NZ):
            mine_ref[k] = 0
        mine_ref[z] = (y == other).astype(jnp.int32)
        for j in range(NEAR):
            cluster = near_ref[j, other * NZ + z]
            mine_ref[jnp.where((cluster >> 4) == y, cluster & 15, NZ)] = 1
        near_count = jnp.int32(0)
        far_count = jnp.int32(0)
        for k in range(NZ):
            mine = mine_ref[k]
            chunk_ref[total + near_count] = k
            far_ref[other, far_count] = k
            near_count = near_count + mine
            far_count = far_count + 1 - mine
        for k in range(3):
            far_ref[other, far_count + k] = NZ
        far_blocks = (far_count + 3) // 4
        start = total + near_count
        for k in range(4):
            chunk_ref[start + k] = FAR + other * 4 + k
        end = start + far_blocks
        chunk_ref[end] = ZERO_BLOCK
        far_ref[other, FAR_SLOTS - 1] = far_blocks
        rounded = ((end + 1) >> 1) << 1

        def owner(k, carry):
            chunk_ref[CHUNK_OWNER + k] = other
            return carry

        lax.fori_loop(total >> 1, rounded >> 1, owner, 0)
        total = rounded
    count_ref[0] = total >> 1


def prologue_kernel(count_ref, centers_hbm, charges_hbm, coords_hbm, zsend_ref, current_ref, coords_ref, centers_ref, sem):
    y, z, member = here()
    leaf = (y * NZ + z) * MEMBERS + member
    copies = [
        pltpu.make_async_copy(charges_hbm, current_ref, sem.at[0]),
        pltpu.make_async_copy(coords_hbm, coords_ref, sem.at[1]),
        pltpu.make_async_copy(centers_hbm, centers_ref, sem.at[2]),
    ]
    for copy in copies:
        copy.start()
    for copy in copies:
        copy.wait()
    current = current_ref[...] * (iota((8, 128), 1) < count_ref[0]).astype(f32)
    current_ref[...] = current
    u = jnp.concatenate([coords_ref[...], jnp.zeros((5, 128), f32)], 0)
    center = column3(centers_ref[0, leaf], centers_ref[1, leaf], centers_ref[2, leaf], (8, 128))
    shifted = jnp.concatenate([jnp.zeros((5, 128), f32), coords_ref[...]], 0)
    rows = source_rows(center + HALF_SIDE * u, shifted)
    for k in range(NZ):
        zsend_ref[k, 0:8] = current
        zsend_ref[k, 8:16] = rows


def prep_kernel(
    centers_ref, near_ref, count_ref, steps_ref, boundary_hbm, targets_hbm,
    tsend_ref, held_ref, far_ref, chunk_ref, chunks_ref, proxy_ref,
    mine_ref, wide_ref, targets_ref, sem,
):
    y, z, member = here()
    copies = [
        pltpu.make_async_copy(boundary_hbm, held_ref.at[0], sem.at[0]),
        pltpu.make_async_copy(targets_hbm, targets_ref, sem.at[1]),
    ]
    for copy in copies:
        copy.start()
    make_lists(y, z, near_ref, far_ref, chunk_ref, chunks_ref, mine_ref)
    for copy in copies:
        copy.wait()
    rows = target_rows(jnp.concatenate([targets_ref[...], jnp.zeros((5, 128), f32)], 0))
    for k in range(PLANE):
        tsend_ref[k] = rows
    lane = iota((8, 128), 1)
    row = iota((8, 128), 0)
    steps = jnp.zeros((8, 128), f32)
    for k in range(8):
        steps = jnp.where(row == k, steps_ref[k], steps)
    held_ref[1] = steps
    held_ref[2] = (lane < count_ref[0]).astype(f32)
    p = lane & 31
    offset = jnp.where(
        row == 0,
        pick(p >> 4, cheby_nodes(2)),
        jnp.where(row == 1, pick((p >> 2) & 3, cheby_nodes(4)), jnp.where(row == 2, pick(p & 3, cheby_nodes(4)), 0.0)),
    )
    for block in range(4):
        center = jnp.zeros((8, 128), f32)
        for k in range(4):
            leaf = (y * NZ + block * 4 + k) * MEMBERS + member
            column = column3(centers_ref[0, leaf], centers_ref[1, leaf], centers_ref[2, leaf], (8, 128))
            center = jnp.where((lane >> 5) == k, column, center)
        rows = source_rows(center + HALF_SIDE * offset, 0.0)
        wide_ref[block * 128 : (block + 1) * 128, :DEPTH] = a_block(rows)
    wide_ref[512:544, :DEPTH] = wide_ref[0:32, :DEPTH]
    for other in range(NY):
        for block in range(4):

            @pl.when(block < far_ref[other, FAR_SLOTS - 1])
            def _(other=other, block=block):
                for k in range(4):
                    leaf = far_ref[other, block * 4 + k]
                    base = (other * 4 + block) * 128 + k * 32
                    proxy_ref[base : base + 32] = wide_ref[pl.ds(pl.multiple_of(leaf * 32, 32), 32)]


def charge_blocks(recv_ref, ih_ref, il_ref, far_ref, q_ref, wide_ref):
    far = []
    nt = (((1,), (1,)), ((), ()))
    for k in range(NZ):
        hi, lo = split2(recv_ref[k, 0:8])
        q = jnp.concatenate([hi.astype(f32), lo.astype(f32)], 0).astype(bf16)
        q_ref[k] = q
        both = lax.dot_general(q, ih_ref[k * 32 : (k + 1) * 32], nt, preferred_element_type=f32)
        both = both + lax.dot_general(q, il_ref[k * 32 : (k + 1) * 32], nt, preferred_element_type=f32)
        far.append(both[0:8] + both[8:16])
    for k in range(4):
        wide = jnp.concatenate(far[4 * k : 4 * k + 4], 1)
        hi = wide.astype(bf16).astype(f32)
        wide_ref[k] = jnp.concatenate([hi, wide - hi], 0)
    wide_ref[4] = jnp.zeros((16, 128), f32)
    q_ref[ZERO_BLOCK] = jnp.zeros((16, 128), bf16)
    group = iota((16, 128), 1) >> 5
    for other in range(NY):
        for block in range(4):

            @pl.when(block < far_ref[other, FAR_SLOTS - 1])
            def _(other=other, block=block):
                out = jnp.zeros((16, 128), f32)
                for k in range(4):
                    leaf = far_ref[other, block * 4 + k]
                    moved = pltpu.roll(wide_ref[leaf >> 2], ((4 + k - leaf) & 3) * 32, 1)
                    out = jnp.where(group == k, moved, out)
                q_ref[FAR + other * 4 + block] = out.astype(bf16)


def setup_kernel(far_ref, recv_ref, proxy_ref, a_ref, ih_ref, il_ref, q_ref, wide_ref):
    tables = interp_tables()
    for k in range(NZ):
        rows = recv_ref[k, 8:16]
        a_ref[k * 128 : (k + 1) * 128, :DEPTH] = a_block(rows)
        value = None
        for axis, (roots, scale) in enumerate(tables):
            u = jnp.broadcast_to(rows[5 + axis : 6 + axis], (32, 128))
            line = scale
            for root in roots:
                line = line * (u - root)
            value = line if value is None else value * line
        hi, lo = split2(value)
        ih_ref[k * 32 : (k + 1) * 32] = hi
        il_ref[k * 32 : (k + 1) * 32] = lo
    a_ref[FAR * 128 :] = proxy_ref[...]
    charge_blocks(recv_ref, ih_ref, il_ref, far_ref, q_ref, wide_ref)


def charges_of(chunk_ref, q_ref, i):
    return jnp.concatenate([q_ref[chunk_ref[2 * i + k]] for k in range(2)], 1)


def multiply(chunk_ref, q_ref, acc_ref, i, hi_ref, lo_ref, j):
    q = charges_of(chunk_ref, q_ref, i)
    rows = pl.ds(pl.multiple_of(chunk_ref[CHUNK_OWNER + i] * 16, 16), 16)
    part = jnp.dot(q, hi_ref[j], preferred_element_type=f32) + jnp.dot(q, lo_ref[j], preferred_element_type=f32)
    acc_ref[rows] = acc_ref[rows] + part


def write_sums(acc_ref, out_ref):
    for other in range(NY):
        total = acc_ref[other * 16 : other * 16 + 8] + acc_ref[other * 16 + 8 : other * 16 + 16]
        for k in range(MEMBERS):
            out_ref[other * MEMBERS + k] = total[:, k * 128 : (k + 1) * 128]


def first_kernel(chunk_ref, count_ref, tgt_ref, a_ref, q_ref, out_ref, eh_ref, el_ref, oh_ref, ol_ref, b_ref, acc_ref):
    for other in range(NY):
        h, m, low = split3(jnp.concatenate([tgt_ref[other * MEMBERS + k] for k in range(MEMBERS)], 1))
        b_ref[other] = jnp.concatenate([h, m, h, m, low, h], 0).astype(bf16)
    acc_ref[...] = jnp.zeros_like(acc_ref)
    count = count_ref[0]

    def evaluate(i, hi_ref, lo_ref, j):
        blocks = [chunk_ref[2 * i + k] for k in range(2)]
        starts = [pl.multiple_of(jnp.where(n == ZERO_BLOCK, 0, n) * 128, 128) for n in blocks]
        a = jnp.concatenate([a_ref[pl.ds(n, 128), :DEPTH] for n in starts], 0)
        square = jnp.dot(a, b_ref[chunk_ref[CHUNK_OWNER + i]], preferred_element_type=f32)
        hi, lo = split2(lax.rsqrt(square))
        hi_ref[j] = hi
        lo_ref[j] = lo

    even, odd = (eh_ref, el_ref), (oh_ref, ol_ref)
    mul = functools.partial(multiply, chunk_ref, q_ref, acc_ref)
    evaluate(0, *even, 0)

    def pair(j, carry):
        evaluate(2 * j + 1, *odd, j)
        mul(2 * j, *even, j)
        evaluate(2 * j + 2, *even, j + 1)
        mul(2 * j + 1, *odd, j)
        return carry

    pairs = (count - 1) >> 1
    lax.fori_loop(0, pairs, pair, 0)

    @pl.when((count & 1) == 0)
    def _():
        evaluate(2 * pairs + 1, *odd, pairs)
        mul(2 * pairs, *even, pairs)
        mul(2 * pairs + 1, *odd, pairs)

    @pl.when((count & 1) == 1)
    def _():
        mul(2 * pairs, *even, pairs)

    write_sums(acc_ref, out_ref)


def second_kernel(chunk_ref, count_ref, far_ref, recv_ref, ih_ref, il_ref, eh_ref, el_ref, oh_ref, ol_ref, out_ref, q_ref, wide_ref, acc_ref):
    charge_blocks(recv_ref, ih_ref, il_ref, far_ref, q_ref, wide_ref)
    acc_ref[...] = jnp.zeros_like(acc_ref)
    count = count_ref[0]
    mul = functools.partial(multiply, chunk_ref, q_ref, acc_ref)

    def pair(j, carry):
        mul(2 * j, eh_ref, el_ref, j)
        mul(2 * j + 1, oh_ref, ol_ref, j)
        return carry

    lax.fori_loop(0, count >> 1, pair, 0)

    @pl.when((count & 1) == 1)
    def _():
        mul(count - 1, eh_ref, el_ref, count >> 1)

    write_sums(acc_ref, out_ref)


def update_kernel(scale, last, recv_ref, held_ref, current_ref, new_ref, other_ref):
    parts = [recv_ref[k] for k in range(PLANE)]
    while len(parts) > 1:
        parts = [parts[i] + parts[i + 1] for i in range(0, len(parts), 2)]
    live = held_ref[2]
    residual = live * (held_ref[0] - scale * parts[0])
    new = live * (current_ref[...] + held_ref[1] * residual / (1.0 + jnp.abs(residual)))
    new_ref[...] = new
    if last:
        other_ref[...] = residual
    else:
        for k in range(NZ):
            other_ref[k] = new


VM = pl.BlockSpec(memory_space=pltpu.VMEM)
SM = pl.BlockSpec(memory_space=pltpu.SMEM)
HB = pl.BlockSpec(memory_space=pltpu.HBM)


def sds(shape, dtype=f32):
    return jax.ShapeDtypeStruct(shape, dtype)


def body(leaf_centers, source_coords, target_points, charges, boundary_data, step_sizes, valid_count, near_lists):
    plane = ("y", "x", "core")
    params = pltpu.CompilerParams(vmem_limit_bytes=12 * 2**20)
    small = pltpu.CompilerParams(vmem_limit_bytes=4 * 2**20)
    hbm = functools.partial(pltpu.with_memory_space_constraint, memory_space=pltpu.HBM)
    charges, source_coords, boundary_data, target_points = map(hbm, (charges, source_coords, boundary_data, target_points))
    zsend, current = pl.pallas_call(
        prologue_kernel,
        out_shape=(sds((NZ, 16, 128)), sds((8, 128))),
        in_specs=[SM, HB, HB, HB],
        out_specs=(VM, VM),
        scratch_shapes=[pltpu.VMEM((3, 128), f32), pltpu.SMEM((3, NZ * NY * MEMBERS), f32), pltpu.SemaphoreType.DMA((3,))],
        compiler_params=small,
        name="prologue",
    )(valid_count, hbm(leaf_centers), charges, source_coords)
    recv = lax.all_to_all(zsend, "z", 0, 0, tiled=True)
    tsend, held, far, chunks, count, proxies = pl.pallas_call(
        prep_kernel,
        out_shape=(
            sds((PLANE, 8, 128)),
            sds((3, 8, 128)),
            sds((NY, FAR_SLOTS), jnp.int32),
            sds((CHUNK_SLOTS,), jnp.int32),
            sds((1,), jnp.int32),
            sds((4 * NY * 128, 128), bf16),
        ),
        in_specs=[SM, SM, SM, SM, HB, HB],
        out_specs=(VM, VM, SM, SM, SM, VM),
        scratch_shapes=[
            pltpu.SMEM((NZ + 1,), jnp.int32),
            pltpu.VMEM((544, 128), bf16),
            pltpu.VMEM((3, 128), f32),
            pltpu.SemaphoreType.DMA((2,)),
        ],
        compiler_params=small,
        cost_estimate=pl.CostEstimate(flops=10**9, bytes_accessed=12 * 10**6, transcendentals=0),
        name="prep",
    )(leaf_centers, near_lists.T, valid_count, step_sizes, boundary_data, target_points)
    recv, tsend = lax.optimization_barrier((recv, tsend))
    targets = lax.all_to_all(tsend, plane, 0, 0, tiled=True)
    interp = sds((NZ * 32, 128), bf16)
    a, ih, il, q = pl.pallas_call(
        setup_kernel,
        out_shape=(sds((ZERO_BLOCK * 128, 128), bf16), interp, interp, sds((ZERO_BLOCK + 1, 16, 128), bf16)),
        in_specs=[SM, VM, VM],
        out_specs=(VM,) * 4,
        scratch_shapes=[pltpu.VMEM((5, 16, 128), f32)],
        compiler_params=params,
        cost_estimate=pl.CostEstimate(flops=10**9, bytes_accessed=8 * 10**6, transcendentals=0),
        name="setup",
    )(far, recv, proxies)
    scale = 1.0 / math.sqrt(NY * NZ * MEMBERS * 128)
    half = pltpu.VMEM((PAIRS, 256, MEMBERS * 128), bf16)
    sums, *kernels = pl.pallas_call(
        first_kernel,
        out_shape=(sds((PLANE, 8, 128)), half, half, half, half),
        in_specs=[SM, SM, VM, VM, VM],
        out_specs=(VM,) * 5,
        scratch_shapes=[pltpu.VMEM((NY, DEPTH, MEMBERS * 128), bf16), pltpu.VMEM((NY * 16, MEMBERS * 128), f32)],
        compiler_params=params,
        name="first",
    )(chunks, count, targets, a, q)

    def update(sums, current, last):
        return pl.pallas_call(
            functools.partial(update_kernel, scale, last),
            out_shape=(sds((8, 128)), sds((8, 128) if last else (NZ, 8, 128))),
            in_specs=[VM, VM, VM],
            out_specs=(VM, VM),
            compiler_params=small,
            name="update",
        )(lax.all_to_all(sums, plane, 0, 0, tiled=True), held, current)

    current, zsend = update(sums, current, False)
    recv = lax.all_to_all(zsend, "z", 0, 0, tiled=True)
    sums = pl.pallas_call(
        second_kernel,
        out_shape=sds((PLANE, 8, 128)),
        in_specs=[SM, SM, SM] + [VM] * 7,
        out_specs=VM,
        scratch_shapes=[
            pltpu.VMEM((ZERO_BLOCK + 1, 16, 128), bf16),
            pltpu.VMEM((5, 16, 128), f32),
            pltpu.VMEM((NY * 16, MEMBERS * 128), f32),
        ],
        compiler_params=params,
        name="second",
    )(chunks, count, far, recv, ih, il, *kernels)
    current, residual = update(sums, current, True)
    return (current, residual)


def solution(mesh):
    grid = Mesh(mesh.devices.reshape(NY, NZ, NX, NC), ("y", "z", "x", "core"))
    split = P(None, ("y", "z", "x", "core"))
    in_specs = (P(), split, split, split, split, P(), P(("y", "z", "x", "core")), P())
    return jax.shard_map(body, mesh=grid, in_specs=in_specs, out_specs=(split, split), check_vma=False)
```

```python
import functools
import math

import jax
import jax.numpy as jnp
import numpy as np
from jax import lax
from jax.experimental import pallas as pl
from jax.experimental.pallas import tpu as pltpu
from jax.sharding import Mesh
from jax.sharding import PartitionSpec as P

HALF_SIDE = 0.08
SOFTENING = 0.0025
NY, NZ, NX, NC = 4, 16, 4, 2
MEMBERS = NX * NC
PLANE = NY * MEMBERS
NEAR = 26
DEPTH = 48
FAR = NZ
ZERO_BLOCK = FAR + 4 * NY
FAR_SLOTS = 32
CHUNK_OWNER = 80
CHUNK_SLOTS = 128
PAIRS = 17
TILE = 256
TILES = MEMBERS * 128 // TILE
bf16, f32 = jnp.bfloat16, jnp.float32


def cheby_nodes(number):
    return np.cos(np.pi * (2 * np.arange(number) + 1) / (2 * number))


def pick(index, values):
    out = jnp.full(index.shape, float(values[0]), f32)
    for k in range(1, len(values)):
        out = jnp.where(index == k, float(values[k]), out)
    return out


def iota(shape, dim):
    return lax.broadcasted_iota(jnp.int32, shape, dim)


def split3(v):
    h = v.astype(bf16).astype(f32)
    r = v - h
    m = r.astype(bf16).astype(f32)
    low = (r - m).astype(bf16).astype(f32)
    return h, m, low


def split2(v):
    h = v.astype(bf16)
    return h, (v - h.astype(f32)).astype(bf16)


def source_rows(pts):
    row = iota(pts.shape, 0)
    s = jnp.where(row < 3, pts - 0.5, 0.0)
    norm = jnp.sum(s * s, axis=0, keepdims=True) + SOFTENING
    return jnp.where(row < 3, -2.0 * s, jnp.where(row == 3, norm, jnp.where(row == 4, 1.0, 0.0)))


def target_rows(pts):
    row = iota(pts.shape, 0)
    t = jnp.where(row < 3, pts - 0.5, 0.0)
    norm = jnp.sum(t * t, axis=0, keepdims=True)
    return jnp.where(row < 3, t, jnp.where(row == 3, 1.0, jnp.where(row == 4, norm, 0.0)))


def column3(a, b, c, shape):
    row = iota(shape, 0)
    return jnp.where(row == 0, a, jnp.where(row == 1, b, jnp.where(row == 2, c, 0.0)))


def here():
    member = lax.axis_index("x") * NC + lax.axis_index("core")
    return lax.axis_index("y"), lax.axis_index("z"), member


def a_block(rows):
    h, m, low = split3(rows)
    return jnp.concatenate([h, h, m, m, h, low], 0).T.astype(bf16)


def interp_tables():
    p = iota((32, 128), 0)
    parts = (p >> 4, (p >> 2) & 3, p & 3)
    tables = []
    for index, number in zip(parts, (2, 4, 4)):
        nodes = cheby_nodes(number)
        others = [[nodes[i] for i in range(number) if i != k] for k in range(number)]
        roots = [pick(index, [others[k][j] for k in range(number)]) for j in range(number - 1)]
        scale = pick(index, [1.0 / np.prod([nodes[k] - o for o in others[k]]) for k in range(number)])
        tables.append((roots, scale))
    return tables


def make_lists(y, z, near_ref, far_ref, chunk_ref, count_ref, mine_ref):
    total = jnp.int32(0)
    for other in range(NY):
        for k in range(NZ):
            mine_ref[k] = 0
            far_ref[other, k] = NZ
        mine_ref[z] = (y == other).astype(jnp.int32)
        for j in range(NEAR):
            cluster = near_ref[j, other * NZ + z]
            mine_ref[jnp.where((cluster >> 4) == y, cluster & 15, NZ)] = 1
        near_count = jnp.int32(0)
        far_count = jnp.int32(0)
        for k in range(NZ):
            mine = mine_ref[k]
            chunk_ref[total + near_count] = k
            far_ref[other, far_count] = jnp.where(mine > 0, NZ, k)
            near_count = near_count + mine
            far_count = far_count + 1 - mine
        far_blocks = (far_count + 3) // 4
        start = total + near_count
        for k in range(4):
            chunk_ref[start + k] = FAR + other * 4 + k
        end = start + far_blocks
        chunk_ref[end] = ZERO_BLOCK
        far_ref[other, FAR_SLOTS - 1] = far_blocks
        rounded = ((end + 1) >> 1) << 1

        def owner(k, carry):
            chunk_ref[CHUNK_OWNER + k] = other
            return carry

        lax.fori_loop(total >> 1, rounded >> 1, owner, 0)
        total = rounded
    count_ref[0] = total >> 1


def prologue_kernel(count_ref, charges_hbm, coords_hbm, zsend_ref, current_ref, coords_ref, sem):
    copies = [pltpu.make_async_copy(charges_hbm, current_ref, sem.at[0]), pltpu.make_async_copy(coords_hbm, coords_ref, sem.at[1])]
    for copy in copies:
        copy.start()
    for copy in copies:
        copy.wait()
    current = current_ref[...] * (iota((8, 128), 1) < count_ref[0]).astype(f32)
    current_ref[...] = current
    coords = jnp.concatenate([coords_ref[...], jnp.zeros((1, 128), f32)], 0)
    for k in range(NZ):
        zsend_ref[3 * k] = current[0:4]
        zsend_ref[3 * k + 1] = current[4:8]
        zsend_ref[3 * k + 2] = coords


def prep_kernel(
    centers_ref, near_ref, count_ref, steps_ref, boundary_hbm, targets_hbm,
    tsend_ref, held_ref, far_ref, chunk_ref, chunks_ref, proxy_ref,
    mine_ref, wide_ref, targets_ref, sem,
):
    y, z, member = here()
    copies = [
        pltpu.make_async_copy(boundary_hbm, held_ref.at[0], sem.at[0]),
        pltpu.make_async_copy(targets_hbm, targets_ref, sem.at[1]),
    ]
    for copy in copies:
        copy.start()
    make_lists(y, z, near_ref, far_ref, chunk_ref, chunks_ref, mine_ref)
    for copy in copies:
        copy.wait()
    rows = target_rows(jnp.concatenate([targets_ref[...], jnp.zeros((5, 128), f32)], 0))
    for k in range(PLANE):
        tsend_ref[k] = rows
    lane = iota((8, 128), 1)
    row = iota((8, 128), 0)
    steps = jnp.zeros((8, 128), f32)
    for k in range(8):
        steps = jnp.where(row == k, steps_ref[k], steps)
    held_ref[1] = steps
    held_ref[2] = (lane < count_ref[0]).astype(f32)
    p = lane & 31
    offset = jnp.where(
        row == 0,
        pick(p >> 4, cheby_nodes(2)),
        jnp.where(row == 1, pick((p >> 2) & 3, cheby_nodes(4)), jnp.where(row == 2, pick(p & 3, cheby_nodes(4)), 0.0)),
    )
    for block in range(4):
        center = jnp.zeros((8, 128), f32)
        for k in range(4):
            leaf = (y * NZ + block * 4 + k) * MEMBERS + member
            column = column3(centers_ref[0, leaf], centers_ref[1, leaf], centers_ref[2, leaf], (8, 128))
            center = jnp.where((lane >> 5) == k, column, center)
        rows = source_rows(center + HALF_SIDE * offset)
        wide_ref[block * 128 : (block + 1) * 128, :DEPTH] = a_block(rows)
    wide_ref[512:544, :DEPTH] = wide_ref[0:32, :DEPTH]
    for other in range(NY):
        for block in range(4):

            @pl.when(block < far_ref[other, FAR_SLOTS - 1])
            def _(other=other, block=block):
                for k in range(4):
                    leaf = far_ref[other, block * 4 + k]
                    base = (other * 4 + block) * 128 + k * 32
                    proxy_ref[base : base + 32] = wide_ref[pl.ds(pl.multiple_of(leaf * 32, 32), 32)]


def charge_blocks(charges, ih_ref, il_ref, far_ref, q_ref, wide_ref):
    far = []
    nt = (((1,), (1,)), ((), ()))
    for k in range(NZ):
        hi, lo = split2(charges(k))
        q = jnp.concatenate([hi.astype(f32), lo.astype(f32)], 0).astype(bf16)
        q_ref[k] = q
        both = lax.dot_general(q, ih_ref[k * 32 : (k + 1) * 32], nt, preferred_element_type=f32)
        both = both + lax.dot_general(q, il_ref[k * 32 : (k + 1) * 32], nt, preferred_element_type=f32)
        far.append(both[0:8] + both[8:16])
    for k in range(4):
        wide = jnp.concatenate(far[4 * k : 4 * k + 4], 1)
        hi = wide.astype(bf16).astype(f32)
        wide_ref[k] = jnp.concatenate([hi, wide - hi], 0)
    wide_ref[4] = jnp.zeros((16, 128), f32)
    q_ref[ZERO_BLOCK] = jnp.zeros((16, 128), bf16)
    group = iota((16, 128), 1) >> 5
    for other in range(NY):
        for block in range(4):
            out = None
            for k in range(4):
                leaf = far_ref[other, block * 4 + k]
                moved = pltpu.roll(wide_ref[leaf >> 2], ((4 + k - leaf) & 3) * 32, 1)
                out = moved if out is None else jnp.where(group == k, moved, out)
            q_ref[FAR + other * 4 + block] = out.astype(bf16)


def setup_kernel(far_ref, centers_ref, recv_ref, proxy_ref, a_ref, ih_ref, il_ref, q_ref, wide_ref):
    tables = interp_tables()
    y, _, member = here()
    for k in range(NZ):
        rows = recv_ref[3 * k + 2]
        leaf = (y * NZ + k) * MEMBERS + member
        center = column3(centers_ref[0, leaf], centers_ref[1, leaf], centers_ref[2, leaf], (8, 128))
        points = center + HALF_SIDE * jnp.concatenate([rows, jnp.zeros((4, 128), f32)], 0)
        a_ref[k * 128 : (k + 1) * 128, :DEPTH] = a_block(source_rows(points))
        value = None
        for axis, (roots, scale) in enumerate(tables):
            u = jnp.broadcast_to(rows[axis : axis + 1], (32, 128))
            line = scale
            for root in roots:
                line = line * (u - root)
            value = line if value is None else value * line
        hi, lo = split2(value)
        ih_ref[k * 32 : (k + 1) * 32] = hi
        il_ref[k * 32 : (k + 1) * 32] = lo
    a_ref[FAR * 128 :] = proxy_ref[...]
    charge_blocks(lambda k: jnp.concatenate([recv_ref[3 * k], recv_ref[3 * k + 1]], 0), ih_ref, il_ref, far_ref, q_ref, wide_ref)


def multiply_tile(chunk_ref, q_ref, acc_ref, i, hi_ref, lo_ref, j, t):
    q = jnp.concatenate([q_ref[chunk_ref[2 * i + k]] for k in range(2)], 1)
    rows = pl.ds(pl.multiple_of(chunk_ref[CHUNK_OWNER + i] * 16, 16), 16)
    cols = slice(t * TILE, (t + 1) * TILE)
    both = jnp.concatenate([hi_ref[j, t], lo_ref[j, t]], 0)
    acc_ref[rows, cols] = acc_ref[rows, cols] + jnp.dot(jnp.concatenate([q, q], 1), both, preferred_element_type=f32)


def write_sums(acc_ref, out_ref):
    for other in range(NY):
        total = acc_ref[other * 16 : other * 16 + 8] + acc_ref[other * 16 + 8 : other * 16 + 16]
        for k in range(MEMBERS):
            out_ref[other * MEMBERS + k] = total[:, k * 128 : (k + 1) * 128]


def first_kernel(chunk_ref, count_ref, tgt_ref, a_ref, q_ref, out_ref, eh_ref, el_ref, oh_ref, ol_ref, b_ref, acc_ref):
    for other in range(NY):
        h, m, low = split3(jnp.concatenate([tgt_ref[other * MEMBERS + k] for k in range(MEMBERS)], 1))
        b_ref[other] = jnp.concatenate([h, m, h, m, low, h], 0).astype(bf16)
    acc_ref[...] = jnp.zeros_like(acc_ref)
    count = count_ref[0]

    def rows_of(i):
        blocks = [chunk_ref[2 * i + k] for k in range(2)]
        starts = [pl.multiple_of(jnp.where(n == ZERO_BLOCK, 0, n) * 128, 128) for n in blocks]
        return jnp.concatenate([a_ref[pl.ds(n, 128), :DEPTH] for n in starts], 0), chunk_ref[CHUNK_OWNER + i]

    def evaluate_tile(rows, hi_ref, lo_ref, j, t):
        square = jnp.dot(rows[0], b_ref[rows[1], :, t * TILE : (t + 1) * TILE], preferred_element_type=f32)
        hi, lo = split2(lax.rsqrt(square))
        hi_ref[j, t] = hi
        lo_ref[j, t] = lo

    even, odd = (eh_ref, el_ref), (oh_ref, ol_ref)
    mul = functools.partial(multiply_tile, chunk_ref, q_ref, acc_ref)

    def both(done, source, js, new, target, jt):
        rows = rows_of(new)
        for t in range(TILES):
            mul(done, *source, js, t)
            evaluate_tile(rows, *target, jt, t)

    rows = rows_of(0)
    for t in range(TILES):
        evaluate_tile(rows, *even, 0, t)

    def pair(j, carry):
        both(2 * j, even, j, 2 * j + 1, odd, j)
        both(2 * j + 1, odd, j, 2 * j + 2, even, j + 1)
        return carry

    pairs = (count - 1) >> 1
    lax.fori_loop(0, pairs, pair, 0)

    @pl.when((count & 1) == 0)
    def _():
        both(2 * pairs, even, pairs, 2 * pairs + 1, odd, pairs)
        for t in range(TILES):
            mul(2 * pairs + 1, *odd, pairs, t)

    @pl.when((count & 1) == 1)
    def _():
        for t in range(TILES):
            mul(2 * pairs, *even, pairs, t)

    write_sums(acc_ref, out_ref)


def second_kernel(chunk_ref, count_ref, far_ref, recv_ref, ih_ref, il_ref, eh_ref, el_ref, oh_ref, ol_ref, out_ref, q_ref, wide_ref, acc_ref):
    charge_blocks(lambda k: recv_ref[k], ih_ref, il_ref, far_ref, q_ref, wide_ref)
    acc_ref[...] = jnp.zeros_like(acc_ref)
    count = count_ref[0]
    mul = functools.partial(multiply_tile, chunk_ref, q_ref, acc_ref)

    def pair(j):
        for t in range(TILES):
            mul(2 * j, eh_ref, el_ref, j, t)
            mul(2 * j + 1, oh_ref, ol_ref, j, t)

    def four(j, carry):
        pair(2 * j)
        pair(2 * j + 1)
        return carry

    lax.fori_loop(0, count >> 2, four, 0)

    @pl.when((count & 2) == 2)
    def _():
        pair((count >> 2) * 2)

    @pl.when((count & 1) == 1)
    def _():
        for t in range(TILES):
            mul(count - 1, eh_ref, el_ref, count >> 1, t)

    write_sums(acc_ref, out_ref)


def update_kernel(scale, last, recv_ref, held_ref, current_ref, new_ref, other_ref):
    parts = [recv_ref[k] for k in range(PLANE)]
    while len(parts) > 1:
        parts = [parts[i] + parts[i + 1] for i in range(0, len(parts), 2)]
    live = held_ref[2]
    residual = live * (held_ref[0] - scale * parts[0])
    new = live * (current_ref[...] + held_ref[1] * residual / (1.0 + jnp.abs(residual)))
    new_ref[...] = new
    if last:
        other_ref[...] = residual
    else:
        for k in range(NZ):
            other_ref[k] = new


VM = pl.BlockSpec(memory_space=pltpu.VMEM)
SM = pl.BlockSpec(memory_space=pltpu.SMEM)
HB = pl.BlockSpec(memory_space=pltpu.HBM)


def sds(shape, dtype=f32):
    return jax.ShapeDtypeStruct(shape, dtype)


def body(leaf_centers, source_coords, target_points, charges, boundary_data, step_sizes, valid_count, near_lists):
    plane = ("y", "x", "core")
    params = pltpu.CompilerParams(vmem_limit_bytes=12 * 2**20)
    small = pltpu.CompilerParams(vmem_limit_bytes=4 * 2**20)
    hbm = functools.partial(pltpu.with_memory_space_constraint, memory_space=pltpu.HBM)
    charges, source_coords, boundary_data, target_points = map(hbm, (charges, source_coords, boundary_data, target_points))
    zsend, current = pl.pallas_call(
        prologue_kernel,
        out_shape=(sds((3 * NZ, 4, 128)), sds((8, 128))),
        in_specs=[SM, HB, HB],
        out_specs=(VM, VM),
        scratch_shapes=[pltpu.VMEM((3, 128), f32), pltpu.SemaphoreType.DMA((2,))],
        compiler_params=small,
        name="prologue",
    )(valid_count, charges, source_coords)
    recv = lax.all_to_all(zsend, "z", 0, 0, tiled=True)
    tsend, held, far, chunks, count, proxies = pl.pallas_call(
        prep_kernel,
        out_shape=(
            sds((PLANE, 8, 128)),
            sds((3, 8, 128)),
            sds((NY, FAR_SLOTS), jnp.int32),
            sds((CHUNK_SLOTS,), jnp.int32),
            sds((1,), jnp.int32),
            sds((4 * NY * 128, 128), bf16),
        ),
        in_specs=[SM, SM, SM, SM, HB, HB],
        out_specs=(VM, VM, SM, SM, SM, VM),
        scratch_shapes=[
            pltpu.SMEM((NZ + 1,), jnp.int32),
            pltpu.VMEM((544, 128), bf16),
            pltpu.VMEM((3, 128), f32),
            pltpu.SemaphoreType.DMA((2,)),
        ],
        compiler_params=small,
        cost_estimate=pl.CostEstimate(flops=10**9, bytes_accessed=12 * 10**6, transcendentals=0),
        name="prep",
    )(leaf_centers, near_lists.T, valid_count, step_sizes, boundary_data, target_points)
    recv, tsend = lax.optimization_barrier((recv, tsend))
    targets = lax.all_to_all(tsend, plane, 0, 0, tiled=True)
    interp = sds((NZ * 32, 128), bf16)
    a, ih, il, q = pl.pallas_call(
        setup_kernel,
        out_shape=(sds((ZERO_BLOCK * 128, 128), bf16), interp, interp, sds((ZERO_BLOCK + 1, 16, 128), bf16)),
        in_specs=[SM, SM, VM, VM],
        out_specs=(VM,) * 4,
        scratch_shapes=[pltpu.VMEM((5, 16, 128), f32)],
        compiler_params=params,
        cost_estimate=pl.CostEstimate(flops=10**9, bytes_accessed=8 * 10**6, transcendentals=0),
        name="setup",
    )(far, leaf_centers, recv, proxies)
    scale = 1.0 / math.sqrt(NY * NZ * MEMBERS * 128)
    half = pltpu.VMEM((PAIRS, TILES, 256, TILE), bf16)
    sums, *kernels = pl.pallas_call(
        first_kernel,
        out_shape=(sds((PLANE, 8, 128)), half, half, half, half),
        in_specs=[SM, SM, VM, VM, VM],
        out_specs=(VM,) * 5,
        scratch_shapes=[pltpu.VMEM((NY, DEPTH, MEMBERS * 128), bf16), pltpu.VMEM((NY * 16, MEMBERS * 128), f32)],
        compiler_params=params,
        name="first",
    )(chunks, count, targets, a, q)

    def update(sums, current, last):
        return pl.pallas_call(
            functools.partial(update_kernel, scale, last),
            out_shape=(sds((8, 128)), sds((8, 128) if last else (NZ, 8, 128))),
            in_specs=[VM, VM, VM],
            out_specs=(VM, VM),
            compiler_params=small,
            name="update",
        )(lax.all_to_all(sums, plane, 0, 0, tiled=True), held, current)

    current, zsend = update(sums, current, False)
    recv = lax.all_to_all(zsend, "z", 0, 0, tiled=True)
    sums = pl.pallas_call(
        second_kernel,
        out_shape=sds((PLANE, 8, 128)),
        in_specs=[SM, SM, SM] + [VM] * 7,
        out_specs=VM,
        scratch_shapes=[
            pltpu.VMEM((ZERO_BLOCK + 1, 16, 128), bf16),
            pltpu.VMEM((5, 16, 128), f32),
            pltpu.VMEM((NY * 16, MEMBERS * 128), f32),
        ],
        compiler_params=params,
        name="second",
    )(chunks, count, far, recv, ih, il, *kernels)
    current, residual = update(sums, current, True)
    return (current, residual)


def solution(mesh):
    grid = Mesh(mesh.devices.reshape(NY, NZ, NX, NC), ("y", "z", "x", "core"))
    split = P(None, ("y", "z", "x", "core"))
    in_specs = (P(), split, split, split, split, P(), P(("y", "z", "x", "core")), P())
    return jax.shard_map(body, mesh=grid, in_specs=in_specs, out_specs=(split, split), check_vma=False)
```

```python
import functools
import math

import jax
import jax.numpy as jnp
import numpy as np
from jax import lax
from jax.experimental import pallas as pl
from jax.experimental.pallas import tpu as pltpu
from jax.sharding import Mesh
from jax.sharding import PartitionSpec as P

HALF_SIDE = 0.08
SOFTENING = 0.0025
NY, NZ, NX, NC = 4, 16, 4, 2
MEMBERS = NX * NC
PLANE = NY * MEMBERS
NEAR = 26
DEPTH = 48
FAR = NZ
ZERO_BLOCK = FAR + 4 * NY
FAR_SLOTS = 16
CHUNK_OWNER = 80
CHUNK_SLOTS = 128
PAIRS = 17
TILE = 256
TILES = MEMBERS * 128 // TILE
bf16, f32 = jnp.bfloat16, jnp.float32


def cheby_nodes(number):
    return np.cos(np.pi * (2 * np.arange(number) + 1) / (2 * number))


def pick(index, values):
    out = jnp.full(index.shape, float(values[0]), f32)
    for k in range(1, len(values)):
        out = jnp.where(index == k, float(values[k]), out)
    return out


def iota(shape, dim):
    return lax.broadcasted_iota(jnp.int32, shape, dim)


def split3(v):
    h = v.astype(bf16).astype(f32)
    r = v - h
    m = r.astype(bf16).astype(f32)
    low = (r - m).astype(bf16).astype(f32)
    return h, m, low


def split2(v):
    h = v.astype(bf16)
    return h, (v - h.astype(f32)).astype(bf16)


def source_rows(pts):
    row = iota(pts.shape, 0)
    s = jnp.where(row < 3, pts - 0.5, 0.0)
    norm = jnp.sum(s * s, axis=0, keepdims=True) + SOFTENING
    return jnp.where(row < 3, -2.0 * s, jnp.where(row == 3, norm, jnp.where(row == 4, 1.0, 0.0)))


def target_rows(pts):
    row = iota(pts.shape, 0)
    t = jnp.where(row < 3, pts - 0.5, 0.0)
    norm = jnp.sum(t * t, axis=0, keepdims=True)
    return jnp.where(row < 3, t, jnp.where(row == 3, 1.0, jnp.where(row == 4, norm, 0.0)))


def column3(a, b, c, shape):
    row = iota(shape, 0)
    return jnp.where(row == 0, a, jnp.where(row == 1, b, jnp.where(row == 2, c, 0.0)))


def here():
    member = lax.axis_index("x") * NC + lax.axis_index("core")
    return lax.axis_index("y"), lax.axis_index("z"), member


def a_block(rows):
    h, m, low = split3(rows)
    return jnp.concatenate([h, h, m, m, h, low], 0).T.astype(bf16)


def interp_tables():
    p = iota((32, 128), 0)
    parts = (p >> 4, (p >> 2) & 3, p & 3)
    tables = []
    for index, number in zip(parts, (2, 4, 4)):
        nodes = cheby_nodes(number)
        others = [[nodes[i] for i in range(number) if i != k] for k in range(number)]
        roots = [pick(index, [others[k][j] for k in range(number)]) for j in range(number - 1)]
        scale = pick(index, [1.0 / np.prod([nodes[k] - o for o in others[k]]) for k in range(number)])
        tables.append((roots, scale))
    return tables


def make_lists(y, z, near_ref, far_ref, chunk_ref, count_ref):
    total = jnp.int32(0)
    for other in range(NY):
        bits = jnp.where(y == other, 1 << z, 0)
        for j in range(NEAR):
            cluster = near_ref[j, other * NZ + z]
            bits = bits | jnp.where((cluster >> 4) == y, 1 << (cluster & 15), 0)
        near_count = jnp.int32(0)
        for k in range(NZ):
            far_ref[other, k] = NZ
        for k in range(NZ):
            mine = (bits >> k) & 1
            chunk_ref[total + near_count] = k
            far_ref[other, k - near_count] = jnp.where(mine > 0, NZ, k)
            near_count = near_count + mine
        far_blocks = (NZ + 3 - near_count) >> 2
        start = total + near_count
        for k in range(4):
            chunk_ref[start + k] = FAR + other * 4 + k
        end = start + far_blocks
        chunk_ref[end] = ZERO_BLOCK
        for k in range(8):
            chunk_ref[CHUNK_OWNER + (total >> 1) + k] = other
        total = ((end + 1) >> 1) << 1
    count_ref[0] = total >> 1


def prologue_kernel(count_ref, charges_hbm, coords_hbm, zsend_ref, current_ref, coords_ref, sem):
    copies = [pltpu.make_async_copy(charges_hbm, current_ref, sem.at[0]), pltpu.make_async_copy(coords_hbm, coords_ref, sem.at[1])]
    for copy in copies:
        copy.start()
    for copy in copies:
        copy.wait()
    current = current_ref[...] * (iota((8, 128), 1) < count_ref[0]).astype(f32)
    current_ref[...] = current
    coords = jnp.concatenate([coords_ref[...], jnp.zeros((1, 128), f32)], 0)
    for k in range(NZ):
        zsend_ref[3 * k] = current[0:4]
        zsend_ref[3 * k + 1] = current[4:8]
        zsend_ref[3 * k + 2] = coords


def prep_kernel(
    count_ref, steps_ref, centers_hbm, near_hbm, boundary_hbm, targets_hbm,
    tsend_ref, held_ref, near_ref, center_ref, proxy_ref,
    centers_ref, targets_ref, sem,
):
    y, _, member = here()
    moves = ((targets_hbm, targets_ref), (centers_hbm, centers_ref), (boundary_hbm, held_ref.at[0]), (near_hbm, near_ref))
    copies = [pltpu.make_async_copy(source, target, sem.at[k]) for k, (source, target) in enumerate(moves)]
    for copy in copies:
        copy.start()
    lane = iota((8, 128), 1)
    row = iota((8, 128), 0)
    p = lane & 31
    offset = jnp.where(
        row == 0,
        pick(p >> 4, cheby_nodes(2)),
        jnp.where(row == 1, pick((p >> 2) & 3, cheby_nodes(4)), jnp.where(row == 2, pick(p & 3, cheby_nodes(4)), 0.0)),
    )
    steps = jnp.zeros((8, 128), f32)
    for k in range(8):
        steps = jnp.where(row == k, steps_ref[k], steps)
    held_ref[1] = steps
    held_ref[2] = (lane < count_ref[0]).astype(f32)
    for copy in copies:
        copy.wait()
    rows = target_rows(jnp.concatenate([targets_ref[...], jnp.zeros((5, 128), f32)], 0))
    for k in range(PLANE):
        tsend_ref[k] = rows
    for block in range(4):
        center = jnp.zeros((8, 128), f32)
        for k in range(4):
            leaf = (y * NZ + block * 4 + k) * MEMBERS + member
            column = column3(centers_ref[0, leaf], centers_ref[1, leaf], centers_ref[2, leaf], (8, 128))
            center_ref[block * 4 + k] = column
            center = jnp.where((lane >> 5) == k, column, center)
        rows = source_rows(center + HALF_SIDE * offset)
        proxy_ref[block * 128 : (block + 1) * 128, :DEPTH] = a_block(rows)
    proxy_ref[512:544, :DEPTH] = proxy_ref[0:32, :DEPTH]


def charge_blocks(charges, ih_ref, il_ref, far_ref, q_ref, wide_ref):
    far = []
    nt = (((1,), (1,)), ((), ()))
    for k in range(NZ):
        hi, lo = split2(charges(k))
        q = jnp.concatenate([hi.astype(f32), lo.astype(f32)], 0).astype(bf16)
        q_ref[k] = q
        both = lax.dot_general(q, ih_ref[k * 32 : (k + 1) * 32], nt, preferred_element_type=f32)
        both = both + lax.dot_general(q, il_ref[k * 32 : (k + 1) * 32], nt, preferred_element_type=f32)
        far.append(both[0:8] + both[8:16])
    for k in range(4):
        wide = jnp.concatenate(far[4 * k : 4 * k + 4], 1)
        hi = wide.astype(bf16).astype(f32)
        wide_ref[k] = jnp.concatenate([hi, wide - hi], 0)
    wide_ref[4] = jnp.zeros((16, 128), f32)
    q_ref[ZERO_BLOCK] = jnp.zeros((16, 128), bf16)
    group = iota((16, 128), 1) >> 5
    for other in range(NY):
        for block in range(4):
            out = None
            for k in range(4):
                leaf = far_ref[other, block * 4 + k]
                moved = pltpu.roll(wide_ref[leaf >> 2], ((4 + k - leaf) & 3) * 32, 1)
                out = moved if out is None else jnp.where(group == k, moved, out)
            q_ref[FAR + other * 4 + block] = out.astype(bf16)


def setup_kernel(
    near_ref, center_ref, recv_ref, proxy_ref, a_ref, ih_ref, il_ref, q_ref, far_ref, chunk_ref, count_ref, wide_ref
):
    y, z, _ = here()
    make_lists(y, z, near_ref, far_ref, chunk_ref, count_ref)
    tables = interp_tables()
    for k in range(NZ):
        rows = recv_ref[3 * k + 2]
        points = center_ref[k] + HALF_SIDE * jnp.concatenate([rows, jnp.zeros((4, 128), f32)], 0)
        a_ref[k * 128 : (k + 1) * 128, :DEPTH] = a_block(source_rows(points))
        value = None
        for axis, (roots, scale) in enumerate(tables):
            u = jnp.broadcast_to(rows[axis : axis + 1], (32, 128))
            line = scale
            for root in roots:
                line = line * (u - root)
            value = line if value is None else value * line
        hi, lo = split2(value)
        ih_ref[k * 32 : (k + 1) * 32] = hi
        il_ref[k * 32 : (k + 1) * 32] = lo
    for other in range(NY):
        for k in range(NZ):
            base = (FAR + other * 4) * 128 + k * 32
            a_ref[base : base + 32] = proxy_ref[pl.ds(pl.multiple_of(far_ref[other, k] * 32, 32), 32)]
    charge_blocks(lambda k: jnp.concatenate([recv_ref[3 * k], recv_ref[3 * k + 1]], 0), ih_ref, il_ref, far_ref, q_ref, wide_ref)


def multiply_tile(chunk_ref, q_ref, acc_ref, i, hi_ref, lo_ref, j, t):
    q = jnp.concatenate([q_ref[chunk_ref[2 * i + k]] for k in range(2)], 1)
    rows = pl.ds(pl.multiple_of(chunk_ref[CHUNK_OWNER + i] * 16, 16), 16)
    cols = slice(t * TILE, (t + 1) * TILE)
    both = jnp.concatenate([hi_ref[j, t], lo_ref[j, t]], 0)
    acc_ref[rows, cols] = acc_ref[rows, cols] + jnp.dot(jnp.concatenate([q, q], 1), both, preferred_element_type=f32)


def write_sums(acc_ref, out_ref):
    for other in range(NY):
        total = acc_ref[other * 16 : other * 16 + 8] + acc_ref[other * 16 + 8 : other * 16 + 16]
        for k in range(MEMBERS):
            out_ref[other * MEMBERS + k] = total[:, k * 128 : (k + 1) * 128]


def first_kernel(chunk_ref, count_ref, tgt_ref, a_ref, q_ref, out_ref, eh_ref, el_ref, oh_ref, ol_ref, b_ref, acc_ref):
    for other in range(NY):
        h, m, low = split3(jnp.concatenate([tgt_ref[other * MEMBERS + k] for k in range(MEMBERS)], 1))
        b_ref[other] = jnp.concatenate([h, m, h, m, low, h], 0).astype(bf16)
    acc_ref[...] = jnp.zeros_like(acc_ref)
    count = count_ref[0]

    def rows_of(i):
        blocks = [chunk_ref[2 * i + k] for k in range(2)]
        starts = [pl.multiple_of(jnp.where(n == ZERO_BLOCK, 0, n) * 128, 128) for n in blocks]
        return jnp.concatenate([a_ref[pl.ds(n, 128), :DEPTH] for n in starts], 0), chunk_ref[CHUNK_OWNER + i]

    def evaluate_tile(rows, hi_ref, lo_ref, j, t):
        square = jnp.dot(rows[0], b_ref[rows[1], :, t * TILE : (t + 1) * TILE], preferred_element_type=f32)
        hi, lo = split2(lax.rsqrt(square))
        hi_ref[j, t] = hi
        lo_ref[j, t] = lo

    even, odd = (eh_ref, el_ref), (oh_ref, ol_ref)
    mul = functools.partial(multiply_tile, chunk_ref, q_ref, acc_ref)

    def both(done, source, js, new, target, jt):
        rows = rows_of(new)
        for t in range(TILES):
            mul(done, *source, js, t)
            evaluate_tile(rows, *target, jt, t)

    rows = rows_of(0)
    for t in range(TILES):
        evaluate_tile(rows, *even, 0, t)

    def pair(j, carry):
        both(2 * j, even, j, 2 * j + 1, odd, j)
        both(2 * j + 1, odd, j, 2 * j + 2, even, j + 1)
        return carry

    pairs = (count - 1) >> 1
    lax.fori_loop(0, pairs, pair, 0)

    @pl.when((count & 1) == 0)
    def _():
        both(2 * pairs, even, pairs, 2 * pairs + 1, odd, pairs)
        for t in range(TILES):
            mul(2 * pairs + 1, *odd, pairs, t)

    @pl.when((count & 1) == 1)
    def _():
        for t in range(TILES):
            mul(2 * pairs, *even, pairs, t)

    write_sums(acc_ref, out_ref)


def second_kernel(chunk_ref, count_ref, far_ref, recv_ref, ih_ref, il_ref, eh_ref, el_ref, oh_ref, ol_ref, out_ref, q_ref, wide_ref, acc_ref):
    charge_blocks(lambda k: recv_ref[k], ih_ref, il_ref, far_ref, q_ref, wide_ref)
    acc_ref[...] = jnp.zeros_like(acc_ref)
    count = count_ref[0]
    mul = functools.partial(multiply_tile, chunk_ref, q_ref, acc_ref)

    def pair(j):
        for t in range(TILES):
            mul(2 * j, eh_ref, el_ref, j, t)
            mul(2 * j + 1, oh_ref, ol_ref, j, t)

    def four(j, carry):
        pair(2 * j)
        pair(2 * j + 1)
        return carry

    lax.fori_loop(0, count >> 2, four, 0)

    @pl.when((count & 2) == 2)
    def _():
        pair((count >> 2) * 2)

    @pl.when((count & 1) == 1)
    def _():
        for t in range(TILES):
            mul(count - 1, eh_ref, el_ref, count >> 1, t)

    write_sums(acc_ref, out_ref)


def update_kernel(scale, last, recv_ref, held_ref, current_ref, new_ref, other_ref):
    parts = [recv_ref[k] for k in range(PLANE)]
    while len(parts) > 1:
        parts = [parts[i] + parts[i + 1] for i in range(0, len(parts), 2)]
    live = held_ref[2]
    residual = live * (held_ref[0] - scale * parts[0])
    new = live * (current_ref[...] + held_ref[1] * residual / (1.0 + jnp.abs(residual)))
    new_ref[...] = new
    if last:
        other_ref[...] = residual
    else:
        for k in range(NZ):
            other_ref[k] = new


VM = pl.BlockSpec(memory_space=pltpu.VMEM)
SM = pl.BlockSpec(memory_space=pltpu.SMEM)
HB = pl.BlockSpec(memory_space=pltpu.HBM)


def sds(shape, dtype=f32):
    return jax.ShapeDtypeStruct(shape, dtype)


def body(leaf_centers, source_coords, target_points, charges, boundary_data, step_sizes, valid_count, near_lists):
    plane = ("y", "x", "core")
    params = pltpu.CompilerParams(vmem_limit_bytes=12 * 2**20)
    small = pltpu.CompilerParams(vmem_limit_bytes=4 * 2**20)
    hbm = functools.partial(pltpu.with_memory_space_constraint, memory_space=pltpu.HBM)
    charges, source_coords, boundary_data, target_points = map(hbm, (charges, source_coords, boundary_data, target_points))
    zsend, current = pl.pallas_call(
        prologue_kernel,
        out_shape=(sds((3 * NZ, 4, 128)), sds((8, 128))),
        in_specs=[SM, HB, HB],
        out_specs=(VM, VM),
        scratch_shapes=[pltpu.VMEM((3, 128), f32), pltpu.SemaphoreType.DMA((2,))],
        compiler_params=small,
        name="prologue",
    )(valid_count, charges, source_coords)
    recv = lax.all_to_all(zsend, "z", 0, 0, tiled=True)
    tsend, held, near, centers, proxies = pl.pallas_call(
        prep_kernel,
        out_shape=(
            sds((PLANE, 8, 128)),
            sds((3, 8, 128)),
            sds((NEAR, NY * NZ), jnp.int32),
            sds((NZ, 8, 128)),
            sds((544, 128), bf16),
        ),
        in_specs=[SM, SM, HB, HB, HB, HB],
        out_specs=(VM,) * 5,
        scratch_shapes=[pltpu.SMEM((3, NZ * NY * MEMBERS), f32), pltpu.VMEM((3, 128), f32), pltpu.SemaphoreType.DMA((4,))],
        compiler_params=small,
        cost_estimate=pl.CostEstimate(flops=10**9, bytes_accessed=12 * 10**6, transcendentals=0),
        name="prep",
    )(valid_count, step_sizes, hbm(leaf_centers), hbm(near_lists.T), boundary_data, target_points)
    recv, tsend = lax.optimization_barrier((recv, tsend))
    targets = lax.all_to_all(tsend, plane, 0, 0, tiled=True)
    interp = sds((NZ * 32, 128), bf16)
    a, ih, il, q, far, chunks, count = pl.pallas_call(
        setup_kernel,
        out_shape=(
            sds((ZERO_BLOCK * 128, 128), bf16),
            interp,
            interp,
            sds((ZERO_BLOCK + 1, 16, 128), bf16),
            sds((NY, FAR_SLOTS), jnp.int32),
            sds((CHUNK_SLOTS,), jnp.int32),
            sds((1,), jnp.int32),
        ),
        in_specs=[SM, VM, VM, VM],
        out_specs=(VM,) * 4 + (SM,) * 3,
        scratch_shapes=[pltpu.VMEM((5, 16, 128), f32)],
        compiler_params=params,
        cost_estimate=pl.CostEstimate(flops=10**9, bytes_accessed=8 * 10**6, transcendentals=0),
        name="setup",
    )(near, centers, recv, proxies)
    scale = 1.0 / math.sqrt(NY * NZ * MEMBERS * 128)
    half = pltpu.VMEM((PAIRS, TILES, 256, TILE), bf16)
    sums, *kernels = pl.pallas_call(
        first_kernel,
        out_shape=(sds((PLANE, 8, 128)), half, half, half, half),
        in_specs=[SM, SM, VM, VM, VM],
        out_specs=(VM,) * 5,
        scratch_shapes=[pltpu.VMEM((NY, DEPTH, MEMBERS * 128), bf16), pltpu.VMEM((NY * 16, MEMBERS * 128), f32)],
        compiler_params=params,
        name="first",
    )(chunks, count, targets, a, q)

    def update(sums, current, last):
        return pl.pallas_call(
            functools.partial(update_kernel, scale, last),
            out_shape=(sds((8, 128)), sds((8, 128) if last else (NZ, 8, 128))),
            in_specs=[VM, VM, VM],
            out_specs=(VM, VM),
            compiler_params=small,
            name="update",
        )(lax.all_to_all(sums, plane, 0, 0, tiled=True), held, current)

    current, zsend = update(sums, current, False)
    recv = lax.all_to_all(zsend, "z", 0, 0, tiled=True)
    sums = pl.pallas_call(
        second_kernel,
        out_shape=sds((PLANE, 8, 128)),
        in_specs=[SM, SM, SM] + [VM] * 7,
        out_specs=VM,
        scratch_shapes=[
            pltpu.VMEM((ZERO_BLOCK + 1, 16, 128), bf16),
            pltpu.VMEM((5, 16, 128), f32),
            pltpu.VMEM((NY * 16, MEMBERS * 128), f32),
        ],
        compiler_params=params,
        name="second",
    )(chunks, count, far, recv, ih, il, *kernels)
    current, residual = update(sums, current, True)
    return (current, residual)


def solution(mesh):
    grid = Mesh(mesh.devices.reshape(NY, NZ, NX, NC), ("y", "z", "x", "core"))
    split = P(None, ("y", "z", "x", "core"))
    in_specs = (P(), split, split, split, split, P(), P(("y", "z", "x", "core")), P())
    return jax.shard_map(body, mesh=grid, in_specs=in_specs, out_specs=(split, split), check_vma=False)
```

```python
import functools
import math

import jax
import jax.numpy as jnp
import numpy as np
from jax import lax
from jax.experimental import pallas as pl
from jax.experimental.pallas import tpu as pltpu
from jax.sharding import Mesh
from jax.sharding import PartitionSpec as P

HALF_SIDE = 0.08
SOFTENING = 0.0025
NY, NZ, NX, NC = 4, 16, 4, 2
MEMBERS = NX * NC
PLANE = NY * MEMBERS
NEAR = 26
DEPTH = 48
FAR = NZ
ZERO_BLOCK = FAR + 4 * NY
FAR_SLOTS = 16
CHUNK_OWNER = 80
CHUNK_SLOTS = 128
PAIRS = 17
TILE = 256
TILES = MEMBERS * 128 // TILE
bf16, f32 = jnp.bfloat16, jnp.float32


def cheby_nodes(number):
    return np.cos(np.pi * (2 * np.arange(number) + 1) / (2 * number))


def pick(index, values):
    out = jnp.full(index.shape, float(values[0]), f32)
    for k in range(1, len(values)):
        out = jnp.where(index == k, float(values[k]), out)
    return out


def iota(shape, dim):
    return lax.broadcasted_iota(jnp.int32, shape, dim)


def split3(v):
    h = v.astype(bf16).astype(f32)
    r = v - h
    m = r.astype(bf16).astype(f32)
    low = (r - m).astype(bf16).astype(f32)
    return h, m, low


def split2(v):
    h = v.astype(bf16)
    return h, (v - h.astype(f32)).astype(bf16)


def source_rows(pts):
    row = iota(pts.shape, 0)
    s = jnp.where(row < 3, pts - 0.5, 0.0)
    norm = jnp.sum(s * s, axis=0, keepdims=True) + SOFTENING
    return jnp.where(row < 3, -2.0 * s, jnp.where(row == 3, norm, jnp.where(row == 4, 1.0, 0.0)))


def target_rows(pts):
    row = iota(pts.shape, 0)
    t = jnp.where(row < 3, pts - 0.5, 0.0)
    norm = jnp.sum(t * t, axis=0, keepdims=True)
    return jnp.where(row < 3, t, jnp.where(row == 3, 1.0, jnp.where(row == 4, norm, 0.0)))


def column3(a, b, c, shape):
    row = iota(shape, 0)
    return jnp.where(row == 0, a, jnp.where(row == 1, b, jnp.where(row == 2, c, 0.0)))


def here():
    member = lax.axis_index("x") * NC + lax.axis_index("core")
    return lax.axis_index("y"), lax.axis_index("z"), member


def a_block(rows):
    h, m, low = split3(rows)
    return jnp.concatenate([h, h, m, m, h, low], 0).T.astype(bf16)


def interp_tables():
    p = iota((32, 128), 0)
    parts = (p >> 4, (p >> 2) & 3, p & 3)
    tables = []
    for index, number in zip(parts, (2, 4, 4)):
        nodes = cheby_nodes(number)
        others = [[nodes[i] for i in range(number) if i != k] for k in range(number)]
        roots = [pick(index, [others[k][j] for k in range(number)]) for j in range(number - 1)]
        scale = pick(index, [1.0 / np.prod([nodes[k] - o for o in others[k]]) for k in range(number)])
        tables.append((roots, scale))
    return tables


def make_lists(y, z, near_ref, far_ref, chunk_ref, count_ref):
    total = jnp.int32(0)
    for other in range(NY):
        bits = jnp.where(y == other, 1 << z, 0)
        for j in range(NEAR):
            cluster = near_ref[j, other * NZ + z]
            bits = bits | jnp.where((cluster >> 4) == y, 1 << (cluster & 15), 0)
        near_count = jnp.int32(0)
        for k in range(NZ):
            far_ref[other, k] = NZ
        for k in range(NZ):
            mine = (bits >> k) & 1
            chunk_ref[total + near_count] = k
            far_ref[other, k - near_count] = jnp.where(mine > 0, NZ, k)
            near_count = near_count + mine
        far_blocks = (NZ + 3 - near_count) >> 2
        start = total + near_count
        for k in range(4):
            chunk_ref[start + k] = FAR + other * 4 + k
        end = start + far_blocks
        chunk_ref[end] = ZERO_BLOCK
        for k in range(8):
            chunk_ref[CHUNK_OWNER + (total >> 1) + k] = other
        total = ((end + 1) >> 1) << 1
    count_ref[0] = total >> 1


def prologue_kernel(count_ref, charges_hbm, coords_hbm, zsend_ref, current_ref, coords_ref, sem):
    copies = [pltpu.make_async_copy(charges_hbm, current_ref, sem.at[0]), pltpu.make_async_copy(coords_hbm, coords_ref, sem.at[1])]
    for copy in copies:
        copy.start()
    for copy in copies:
        copy.wait()
    current = current_ref[...] * (iota((8, 128), 1) < count_ref[0]).astype(f32)
    current_ref[...] = current
    coords = jnp.concatenate([coords_ref[...], jnp.zeros((1, 128), f32)], 0)
    for k in range(NZ):
        zsend_ref[3 * k] = current[0:4]
        zsend_ref[3 * k + 1] = current[4:8]
        zsend_ref[3 * k + 2] = coords


def prep_kernel(
    count_ref, steps_ref, centers_hbm, near_hbm, boundary_hbm, targets_hbm,
    tsend_ref, held_ref, near_ref, center_ref, proxy_ref,
    centers_ref, targets_ref, sem,
):
    y, _, member = here()
    moves = ((targets_hbm, targets_ref), (centers_hbm, centers_ref), (boundary_hbm, held_ref.at[0]), (near_hbm, near_ref))
    copies = [pltpu.make_async_copy(source, target, sem.at[k]) for k, (source, target) in enumerate(moves)]
    for copy in copies:
        copy.start()
    lane = iota((8, 128), 1)
    row = iota((8, 128), 0)
    p = lane & 31
    offset = jnp.where(
        row == 0,
        pick(p >> 4, cheby_nodes(2)),
        jnp.where(row == 1, pick((p >> 2) & 3, cheby_nodes(4)), jnp.where(row == 2, pick(p & 3, cheby_nodes(4)), 0.0)),
    )
    steps = jnp.zeros((8, 128), f32)
    for k in range(8):
        steps = jnp.where(row == k, steps_ref[k], steps)
    held_ref[1] = steps
    held_ref[2] = (lane < count_ref[0]).astype(f32)
    for copy in copies:
        copy.wait()
    rows = target_rows(jnp.concatenate([targets_ref[...], jnp.zeros((5, 128), f32)], 0))
    for k in range(PLANE):
        tsend_ref[k] = rows
    for block in range(4):
        center = jnp.zeros((8, 128), f32)
        for k in range(4):
            leaf = (y * NZ + block * 4 + k) * MEMBERS + member
            column = column3(centers_ref[0, leaf], centers_ref[1, leaf], centers_ref[2, leaf], (8, 128))
            center_ref[block * 4 + k] = column
            center = jnp.where((lane >> 5) == k, column, center)
        rows = source_rows(center + HALF_SIDE * offset)
        proxy_ref[block * 128 : (block + 1) * 128, :DEPTH] = a_block(rows)
    proxy_ref[512:544, :DEPTH] = proxy_ref[0:32, :DEPTH]


def charge_blocks(charges, ih_ref, il_ref, far_ref, q_ref, wide_ref):
    far = []
    nt = (((1,), (1,)), ((), ()))
    for k in range(NZ):
        hi, lo = split2(charges(k))
        q = jnp.concatenate([hi.astype(f32), lo.astype(f32)], 0).astype(bf16)
        q_ref[k] = q
        both = lax.dot_general(q, ih_ref[k * 32 : (k + 1) * 32], nt, preferred_element_type=f32)
        both = both + lax.dot_general(q, il_ref[k * 32 : (k + 1) * 32], nt, preferred_element_type=f32)
        far.append(both[0:8] + both[8:16])
    for k in range(4):
        wide = jnp.concatenate(far[4 * k : 4 * k + 4], 1)
        hi = wide.astype(bf16).astype(f32)
        wide_ref[k] = jnp.concatenate([hi, wide - hi], 0)
    wide_ref[4] = jnp.zeros((16, 128), f32)
    q_ref[ZERO_BLOCK] = jnp.zeros((16, 128), bf16)
    group = iota((16, 128), 1) >> 5
    for other in range(NY):
        for block in range(4):
            out = None
            for k in range(4):
                leaf = far_ref[other, block * 4 + k]
                moved = pltpu.roll(wide_ref[leaf >> 2], ((4 + k - leaf) & 3) * 32, 1)
                out = moved if out is None else jnp.where(group == k, moved, out)
            q_ref[FAR + other * 4 + block] = out.astype(bf16)


def setup_kernel(
    near_ref, center_ref, recv_ref, proxy_ref, a_ref, ih_ref, il_ref, q_ref, far_ref, chunk_ref, count_ref, wide_ref
):
    y, z, _ = here()
    make_lists(y, z, near_ref, far_ref, chunk_ref, count_ref)
    tables = interp_tables()
    for k in range(NZ):
        rows = recv_ref[3 * k + 2]
        points = center_ref[k] + HALF_SIDE * jnp.concatenate([rows, jnp.zeros((4, 128), f32)], 0)
        a_ref[k * 128 : (k + 1) * 128, :DEPTH] = a_block(source_rows(points))
        value = None
        for axis, (roots, scale) in enumerate(tables):
            u = jnp.broadcast_to(rows[axis : axis + 1], (32, 128))
            line = scale
            for root in roots:
                line = line * (u - root)
            value = line if value is None else value * line
        hi, lo = split2(value)
        ih_ref[k * 32 : (k + 1) * 32] = hi
        il_ref[k * 32 : (k + 1) * 32] = lo
    for other in range(NY):
        for k in range(NZ):
            base = (FAR + other * 4) * 128 + k * 32
            a_ref[base : base + 32] = proxy_ref[pl.ds(pl.multiple_of(far_ref[other, k] * 32, 32), 32)]
    charge_blocks(lambda k: jnp.concatenate([recv_ref[3 * k], recv_ref[3 * k + 1]], 0), ih_ref, il_ref, far_ref, q_ref, wide_ref)


def multiply_tile(chunk_ref, q_ref, acc_ref, i, hi_ref, lo_ref, j, t):
    q = jnp.concatenate([q_ref[chunk_ref[2 * i + k]] for k in range(2)], 1)
    rows = pl.ds(pl.multiple_of(chunk_ref[CHUNK_OWNER + i] * 16, 16), 16)
    cols = slice(t * TILE, (t + 1) * TILE)
    both = jnp.concatenate([hi_ref[j, t], lo_ref[j, t]], 0)
    acc_ref[rows, cols] = acc_ref[rows, cols] + jnp.dot(jnp.concatenate([q, q], 1), both, preferred_element_type=f32)


def in_steps(number, work):
    def four(j, carry):
        for k in range(4):
            work(4 * j + k)
        return carry

    lax.fori_loop(0, number >> 2, four, 0)

    @pl.when((number & 2) == 2)
    def _():
        work((number >> 2) * 4)
        work((number >> 2) * 4 + 1)

    @pl.when((number & 1) == 1)
    def _():
        work(number - 1)


def write_sums(acc_ref, out_ref):
    for other in range(NY):
        total = acc_ref[other * 16 : other * 16 + 8] + acc_ref[other * 16 + 8 : other * 16 + 16]
        for k in range(MEMBERS):
            out_ref[other * MEMBERS + k] = total[:, k * 128 : (k + 1) * 128]


def first_kernel(chunk_ref, count_ref, tgt_ref, a_ref, q_ref, out_ref, eh_ref, el_ref, oh_ref, ol_ref, b_ref, acc_ref):
    for other in range(NY):
        h, m, low = split3(jnp.concatenate([tgt_ref[other * MEMBERS + k] for k in range(MEMBERS)], 1))
        b_ref[other] = jnp.concatenate([h, m, h, m, low, h], 0).astype(bf16)
    acc_ref[...] = jnp.zeros_like(acc_ref)
    count = count_ref[0]

    def rows_of(i):
        blocks = [chunk_ref[2 * i + k] for k in range(2)]
        starts = [pl.multiple_of(jnp.where(n == ZERO_BLOCK, 0, n) * 128, 128) for n in blocks]
        return jnp.concatenate([a_ref[pl.ds(n, 128), :DEPTH] for n in starts], 0), chunk_ref[CHUNK_OWNER + i]

    def evaluate_tile(rows, hi_ref, lo_ref, j, t):
        square = jnp.dot(rows[0], b_ref[rows[1], :, t * TILE : (t + 1) * TILE], preferred_element_type=f32)
        hi, lo = split2(lax.rsqrt(square))
        hi_ref[j, t] = hi
        lo_ref[j, t] = lo

    even, odd = (eh_ref, el_ref), (oh_ref, ol_ref)
    mul = functools.partial(multiply_tile, chunk_ref, q_ref, acc_ref)

    def both(done, source, js, new, target, jt):
        rows = rows_of(new)
        for t in range(TILES):
            mul(done, *source, js, t)
            evaluate_tile(rows, *target, jt, t)

    rows = rows_of(0)
    for t in range(TILES):
        evaluate_tile(rows, *even, 0, t)

    def pair(j):
        both(2 * j, even, j, 2 * j + 1, odd, j)
        both(2 * j + 1, odd, j, 2 * j + 2, even, j + 1)

    pairs = (count - 1) >> 1
    in_steps(pairs, pair)

    @pl.when((count & 1) == 0)
    def _():
        both(2 * pairs, even, pairs, 2 * pairs + 1, odd, pairs)
        for t in range(TILES):
            mul(2 * pairs + 1, *odd, pairs, t)

    @pl.when((count & 1) == 1)
    def _():
        for t in range(TILES):
            mul(2 * pairs, *even, pairs, t)

    write_sums(acc_ref, out_ref)


def second_kernel(chunk_ref, count_ref, far_ref, recv_ref, ih_ref, il_ref, eh_ref, el_ref, oh_ref, ol_ref, out_ref, q_ref, wide_ref, acc_ref):
    charge_blocks(lambda k: recv_ref[k], ih_ref, il_ref, far_ref, q_ref, wide_ref)
    acc_ref[...] = jnp.zeros_like(acc_ref)
    count = count_ref[0]
    mul = functools.partial(multiply_tile, chunk_ref, q_ref, acc_ref)

    def pair(j):
        for t in range(TILES):
            mul(2 * j, eh_ref, el_ref, j, t)
            mul(2 * j + 1, oh_ref, ol_ref, j, t)

    in_steps(count >> 1, pair)

    @pl.when((count & 1) == 1)
    def _():
        for t in range(TILES):
            mul(count - 1, eh_ref, el_ref, count >> 1, t)

    write_sums(acc_ref, out_ref)


def update_kernel(scale, last, recv_ref, held_ref, current_ref, new_ref, other_ref):
    parts = [recv_ref[k] for k in range(PLANE)]
    while len(parts) > 1:
        parts = [parts[i] + parts[i + 1] for i in range(0, len(parts), 2)]
    live = held_ref[2]
    residual = live * (held_ref[0] - scale * parts[0])
    new = live * (current_ref[...] + held_ref[1] * residual / (1.0 + jnp.abs(residual)))
    new_ref[...] = new
    if last:
        other_ref[...] = residual
    else:
        for k in range(NZ):
            other_ref[k] = new


VM = pl.BlockSpec(memory_space=pltpu.VMEM)
SM = pl.BlockSpec(memory_space=pltpu.SMEM)
HB = pl.BlockSpec(memory_space=pltpu.HBM)


def sds(shape, dtype=f32):
    return jax.ShapeDtypeStruct(shape, dtype)


def body(leaf_centers, source_coords, target_points, charges, boundary_data, step_sizes, valid_count, near_lists):
    plane = ("y", "x", "core")
    params = pltpu.CompilerParams(vmem_limit_bytes=12 * 2**20)
    small = pltpu.CompilerParams(vmem_limit_bytes=4 * 2**20)
    hbm = functools.partial(pltpu.with_memory_space_constraint, memory_space=pltpu.HBM)
    charges, source_coords, boundary_data, target_points = map(hbm, (charges, source_coords, boundary_data, target_points))
    zsend, current = pl.pallas_call(
        prologue_kernel,
        out_shape=(sds((3 * NZ, 4, 128)), sds((8, 128))),
        in_specs=[SM, HB, HB],
        out_specs=(VM, VM),
        scratch_shapes=[pltpu.VMEM((3, 128), f32), pltpu.SemaphoreType.DMA((2,))],
        compiler_params=small,
        name="prologue",
    )(valid_count, charges, source_coords)
    recv = lax.all_to_all(zsend, "z", 0, 0, tiled=True)
    tsend, held, near, centers, proxies = pl.pallas_call(
        prep_kernel,
        out_shape=(
            sds((PLANE, 8, 128)),
            sds((3, 8, 128)),
            sds((NEAR, NY * NZ), jnp.int32),
            sds((NZ, 8, 128)),
            sds((544, 128), bf16),
        ),
        in_specs=[SM, SM, HB, HB, HB, HB],
        out_specs=(VM,) * 5,
        scratch_shapes=[pltpu.SMEM((3, NZ * NY * MEMBERS), f32), pltpu.VMEM((3, 128), f32), pltpu.SemaphoreType.DMA((4,))],
        compiler_params=small,
        cost_estimate=pl.CostEstimate(flops=10**9, bytes_accessed=12 * 10**6, transcendentals=0),
        name="prep",
    )(valid_count, step_sizes, hbm(leaf_centers), hbm(near_lists.T), boundary_data, target_points)
    recv, tsend = lax.optimization_barrier((recv, tsend))
    targets = lax.all_to_all(tsend, plane, 0, 0, tiled=True)
    interp = sds((NZ * 32, 128), bf16)
    a, ih, il, q, far, chunks, count = pl.pallas_call(
        setup_kernel,
        out_shape=(
            sds((ZERO_BLOCK * 128, 128), bf16),
            interp,
            interp,
            sds((ZERO_BLOCK + 1, 16, 128), bf16),
            sds((NY, FAR_SLOTS), jnp.int32),
            sds((CHUNK_SLOTS,), jnp.int32),
            sds((1,), jnp.int32),
        ),
        in_specs=[SM, VM, VM, VM],
        out_specs=(VM,) * 4 + (SM,) * 3,
        scratch_shapes=[pltpu.VMEM((5, 16, 128), f32)],
        compiler_params=params,
        cost_estimate=pl.CostEstimate(flops=10**9, bytes_accessed=8 * 10**6, transcendentals=0),
        name="setup",
    )(near, centers, recv, proxies)
    scale = 1.0 / math.sqrt(NY * NZ * MEMBERS * 128)
    half = pltpu.VMEM((PAIRS, TILES, 256, TILE), bf16)
    sums, *kernels = pl.pallas_call(
        first_kernel,
        out_shape=(sds((PLANE, 8, 128)), half, half, half, half),
        in_specs=[SM, SM, VM, VM, VM],
        out_specs=(VM,) * 5,
        scratch_shapes=[pltpu.VMEM((NY, DEPTH, MEMBERS * 128), bf16), pltpu.VMEM((NY * 16, MEMBERS * 128), f32)],
        compiler_params=params,
        name="first",
    )(chunks, count, targets, a, q)

    def update(sums, current, last):
        return pl.pallas_call(
            functools.partial(update_kernel, scale, last),
            out_shape=(sds((8, 128)), sds((8, 128) if last else (NZ, 8, 128))),
            in_specs=[VM, VM, VM],
            out_specs=(VM, VM),
            compiler_params=small,
            name="update",
        )(lax.all_to_all(sums, plane, 0, 0, tiled=True), held, current)

    current, zsend = update(sums, current, False)
    recv = lax.all_to_all(zsend, "z", 0, 0, tiled=True)
    sums = pl.pallas_call(
        second_kernel,
        out_shape=sds((PLANE, 8, 128)),
        in_specs=[SM, SM, SM] + [VM] * 7,
        out_specs=VM,
        scratch_shapes=[
            pltpu.VMEM((ZERO_BLOCK + 1, 16, 128), bf16),
            pltpu.VMEM((5, 16, 128), f32),
            pltpu.VMEM((NY * 16, MEMBERS * 128), f32),
        ],
        compiler_params=params,
        name="second",
    )(chunks, count, far, recv, ih, il, *kernels)
    current, residual = update(sums, current, True)
    return (current, residual)


def solution(mesh):
    grid = Mesh(mesh.devices.reshape(NY, NZ, NX, NC), ("y", "z", "x", "core"))
    split = P(None, ("y", "z", "x", "core"))
    in_specs = (P(), split, split, split, split, P(), P(("y", "z", "x", "core")), P())
    return jax.shard_map(body, mesh=grid, in_specs=in_specs, out_specs=(split, split), check_vma=False)
```

```python
import functools
import math

import jax
import jax.numpy as jnp
import numpy as np
from jax import lax
from jax.experimental import pallas as pl
from jax.experimental.pallas import tpu as pltpu
from jax.sharding import Mesh
from jax.sharding import PartitionSpec as P

HALF_SIDE = 0.08
SOFTENING = 0.0025
NY, NZ, NX, NC = 4, 16, 4, 2
MEMBERS = NX * NC
PLANE = NY * MEMBERS
NEAR = 26
DEPTH = 48
FAR = NZ
ZERO_BLOCK = FAR + 4 * NY
FAR_SLOTS = 16
CHUNK_OWNER = 80
CHUNK_SLOTS = 128
PAIRS = 17
TILE = 256
TILES = MEMBERS * 128 // TILE
bf16, f32 = jnp.bfloat16, jnp.float32


def cheby_nodes(number):
    return np.cos(np.pi * (2 * np.arange(number) + 1) / (2 * number))


def pick(index, values):
    out = jnp.full(index.shape, float(values[0]), f32)
    for k in range(1, len(values)):
        out = jnp.where(index == k, float(values[k]), out)
    return out


def iota(shape, dim):
    return lax.broadcasted_iota(jnp.int32, shape, dim)


def split3(v):
    h = v.astype(bf16).astype(f32)
    r = v - h
    m = r.astype(bf16).astype(f32)
    low = (r - m).astype(bf16).astype(f32)
    return h, m, low


def split2(v):
    h = v.astype(bf16)
    return h, (v - h.astype(f32)).astype(bf16)


def source_rows(pts):
    row = iota(pts.shape, 0)
    s = jnp.where(row < 3, pts - 0.5, 0.0)
    norm = jnp.sum(s * s, axis=0, keepdims=True) + SOFTENING
    return jnp.where(row < 3, -2.0 * s, jnp.where(row == 3, norm, jnp.where(row == 4, 1.0, 0.0)))


def target_rows(pts):
    row = iota(pts.shape, 0)
    t = jnp.where(row < 3, pts - 0.5, 0.0)
    norm = jnp.sum(t * t, axis=0, keepdims=True)
    return jnp.where(row < 3, t, jnp.where(row == 3, 1.0, jnp.where(row == 4, norm, 0.0)))


def column3(a, b, c, shape):
    row = iota(shape, 0)
    return jnp.where(row == 0, a, jnp.where(row == 1, b, jnp.where(row == 2, c, 0.0)))


def here():
    member = lax.axis_index("x") * NC + lax.axis_index("core")
    return lax.axis_index("y"), lax.axis_index("z"), member


def a_block(rows):
    h, m, low = split3(rows)
    return jnp.concatenate([h, h, m, m, h, low], 0).T.astype(bf16)


def interp_tables():
    p = iota((32, 128), 0)
    parts = (p >> 4, (p >> 2) & 3, p & 3)
    tables = []
    for index, number in zip(parts, (2, 4, 4)):
        nodes = cheby_nodes(number)
        others = [[nodes[i] for i in range(number) if i != k] for k in range(number)]
        roots = [pick(index, [others[k][j] for k in range(number)]) for j in range(number - 1)]
        scale = pick(index, [1.0 / np.prod([nodes[k] - o for o in others[k]]) for k in range(number)])
        tables.append((roots, scale))
    return tables


def make_lists(y, z, near_ref, far_ref, chunk_ref, count_ref):
    total = jnp.int32(0)
    for other in range(NY):
        bits = jnp.where(y == other, 1 << z, 0)
        for j in range(NEAR):
            cluster = near_ref[j, other * NZ + z]
            bits = bits | jnp.where((cluster >> 4) == y, 1 << (cluster & 15), 0)
        near_count = jnp.int32(0)
        for k in range(NZ):
            far_ref[other, k] = NZ
        for k in range(NZ):
            mine = (bits >> k) & 1
            chunk_ref[total + near_count] = k
            far_ref[other, k - near_count] = jnp.where(mine > 0, NZ, k)
            near_count = near_count + mine
        far_blocks = (NZ + 3 - near_count) >> 2
        start = total + near_count
        for k in range(4):
            chunk_ref[start + k] = FAR + other * 4 + k
        end = start + far_blocks
        chunk_ref[end] = ZERO_BLOCK
        for k in range(8):
            chunk_ref[CHUNK_OWNER + (total >> 1) + k] = other
        total = ((end + 1) >> 1) << 1
    count_ref[0] = total >> 1


def prologue_kernel(count_ref, charges_hbm, coords_hbm, targets_hbm, zsend_ref, tsend_ref, current_ref, coords_ref, targets_ref, sem):
    moves = ((charges_hbm, current_ref), (coords_hbm, coords_ref), (targets_hbm, targets_ref))
    copies = [pltpu.make_async_copy(source, target, sem.at[k]) for k, (source, target) in enumerate(moves)]
    for copy in copies:
        copy.start()
    for copy in copies:
        copy.wait()
    current = current_ref[...] * (iota((8, 128), 1) < count_ref[0]).astype(f32)
    current_ref[...] = current
    coords = jnp.concatenate([coords_ref[...], jnp.zeros((1, 128), f32)], 0)
    for k in range(NZ):
        zsend_ref[3 * k] = current[0:4]
        zsend_ref[3 * k + 1] = current[4:8]
        zsend_ref[3 * k + 2] = coords
    rows = target_rows(jnp.concatenate([targets_ref[...], jnp.zeros((5, 128), f32)], 0))
    for k in range(PLANE):
        tsend_ref[k] = rows


def charge_blocks(charges, ih_ref, il_ref, far_ref, q_ref, wide_ref):
    far = []
    nt = (((1,), (1,)), ((), ()))
    for k in range(NZ):
        hi, lo = split2(charges(k))
        q = jnp.concatenate([hi.astype(f32), lo.astype(f32)], 0).astype(bf16)
        q_ref[k] = q
        both = lax.dot_general(q, ih_ref[k * 32 : (k + 1) * 32], nt, preferred_element_type=f32)
        both = both + lax.dot_general(q, il_ref[k * 32 : (k + 1) * 32], nt, preferred_element_type=f32)
        far.append(both[0:8] + both[8:16])
    for k in range(4):
        wide = jnp.concatenate(far[4 * k : 4 * k + 4], 1)
        hi = wide.astype(bf16).astype(f32)
        wide_ref[k] = jnp.concatenate([hi, wide - hi], 0)
    wide_ref[4] = jnp.zeros((16, 128), f32)
    q_ref[ZERO_BLOCK] = jnp.zeros((16, 128), bf16)
    group = iota((16, 128), 1) >> 5
    for other in range(NY):
        for block in range(4):
            out = None
            for k in range(4):
                leaf = far_ref[other, block * 4 + k]
                moved = pltpu.roll(wide_ref[leaf >> 2], ((4 + k - leaf) & 3) * 32, 1)
                out = moved if out is None else jnp.where(group == k, moved, out)
            q_ref[FAR + other * 4 + block] = out.astype(bf16)


def setup_kernel(
    count_ref, steps_ref, centers_hbm, near_hbm, boundary_hbm, recv_ref,
    a_ref, ih_ref, il_ref, q_ref, held_ref, far_ref, chunk_ref, chunks_ref,
    wide_ref, proxy_ref, centers_ref, near_ref, sem,
):
    y, z, member = here()
    moves = ((near_hbm, near_ref), (centers_hbm, centers_ref), (boundary_hbm, held_ref.at[0]))
    copies = [pltpu.make_async_copy(source, target, sem.at[k]) for k, (source, target) in enumerate(moves)]
    for copy in copies:
        copy.start()
    tables = interp_tables()
    for k in range(NZ):
        rows = recv_ref[3 * k + 2]
        value = None
        for axis, (roots, scale) in enumerate(tables):
            u = jnp.broadcast_to(rows[axis : axis + 1], (32, 128))
            line = scale
            for root in roots:
                line = line * (u - root)
            value = line if value is None else value * line
        hi, lo = split2(value)
        ih_ref[k * 32 : (k + 1) * 32] = hi
        il_ref[k * 32 : (k + 1) * 32] = lo
    lane = iota((8, 128), 1)
    row = iota((8, 128), 0)
    p = lane & 31
    offset = jnp.where(
        row == 0,
        pick(p >> 4, cheby_nodes(2)),
        jnp.where(row == 1, pick((p >> 2) & 3, cheby_nodes(4)), jnp.where(row == 2, pick(p & 3, cheby_nodes(4)), 0.0)),
    )
    steps = jnp.zeros((8, 128), f32)
    for k in range(8):
        steps = jnp.where(row == k, steps_ref[k], steps)
    held_ref[1] = steps
    held_ref[2] = (lane < count_ref[0]).astype(f32)
    for copy in copies:
        copy.wait()
    make_lists(y, z, near_ref, far_ref, chunk_ref, chunks_ref)
    for block in range(4):
        center = jnp.zeros((8, 128), f32)
        for k in range(4):
            place = block * 4 + k
            leaf = (y * NZ + place) * MEMBERS + member
            column = column3(centers_ref[0, leaf], centers_ref[1, leaf], centers_ref[2, leaf], (8, 128))
            points = column + HALF_SIDE * jnp.concatenate([recv_ref[3 * place + 2], jnp.zeros((4, 128), f32)], 0)
            a_ref[place * 128 : (place + 1) * 128, :DEPTH] = a_block(source_rows(points))
            center = jnp.where((lane >> 5) == k, column, center)
        proxy_ref[block * 128 : (block + 1) * 128, :DEPTH] = a_block(source_rows(center + HALF_SIDE * offset))
    proxy_ref[512:544, :DEPTH] = proxy_ref[0:32, :DEPTH]
    for other in range(NY):
        for k in range(NZ):
            base = (FAR + other * 4) * 128 + k * 32
            a_ref[base : base + 32] = proxy_ref[pl.ds(pl.multiple_of(far_ref[other, k] * 32, 32), 32)]
    charge_blocks(lambda k: jnp.concatenate([recv_ref[3 * k], recv_ref[3 * k + 1]], 0), ih_ref, il_ref, far_ref, q_ref, wide_ref)


def multiply_tile(chunk_ref, q_ref, acc_ref, i, hi_ref, lo_ref, j, t):
    q = jnp.concatenate([q_ref[chunk_ref[2 * i + k]] for k in range(2)], 1)
    rows = pl.ds(pl.multiple_of(chunk_ref[CHUNK_OWNER + i] * 16, 16), 16)
    cols = slice(t * TILE, (t + 1) * TILE)
    both = jnp.concatenate([hi_ref[j, t], lo_ref[j, t]], 0)
    acc_ref[rows, cols] = acc_ref[rows, cols] + jnp.dot(jnp.concatenate([q, q], 1), both, preferred_element_type=f32)


def in_steps(number, work):
    def four(j, carry):
        for k in range(4):
            work(4 * j + k)
        return carry

    lax.fori_loop(0, number >> 2, four, 0)

    @pl.when((number & 2) == 2)
    def _():
        work((number >> 2) * 4)
        work((number >> 2) * 4 + 1)

    @pl.when((number & 1) == 1)
    def _():
        work(number - 1)


def write_sums(acc_ref, out_ref):
    for other in range(NY):
        total = acc_ref[other * 16 : other * 16 + 8] + acc_ref[other * 16 + 8 : other * 16 + 16]
        for k in range(MEMBERS):
            out_ref[other * MEMBERS + k] = total[:, k * 128 : (k + 1) * 128]


def first_kernel(chunk_ref, count_ref, tgt_ref, a_ref, q_ref, out_ref, eh_ref, el_ref, oh_ref, ol_ref, b_ref, acc_ref):
    for other in range(NY):
        h, m, low = split3(jnp.concatenate([tgt_ref[other * MEMBERS + k] for k in range(MEMBERS)], 1))
        b_ref[other] = jnp.concatenate([h, m, h, m, low, h], 0).astype(bf16)
    acc_ref[...] = jnp.zeros_like(acc_ref)
    count = count_ref[0]

    def rows_of(i):
        blocks = [chunk_ref[2 * i + k] for k in range(2)]
        starts = [pl.multiple_of(jnp.where(n == ZERO_BLOCK, 0, n) * 128, 128) for n in blocks]
        return jnp.concatenate([a_ref[pl.ds(n, 128), :DEPTH] for n in starts], 0), chunk_ref[CHUNK_OWNER + i]

    def evaluate_tile(rows, hi_ref, lo_ref, j, t):
        square = jnp.dot(rows[0], b_ref[rows[1], :, t * TILE : (t + 1) * TILE], preferred_element_type=f32)
        hi, lo = split2(lax.rsqrt(square))
        hi_ref[j, t] = hi
        lo_ref[j, t] = lo

    even, odd = (eh_ref, el_ref), (oh_ref, ol_ref)
    mul = functools.partial(multiply_tile, chunk_ref, q_ref, acc_ref)

    def both(done, source, js, new, target, jt):
        rows = rows_of(new)
        for t in range(TILES):
            mul(done, *source, js, t)
            evaluate_tile(rows, *target, jt, t)

    rows = rows_of(0)
    for t in range(TILES):
        evaluate_tile(rows, *even, 0, t)

    def pair(j):
        both(2 * j, even, j, 2 * j + 1, odd, j)
        both(2 * j + 1, odd, j, 2 * j + 2, even, j + 1)

    pairs = (count - 1) >> 1
    in_steps(pairs, pair)

    @pl.when((count & 1) == 0)
    def _():
        both(2 * pairs, even, pairs, 2 * pairs + 1, odd, pairs)
        for t in range(TILES):
            mul(2 * pairs + 1, *odd, pairs, t)

    @pl.when((count & 1) == 1)
    def _():
        for t in range(TILES):
            mul(2 * pairs, *even, pairs, t)

    write_sums(acc_ref, out_ref)


def second_kernel(chunk_ref, count_ref, far_ref, recv_ref, ih_ref, il_ref, eh_ref, el_ref, oh_ref, ol_ref, out_ref, q_ref, wide_ref, acc_ref):
    charge_blocks(lambda k: recv_ref[k], ih_ref, il_ref, far_ref, q_ref, wide_ref)
    acc_ref[...] = jnp.zeros_like(acc_ref)
    count = count_ref[0]
    mul = functools.partial(multiply_tile, chunk_ref, q_ref, acc_ref)

    def pair(j):
        for t in range(TILES):
            mul(2 * j, eh_ref, el_ref, j, t)
            mul(2 * j + 1, oh_ref, ol_ref, j, t)

    in_steps(count >> 1, pair)

    @pl.when((count & 1) == 1)
    def _():
        for t in range(TILES):
            mul(count - 1, eh_ref, el_ref, count >> 1, t)

    write_sums(acc_ref, out_ref)


def update_kernel(scale, last, recv_ref, held_ref, current_ref, new_ref, other_ref):
    parts = [recv_ref[k] for k in range(PLANE)]
    while len(parts) > 1:
        parts = [parts[i] + parts[i + 1] for i in range(0, len(parts), 2)]
    live = held_ref[2]
    residual = live * (held_ref[0] - scale * parts[0])
    new = live * (current_ref[...] + held_ref[1] * residual / (1.0 + jnp.abs(residual)))
    new_ref[...] = new
    if last:
        other_ref[...] = residual
    else:
        for k in range(NZ):
            other_ref[k] = new


VM = pl.BlockSpec(memory_space=pltpu.VMEM)
SM = pl.BlockSpec(memory_space=pltpu.SMEM)
HB = pl.BlockSpec(memory_space=pltpu.HBM)


def sds(shape, dtype=f32):
    return jax.ShapeDtypeStruct(shape, dtype)


def body(leaf_centers, source_coords, target_points, charges, boundary_data, step_sizes, valid_count, near_lists):
    plane = ("y", "x", "core")
    params = pltpu.CompilerParams(vmem_limit_bytes=12 * 2**20)
    small = pltpu.CompilerParams(vmem_limit_bytes=4 * 2**20)
    hbm = functools.partial(pltpu.with_memory_space_constraint, memory_space=pltpu.HBM)
    zsend, tsend, current = pl.pallas_call(
        prologue_kernel,
        out_shape=(sds((3 * NZ, 4, 128)), sds((PLANE, 8, 128)), sds((8, 128))),
        in_specs=[SM, HB, HB, HB],
        out_specs=(VM,) * 3,
        scratch_shapes=[pltpu.VMEM((3, 128), f32), pltpu.VMEM((3, 128), f32), pltpu.SemaphoreType.DMA((3,))],
        compiler_params=small,
        name="prologue",
    )(valid_count, hbm(charges), hbm(source_coords), hbm(target_points))
    recv = lax.all_to_all(zsend, "z", 0, 0, tiled=True)
    recv, tsend, step_sizes = lax.optimization_barrier((recv, tsend, step_sizes))
    targets = lax.all_to_all(tsend, plane, 0, 0, tiled=True)
    interp = sds((NZ * 32, 128), bf16)
    a, ih, il, q, held, far, chunks, count = pl.pallas_call(
        setup_kernel,
        out_shape=(
            sds((ZERO_BLOCK * 128, 128), bf16),
            interp,
            interp,
            sds((ZERO_BLOCK + 1, 16, 128), bf16),
            sds((3, 8, 128)),
            sds((NY, FAR_SLOTS), jnp.int32),
            sds((CHUNK_SLOTS,), jnp.int32),
            sds((1,), jnp.int32),
        ),
        in_specs=[SM, SM, HB, HB, HB, VM],
        out_specs=(VM,) * 5 + (SM,) * 3,
        scratch_shapes=[
            pltpu.VMEM((5, 16, 128), f32),
            pltpu.VMEM((544, 128), bf16),
            pltpu.SMEM((3, NZ * NY * MEMBERS), f32),
            pltpu.SMEM((NEAR, NY * NZ), jnp.int32),
            pltpu.SemaphoreType.DMA((3,)),
        ],
        compiler_params=params,
        cost_estimate=pl.CostEstimate(flops=10**9, bytes_accessed=12 * 10**6, transcendentals=0),
        name="setup",
    )(valid_count, step_sizes, hbm(leaf_centers), hbm(near_lists.T), hbm(boundary_data), recv)
    scale = 1.0 / math.sqrt(NY * NZ * MEMBERS * 128)
    half = pltpu.VMEM((PAIRS, TILES, 256, TILE), bf16)
    sums, *kernels = pl.pallas_call(
        first_kernel,
        out_shape=(sds((PLANE, 8, 128)), half, half, half, half),
        in_specs=[SM, SM, VM, VM, VM],
        out_specs=(VM,) * 5,
        scratch_shapes=[pltpu.VMEM((NY, DEPTH, MEMBERS * 128), bf16), pltpu.VMEM((NY * 16, MEMBERS * 128), f32)],
        compiler_params=params,
        name="first",
    )(chunks, count, targets, a, q)

    def update(sums, current, last):
        return pl.pallas_call(
            functools.partial(update_kernel, scale, last),
            out_shape=(sds((8, 128)), sds((8, 128) if last else (NZ, 8, 128))),
            in_specs=[VM, VM, VM],
            out_specs=(VM, VM),
            compiler_params=small,
            name="update",
        )(lax.all_to_all(sums, plane, 0, 0, tiled=True), held, current)

    current, zsend = update(sums, current, False)
    recv = lax.all_to_all(zsend, "z", 0, 0, tiled=True)
    sums = pl.pallas_call(
        second_kernel,
        out_shape=sds((PLANE, 8, 128)),
        in_specs=[SM, SM, SM] + [VM] * 7,
        out_specs=VM,
        scratch_shapes=[
            pltpu.VMEM((ZERO_BLOCK + 1, 16, 128), bf16),
            pltpu.VMEM((5, 16, 128), f32),
            pltpu.VMEM((NY * 16, MEMBERS * 128), f32),
        ],
        compiler_params=params,
        name="second",
    )(chunks, count, far, recv, ih, il, *kernels)
    current, residual = update(sums, current, True)
    return (current, residual)


def solution(mesh):
    grid = Mesh(mesh.devices.reshape(NY, NZ, NX, NC), ("y", "z", "x", "core"))
    split = P(None, ("y", "z", "x", "core"))
    in_specs = (P(), split, split, split, split, P(), P(("y", "z", "x", "core")), P())
    return jax.shard_map(body, mesh=grid, in_specs=in_specs, out_specs=(split, split), check_vma=False)
```

```python
import functools
import math

import jax
import jax.numpy as jnp
import numpy as np
from jax import lax
from jax.experimental import pallas as pl
from jax.experimental.pallas import tpu as pltpu
from jax.sharding import Mesh
from jax.sharding import PartitionSpec as P

HALF_SIDE = 0.08
SOFTENING = 0.0025
NY, NZ, NX, NC = 4, 16, 4, 2
MEMBERS = NX * NC
PLANE = NY * MEMBERS
NEAR = 26
DEPTH = 48
FAR = NZ
ZERO_BLOCK = FAR + 4 * NY
FAR_SLOTS = 16
CHUNK_OWNER = 80
CHUNK_SLOTS = 128
PAIRS = 17
TILE = 256
TILES = MEMBERS * 128 // TILE
bf16, f32 = jnp.bfloat16, jnp.float32


def cheby_nodes(number):
    return np.cos(np.pi * (2 * np.arange(number) + 1) / (2 * number))


def pick(index, values):
    out = jnp.full(index.shape, float(values[0]), f32)
    for k in range(1, len(values)):
        out = jnp.where(index == k, float(values[k]), out)
    return out


def iota(shape, dim):
    return lax.broadcasted_iota(jnp.int32, shape, dim)


def split3(v):
    h = v.astype(bf16).astype(f32)
    r = v - h
    m = r.astype(bf16).astype(f32)
    low = (r - m).astype(bf16).astype(f32)
    return h, m, low


def split2(v):
    h = v.astype(bf16)
    return h, (v - h.astype(f32)).astype(bf16)


def source_rows(pts):
    row = iota(pts.shape, 0)
    s = jnp.where(row < 3, pts - 0.5, 0.0)
    norm = jnp.sum(s * s, axis=0, keepdims=True) + SOFTENING
    return jnp.where(row < 3, -2.0 * s, jnp.where(row == 3, norm, jnp.where(row == 4, 1.0, 0.0)))


def target_rows(pts):
    t = pts - 0.5
    return jnp.concatenate([t, jnp.sum(t * t, axis=0, keepdims=True)], 0)


def column3(a, b, c, shape):
    row = iota(shape, 0)
    return jnp.where(row == 0, a, jnp.where(row == 1, b, jnp.where(row == 2, c, 0.0)))


def here():
    member = lax.axis_index("x") * NC + lax.axis_index("core")
    return lax.axis_index("y"), lax.axis_index("z"), member


def a_block(rows):
    h, m, low = split3(rows)
    return jnp.concatenate([h, h, m, m, h, low], 0).T.astype(bf16)


def interp_tables():
    p = iota((32, 128), 0)
    parts = (p >> 4, (p >> 2) & 3, p & 3)
    tables = []
    for index, number in zip(parts, (2, 4, 4)):
        nodes = cheby_nodes(number)
        others = [[nodes[i] for i in range(number) if i != k] for k in range(number)]
        roots = [pick(index, [others[k][j] for k in range(number)]) for j in range(number - 1)]
        scale = pick(index, [1.0 / np.prod([nodes[k] - o for o in others[k]]) for k in range(number)])
        tables.append((roots, scale))
    return tables


def make_lists(y, z, near_ref, far_ref, chunk_ref, count_ref):
    total = jnp.int32(0)
    for other in range(NY):
        bits = jnp.where(y == other, 1 << z, 0)
        for j in range(NEAR):
            cluster = near_ref[j, other * NZ + z]
            bits = bits | jnp.where((cluster >> 4) == y, 1 << (cluster & 15), 0)
        near_count = jnp.int32(0)
        for k in range(NZ):
            far_ref[other, k] = NZ
        for k in range(NZ):
            mine = (bits >> k) & 1
            chunk_ref[total + near_count] = k
            far_ref[other, k - near_count] = jnp.where(mine > 0, NZ, k)
            near_count = near_count + mine
        far_blocks = (NZ + 3 - near_count) >> 2
        start = total + near_count
        for k in range(4):
            chunk_ref[start + k] = FAR + other * 4 + k
        end = start + far_blocks
        chunk_ref[end] = ZERO_BLOCK
        for k in range(8):
            chunk_ref[CHUNK_OWNER + (total >> 1) + k] = other
        total = ((end + 1) >> 1) << 1
    count_ref[0] = total >> 1


def prologue_kernel(count_ref, charges_hbm, coords_hbm, targets_hbm, zsend_ref, tsend_ref, current_ref, coords_ref, targets_ref, sem):
    moves = ((charges_hbm, current_ref), (coords_hbm, coords_ref), (targets_hbm, targets_ref))
    copies = [pltpu.make_async_copy(source, target, sem.at[k]) for k, (source, target) in enumerate(moves)]
    for copy in copies:
        copy.start()
    for copy in copies:
        copy.wait()
    current = current_ref[...] * (iota((8, 128), 1) < count_ref[0]).astype(f32)
    current_ref[...] = current
    coords = jnp.concatenate([coords_ref[...], jnp.zeros((1, 128), f32)], 0)
    for k in range(NZ):
        zsend_ref[3 * k] = current[0:4]
        zsend_ref[3 * k + 1] = current[4:8]
        zsend_ref[3 * k + 2] = coords
    rows = target_rows(targets_ref[...])
    for k in range(PLANE):
        tsend_ref[k] = rows


def charge_blocks(charges, ih_ref, il_ref, far_ref, q_ref, wide_ref):
    far = []
    nt = (((1,), (1,)), ((), ()))
    for k in range(NZ):
        hi, lo = split2(charges(k))
        q = jnp.concatenate([hi.astype(f32), lo.astype(f32)], 0).astype(bf16)
        q_ref[k] = q
        both = lax.dot_general(q, ih_ref[k * 32 : (k + 1) * 32], nt, preferred_element_type=f32)
        both = both + lax.dot_general(q, il_ref[k * 32 : (k + 1) * 32], nt, preferred_element_type=f32)
        far.append(both[0:8] + both[8:16])
    for k in range(4):
        wide = jnp.concatenate(far[4 * k : 4 * k + 4], 1)
        hi = wide.astype(bf16).astype(f32)
        wide_ref[k] = jnp.concatenate([hi, wide - hi], 0)
    wide_ref[4] = jnp.zeros((16, 128), f32)
    q_ref[ZERO_BLOCK] = jnp.zeros((16, 128), bf16)
    group = iota((16, 128), 1) >> 5
    for other in range(NY):
        for block in range(4):
            out = None
            for k in range(4):
                leaf = far_ref[other, block * 4 + k]
                moved = pltpu.roll(wide_ref[leaf >> 2], ((4 + k - leaf) & 3) * 32, 1)
                out = moved if out is None else jnp.where(group == k, moved, out)
            q_ref[FAR + other * 4 + block] = out.astype(bf16)


def setup_kernel(
    count_ref, steps_hbm, centers_hbm, near_hbm, boundary_hbm, recv_ref,
    a_ref, ih_ref, il_ref, q_ref, held_ref, far_ref, chunk_ref, chunks_ref,
    wide_ref, proxy_ref, centers_ref, near_ref, steps_ref, sem,
):
    y, z, member = here()
    moves = ((near_hbm, near_ref), (centers_hbm, centers_ref), (boundary_hbm, held_ref.at[0]), (steps_hbm, steps_ref))
    copies = [pltpu.make_async_copy(source, target, sem.at[k]) for k, (source, target) in enumerate(moves)]
    for copy in copies:
        copy.start()
    tables = interp_tables()
    for k in range(NZ):
        rows = recv_ref[3 * k + 2]
        value = None
        for axis, (roots, scale) in enumerate(tables):
            u = jnp.broadcast_to(rows[axis : axis + 1], (32, 128))
            line = scale
            for root in roots:
                line = line * (u - root)
            value = line if value is None else value * line
        hi, lo = split2(value)
        ih_ref[k * 32 : (k + 1) * 32] = hi
        il_ref[k * 32 : (k + 1) * 32] = lo
    lane = iota((8, 128), 1)
    row = iota((8, 128), 0)
    p = lane & 31
    offset = jnp.where(
        row == 0,
        pick(p >> 4, cheby_nodes(2)),
        jnp.where(row == 1, pick((p >> 2) & 3, cheby_nodes(4)), jnp.where(row == 2, pick(p & 3, cheby_nodes(4)), 0.0)),
    )
    held_ref[2] = (lane < count_ref[0]).astype(f32)
    for copy in copies:
        copy.wait()
    steps = jnp.zeros((8, 128), f32)
    for k in range(8):
        steps = jnp.where(row == k, steps_ref[k], steps)
    held_ref[1] = steps
    make_lists(y, z, near_ref, far_ref, chunk_ref, chunks_ref)
    for block in range(4):
        center = jnp.zeros((8, 128), f32)
        for k in range(4):
            place = block * 4 + k
            leaf = (y * NZ + place) * MEMBERS + member
            column = column3(centers_ref[0, leaf], centers_ref[1, leaf], centers_ref[2, leaf], (8, 128))
            points = column + HALF_SIDE * jnp.concatenate([recv_ref[3 * place + 2], jnp.zeros((4, 128), f32)], 0)
            a_ref[place * 128 : (place + 1) * 128, :DEPTH] = a_block(source_rows(points))
            center = jnp.where((lane >> 5) == k, column, center)
        proxy_ref[block * 128 : (block + 1) * 128, :DEPTH] = a_block(source_rows(center + HALF_SIDE * offset))
    proxy_ref[512:544, :DEPTH] = proxy_ref[0:32, :DEPTH]
    for other in range(NY):
        for k in range(NZ):
            base = (FAR + other * 4) * 128 + k * 32
            a_ref[base : base + 32] = proxy_ref[pl.ds(pl.multiple_of(far_ref[other, k] * 32, 32), 32)]
    charge_blocks(lambda k: jnp.concatenate([recv_ref[3 * k], recv_ref[3 * k + 1]], 0), ih_ref, il_ref, far_ref, q_ref, wide_ref)


def multiply_tile(chunk_ref, q_ref, acc_ref, i, hi_ref, lo_ref, j, t):
    q = jnp.concatenate([q_ref[chunk_ref[2 * i + k]] for k in range(2)], 1)
    rows = pl.ds(pl.multiple_of(chunk_ref[CHUNK_OWNER + i] * 16, 16), 16)
    cols = slice(t * TILE, (t + 1) * TILE)
    both = jnp.concatenate([hi_ref[j, t], lo_ref[j, t]], 0)
    acc_ref[rows, cols] = acc_ref[rows, cols] + jnp.dot(jnp.concatenate([q, q], 1), both, preferred_element_type=f32)


def in_steps(number, work):
    def four(j, carry):
        for k in range(4):
            work(4 * j + k)
        return carry

    lax.fori_loop(0, number >> 2, four, 0)

    @pl.when((number & 2) == 2)
    def _():
        work((number >> 2) * 4)
        work((number >> 2) * 4 + 1)

    @pl.when((number & 1) == 1)
    def _():
        work(number - 1)


def write_sums(acc_ref, out_ref):
    for other in range(NY):
        total = acc_ref[other * 16 : other * 16 + 8] + acc_ref[other * 16 + 8 : other * 16 + 16]
        for k in range(MEMBERS):
            out_ref[other * MEMBERS + k] = total[:, k * 128 : (k + 1) * 128]


def first_kernel(chunk_ref, count_ref, tgt_ref, a_ref, q_ref, out_ref, eh_ref, el_ref, oh_ref, ol_ref, b_ref, acc_ref):
    for other in range(NY):
        got = jnp.concatenate([tgt_ref[other * MEMBERS + k] for k in range(MEMBERS)], 1)
        one, none = jnp.ones((1, MEMBERS * 128), f32), jnp.zeros((3, MEMBERS * 128), f32)
        h, m, low = split3(jnp.concatenate([got[0:3], one, got[3:4], none], 0))
        b_ref[other] = jnp.concatenate([h, m, h, m, low, h], 0).astype(bf16)
    acc_ref[...] = jnp.zeros_like(acc_ref)
    count = count_ref[0]

    def rows_of(i):
        blocks = [chunk_ref[2 * i + k] for k in range(2)]
        starts = [pl.multiple_of(jnp.where(n == ZERO_BLOCK, 0, n) * 128, 128) for n in blocks]
        return jnp.concatenate([a_ref[pl.ds(n, 128), :DEPTH] for n in starts], 0), chunk_ref[CHUNK_OWNER + i]

    def evaluate_tile(rows, hi_ref, lo_ref, j, t):
        square = jnp.dot(rows[0], b_ref[rows[1], :, t * TILE : (t + 1) * TILE], preferred_element_type=f32)
        hi, lo = split2(lax.rsqrt(square))
        hi_ref[j, t] = hi
        lo_ref[j, t] = lo

    even, odd = (eh_ref, el_ref), (oh_ref, ol_ref)
    mul = functools.partial(multiply_tile, chunk_ref, q_ref, acc_ref)

    def both(done, source, js, new, target, jt):
        rows = rows_of(new)
        for t in range(TILES):
            mul(done, *source, js, t)
            evaluate_tile(rows, *target, jt, t)

    rows = rows_of(0)
    for t in range(TILES):
        evaluate_tile(rows, *even, 0, t)

    def pair(j):
        both(2 * j, even, j, 2 * j + 1, odd, j)
        both(2 * j + 1, odd, j, 2 * j + 2, even, j + 1)

    pairs = (count - 1) >> 1
    in_steps(pairs, pair)

    @pl.when((count & 1) == 0)
    def _():
        both(2 * pairs, even, pairs, 2 * pairs + 1, odd, pairs)
        for t in range(TILES):
            mul(2 * pairs + 1, *odd, pairs, t)

    @pl.when((count & 1) == 1)
    def _():
        for t in range(TILES):
            mul(2 * pairs, *even, pairs, t)

    write_sums(acc_ref, out_ref)


def second_kernel(chunk_ref, count_ref, far_ref, recv_ref, ih_ref, il_ref, eh_ref, el_ref, oh_ref, ol_ref, out_ref, q_ref, wide_ref, acc_ref):
    charge_blocks(lambda k: recv_ref[k], ih_ref, il_ref, far_ref, q_ref, wide_ref)
    acc_ref[...] = jnp.zeros_like(acc_ref)
    count = count_ref[0]
    mul = functools.partial(multiply_tile, chunk_ref, q_ref, acc_ref)

    def pair(j):
        for t in range(TILES):
            mul(2 * j, eh_ref, el_ref, j, t)
            mul(2 * j + 1, oh_ref, ol_ref, j, t)

    in_steps(count >> 1, pair)

    @pl.when((count & 1) == 1)
    def _():
        for t in range(TILES):
            mul(count - 1, eh_ref, el_ref, count >> 1, t)

    write_sums(acc_ref, out_ref)


def update_kernel(scale, last, recv_ref, held_ref, current_ref, new_ref, other_ref):
    parts = [recv_ref[k] for k in range(PLANE)]
    while len(parts) > 1:
        parts = [parts[i] + parts[i + 1] for i in range(0, len(parts), 2)]
    live = held_ref[2]
    residual = live * (held_ref[0] - scale * parts[0])
    new = live * (current_ref[...] + held_ref[1] * residual / (1.0 + jnp.abs(residual)))
    new_ref[...] = new
    if last:
        other_ref[...] = residual
    else:
        for k in range(NZ):
            other_ref[k] = new


VM = pl.BlockSpec(memory_space=pltpu.VMEM)
SM = pl.BlockSpec(memory_space=pltpu.SMEM)
HB = pl.BlockSpec(memory_space=pltpu.HBM)


def sds(shape, dtype=f32):
    return jax.ShapeDtypeStruct(shape, dtype)


def body(leaf_centers, source_coords, target_points, charges, boundary_data, step_sizes, valid_count, near_lists):
    plane = ("y", "x", "core")
    params = pltpu.CompilerParams(vmem_limit_bytes=12 * 2**20)
    small = pltpu.CompilerParams(vmem_limit_bytes=4 * 2**20)
    hbm = functools.partial(pltpu.with_memory_space_constraint, memory_space=pltpu.HBM)
    zsend, tsend, current = pl.pallas_call(
        prologue_kernel,
        out_shape=(sds((3 * NZ, 4, 128)), sds((PLANE, 4, 128)), sds((8, 128))),
        in_specs=[SM, HB, HB, HB],
        out_specs=(VM,) * 3,
        scratch_shapes=[pltpu.VMEM((3, 128), f32), pltpu.VMEM((3, 128), f32), pltpu.SemaphoreType.DMA((3,))],
        compiler_params=small,
        name="prologue",
    )(valid_count, hbm(charges), hbm(source_coords), hbm(target_points))
    recv = lax.all_to_all(zsend, "z", 0, 0, tiled=True)
    recv, tsend = lax.optimization_barrier((recv, tsend))
    targets = lax.all_to_all(tsend, plane, 0, 0, tiled=True)
    interp = sds((NZ * 32, 128), bf16)
    a, ih, il, q, held, far, chunks, count = pl.pallas_call(
        setup_kernel,
        out_shape=(
            sds((ZERO_BLOCK * 128, 128), bf16),
            interp,
            interp,
            sds((ZERO_BLOCK + 1, 16, 128), bf16),
            sds((3, 8, 128)),
            sds((NY, FAR_SLOTS), jnp.int32),
            sds((CHUNK_SLOTS,), jnp.int32),
            sds((1,), jnp.int32),
        ),
        in_specs=[SM, HB, HB, HB, HB, VM],
        out_specs=(VM,) * 5 + (SM,) * 3,
        scratch_shapes=[
            pltpu.VMEM((5, 16, 128), f32),
            pltpu.VMEM((544, 128), bf16),
            pltpu.SMEM((3, NZ * NY * MEMBERS), f32),
            pltpu.SMEM((NEAR, NY * NZ), jnp.int32),
            pltpu.SMEM((8,), f32),
            pltpu.SemaphoreType.DMA((4,)),
        ],
        compiler_params=params,
        cost_estimate=pl.CostEstimate(flops=10**9, bytes_accessed=12 * 10**6, transcendentals=0),
        name="setup",
    )(valid_count, hbm(step_sizes), hbm(leaf_centers), hbm(near_lists.T), hbm(boundary_data), recv)
    scale = 1.0 / math.sqrt(NY * NZ * MEMBERS * 128)
    half = pltpu.VMEM((PAIRS, TILES, 256, TILE), bf16)
    sums, *kernels = pl.pallas_call(
        first_kernel,
        out_shape=(sds((PLANE, 8, 128)), half, half, half, half),
        in_specs=[SM, SM, VM, VM, VM],
        out_specs=(VM,) * 5,
        scratch_shapes=[pltpu.VMEM((NY, DEPTH, MEMBERS * 128), bf16), pltpu.VMEM((NY * 16, MEMBERS * 128), f32)],
        compiler_params=params,
        name="first",
    )(chunks, count, targets, a, q)

    def update(sums, current, last):
        return pl.pallas_call(
            functools.partial(update_kernel, scale, last),
            out_shape=(sds((8, 128)), sds((8, 128) if last else (NZ, 8, 128))),
            in_specs=[VM, VM, VM],
            out_specs=(VM, VM),
            compiler_params=small,
            name="update",
        )(lax.all_to_all(sums, plane, 0, 0, tiled=True), held, current)

    current, zsend = update(sums, current, False)
    recv = lax.all_to_all(zsend, "z", 0, 0, tiled=True)
    sums = pl.pallas_call(
        second_kernel,
        out_shape=sds((PLANE, 8, 128)),
        in_specs=[SM, SM, SM] + [VM] * 7,
        out_specs=VM,
        scratch_shapes=[
            pltpu.VMEM((ZERO_BLOCK + 1, 16, 128), bf16),
            pltpu.VMEM((5, 16, 128), f32),
            pltpu.VMEM((NY * 16, MEMBERS * 128), f32),
        ],
        compiler_params=params,
        name="second",
    )(chunks, count, far, recv, ih, il, *kernels)
    current, residual = update(sums, current, True)
    return (current, residual)


def solution(mesh):
    grid = Mesh(mesh.devices.reshape(NY, NZ, NX, NC), ("y", "z", "x", "core"))
    split = P(None, ("y", "z", "x", "core"))
    in_specs = (P(), split, split, split, split, P(), P(("y", "z", "x", "core")), P())
    return jax.shard_map(body, mesh=grid, in_specs=in_specs, out_specs=(split, split), check_vma=False)
```

```python
import functools
import math

import jax
import jax.numpy as jnp
import numpy as np
from jax import lax
from jax.experimental import pallas as pl
from jax.experimental.pallas import tpu as pltpu
from jax.sharding import Mesh
from jax.sharding import PartitionSpec as P

HALF_SIDE = 0.08
SOFTENING = 0.0025
NY, NZ, NX, NC = 4, 16, 4, 2
MEMBERS = NX * NC
PLANE = NY * MEMBERS
NEAR = 26
DEPTH = 48
FAR = NZ
ZERO_BLOCK = FAR + 4 * NY
FAR_SLOTS = 16
CHUNK_OWNER = 80
CHUNK_SLOTS = 128
PAIRS = 17
TILE = 256
TILES = MEMBERS * 128 // TILE
bf16, f32 = jnp.bfloat16, jnp.float32


def cheby_nodes(number):
    return np.cos(np.pi * (2 * np.arange(number) + 1) / (2 * number))


def pick(index, values):
    out = jnp.full(index.shape, float(values[0]), f32)
    for k in range(1, len(values)):
        out = jnp.where(index == k, float(values[k]), out)
    return out


def iota(shape, dim):
    return lax.broadcasted_iota(jnp.int32, shape, dim)


def split3(v):
    h = v.astype(bf16).astype(f32)
    r = v - h
    m = r.astype(bf16).astype(f32)
    low = (r - m).astype(bf16).astype(f32)
    return h, m, low


def split2(v):
    h = v.astype(bf16)
    return h, (v - h.astype(f32)).astype(bf16)


def source_rows(pts):
    row = iota(pts.shape, 0)
    s = jnp.where(row < 3, pts - 0.5, 0.0)
    norm = jnp.sum(s * s, axis=0, keepdims=True) + SOFTENING
    return jnp.where(row < 3, -2.0 * s, jnp.where(row == 3, norm, jnp.where(row == 4, 1.0, 0.0)))


def target_rows(pts):
    t = pts - 0.5
    return jnp.concatenate([t, jnp.sum(t * t, axis=0, keepdims=True)], 0)


def column3(a, b, c, shape):
    row = iota(shape, 0)
    return jnp.where(row == 0, a, jnp.where(row == 1, b, jnp.where(row == 2, c, 0.0)))


def here():
    member = lax.axis_index("x") * NC + lax.axis_index("core")
    return lax.axis_index("y"), lax.axis_index("z"), member


def a_block(rows):
    h, m, low = split3(rows)
    return jnp.concatenate([h, h, m, m, h, low], 0).T.astype(bf16)


def interp_tables():
    p = iota((32, 128), 0)
    parts = (p >> 4, (p >> 2) & 3, p & 3)
    tables = []
    for index, number in zip(parts, (2, 4, 4)):
        nodes = cheby_nodes(number)
        others = [[nodes[i] for i in range(number) if i != k] for k in range(number)]
        roots = [pick(index, [others[k][j] for k in range(number)]) for j in range(number - 1)]
        scale = pick(index, [1.0 / np.prod([nodes[k] - o for o in others[k]]) for k in range(number)])
        tables.append((roots, scale))
    return tables


def make_lists(y, z, near_ref, far_ref, chunk_ref, count_ref):
    total = jnp.int32(0)
    for other in range(NY):
        bits = jnp.where(y == other, 1 << z, 0)
        for j in range(NEAR):
            cluster = near_ref[j, other * NZ + z]
            bits = bits | jnp.where((cluster >> 4) == y, 1 << (cluster & 15), 0)
        near_count = jnp.int32(0)
        for k in range(NZ):
            far_ref[other, k] = NZ
        for k in range(NZ):
            mine = (bits >> k) & 1
            chunk_ref[total + near_count] = k
            far_ref[other, k - near_count] = jnp.where(mine > 0, NZ, k)
            near_count = near_count + mine
        far_blocks = (NZ + 3 - near_count) >> 2
        start = total + near_count
        for k in range(4):
            chunk_ref[start + k] = FAR + other * 4 + k
        end = start + far_blocks
        chunk_ref[end] = ZERO_BLOCK
        for k in range(8):
            chunk_ref[CHUNK_OWNER + (total >> 1) + k] = other
        total = ((end + 1) >> 1) << 1
    count_ref[0] = total >> 1


def prologue_kernel(count_ref, charges_hbm, coords_hbm, targets_hbm, zsend_ref, tsend_ref, current_ref, coords_ref, targets_ref, sem):
    moves = ((charges_hbm, current_ref), (coords_hbm, coords_ref), (targets_hbm, targets_ref))
    copies = [pltpu.make_async_copy(source, target, sem.at[k]) for k, (source, target) in enumerate(moves)]
    for copy in copies:
        copy.start()
    for copy in copies:
        copy.wait()
    current = current_ref[...] * (iota((8, 128), 1) < count_ref[0]).astype(f32)
    current_ref[...] = current
    coords = jnp.concatenate([coords_ref[...], jnp.zeros((1, 128), f32)], 0)
    for k in range(NZ):
        zsend_ref[3 * k] = current[0:4]
        zsend_ref[3 * k + 1] = current[4:8]
        zsend_ref[3 * k + 2] = coords
    rows = target_rows(targets_ref[...])
    for k in range(PLANE):
        tsend_ref[k] = rows


def charge_blocks(charges, ih_ref, il_ref, far_ref, q_ref, wide_ref):
    nt = (((1,), (1,)), ((), ()))
    group = iota((16, 128), 1) >> 5
    for block in range(4):
        rows = []
        for k in range(4 * block, 4 * block + 4):
            hi, lo = split2(charges(k))
            q = jnp.concatenate([hi.astype(f32), lo.astype(f32)], 0).astype(bf16)
            q_ref[k] = q
            rows.append(q)
        rows = jnp.concatenate(rows, 0)
        part = slice(block * 128, (block + 1) * 128)
        both = lax.dot_general(rows, ih_ref[part], nt, preferred_element_type=f32)
        both = both + lax.dot_general(rows, il_ref[part], nt, preferred_element_type=f32)
        own = both[0:16]
        for k in range(1, 4):
            own = jnp.where(group == k, both[16 * k : 16 * k + 16], own)
        wide = own[0:8] + own[8:16]
        hi = wide.astype(bf16).astype(f32)
        wide_ref[block] = jnp.concatenate([hi, wide - hi], 0)
    wide_ref[4] = jnp.zeros((16, 128), f32)
    q_ref[ZERO_BLOCK] = jnp.zeros((16, 128), bf16)
    for other in range(NY):
        for block in range(4):
            out = None
            for k in range(4):
                leaf = far_ref[other, block * 4 + k]
                moved = pltpu.roll(wide_ref[leaf >> 2], ((4 + k - leaf) & 3) * 32, 1)
                out = moved if out is None else jnp.where(group == k, moved, out)
            q_ref[FAR + other * 4 + block] = out.astype(bf16)


def setup_kernel(
    count_ref, steps_hbm, centers_hbm, near_hbm, boundary_hbm, recv_ref,
    a_ref, ih_ref, il_ref, q_ref, held_ref, far_ref, chunk_ref, chunks_ref,
    wide_ref, proxy_ref, centers_ref, near_ref, steps_ref, sem,
):
    y, z, member = here()
    moves = ((near_hbm, near_ref), (centers_hbm, centers_ref), (boundary_hbm, held_ref.at[0]), (steps_hbm, steps_ref))
    copies = [pltpu.make_async_copy(source, target, sem.at[k]) for k, (source, target) in enumerate(moves)]
    for copy in copies:
        copy.start()
    tables = interp_tables()
    for k in range(NZ):
        rows = recv_ref[3 * k + 2]
        value = None
        for axis, (roots, scale) in enumerate(tables):
            u = jnp.broadcast_to(rows[axis : axis + 1], (32, 128))
            line = scale
            for root in roots:
                line = line * (u - root)
            value = line if value is None else value * line
        hi, lo = split2(value)
        ih_ref[k * 32 : (k + 1) * 32] = hi
        il_ref[k * 32 : (k + 1) * 32] = lo
    lane = iota((8, 128), 1)
    row = iota((8, 128), 0)
    p = lane & 31
    offset = jnp.where(
        row == 0,
        pick(p >> 4, cheby_nodes(2)),
        jnp.where(row == 1, pick((p >> 2) & 3, cheby_nodes(4)), jnp.where(row == 2, pick(p & 3, cheby_nodes(4)), 0.0)),
    )
    held_ref[2] = (lane < count_ref[0]).astype(f32)
    for copy in copies:
        copy.wait()
    steps = jnp.zeros((8, 128), f32)
    for k in range(8):
        steps = jnp.where(row == k, steps_ref[k], steps)
    held_ref[1] = steps
    make_lists(y, z, near_ref, far_ref, chunk_ref, chunks_ref)
    for block in range(4):
        center = jnp.zeros((8, 128), f32)
        for k in range(4):
            place = block * 4 + k
            leaf = (y * NZ + place) * MEMBERS + member
            column = column3(centers_ref[0, leaf], centers_ref[1, leaf], centers_ref[2, leaf], (8, 128))
            points = column + HALF_SIDE * jnp.concatenate([recv_ref[3 * place + 2], jnp.zeros((4, 128), f32)], 0)
            a_ref[place * 128 : (place + 1) * 128, :DEPTH] = a_block(source_rows(points))
            center = jnp.where((lane >> 5) == k, column, center)
        proxy_ref[block * 128 : (block + 1) * 128, :DEPTH] = a_block(source_rows(center + HALF_SIDE * offset))
    proxy_ref[512:544, :DEPTH] = proxy_ref[0:32, :DEPTH]
    for other in range(NY):
        for k in range(NZ):
            base = (FAR + other * 4) * 128 + k * 32
            a_ref[base : base + 32] = proxy_ref[pl.ds(pl.multiple_of(far_ref[other, k] * 32, 32), 32)]
    charge_blocks(lambda k: jnp.concatenate([recv_ref[3 * k], recv_ref[3 * k + 1]], 0), ih_ref, il_ref, far_ref, q_ref, wide_ref)


def multiply_tile(chunk_ref, q_ref, acc_ref, i, hi_ref, lo_ref, j, t):
    q = jnp.concatenate([q_ref[chunk_ref[2 * i + k]] for k in range(2)], 1)
    rows = pl.ds(pl.multiple_of(chunk_ref[CHUNK_OWNER + i] * 16, 16), 16)
    cols = slice(t * TILE, (t + 1) * TILE)
    both = jnp.concatenate([hi_ref[j, t], lo_ref[j, t]], 0)
    acc_ref[rows, cols] = acc_ref[rows, cols] + jnp.dot(jnp.concatenate([q, q], 1), both, preferred_element_type=f32)


def in_steps(number, work):
    def four(j, carry):
        for k in range(4):
            work(4 * j + k)
        return carry

    lax.fori_loop(0, number >> 2, four, 0)

    @pl.when((number & 2) == 2)
    def _():
        work((number >> 2) * 4)
        work((number >> 2) * 4 + 1)

    @pl.when((number & 1) == 1)
    def _():
        work(number - 1)


def write_sums(acc_ref, out_ref):
    for other in range(NY):
        total = acc_ref[other * 16 : other * 16 + 8] + acc_ref[other * 16 + 8 : other * 16 + 16]
        for k in range(MEMBERS):
            out_ref[other * MEMBERS + k] = total[:, k * 128 : (k + 1) * 128]


def first_kernel(chunk_ref, count_ref, tgt_ref, a_ref, q_ref, out_ref, eh_ref, el_ref, oh_ref, ol_ref, b_ref, acc_ref):
    for other in range(NY):
        got = jnp.concatenate([tgt_ref[other * MEMBERS + k] for k in range(MEMBERS)], 1)
        one, none = jnp.ones((1, MEMBERS * 128), f32), jnp.zeros((3, MEMBERS * 128), f32)
        h, m, low = split3(jnp.concatenate([got[0:3], one, got[3:4], none], 0))
        b_ref[other] = jnp.concatenate([h, m, h, m, low, h], 0).astype(bf16)
    acc_ref[...] = jnp.zeros_like(acc_ref)
    count = count_ref[0]

    def rows_of(i):
        blocks = [chunk_ref[2 * i + k] for k in range(2)]
        starts = [pl.multiple_of(jnp.where(n == ZERO_BLOCK, 0, n) * 128, 128) for n in blocks]
        return jnp.concatenate([a_ref[pl.ds(n, 128), :DEPTH] for n in starts], 0), chunk_ref[CHUNK_OWNER + i]

    def evaluate_tile(rows, hi_ref, lo_ref, j, t):
        square = jnp.dot(rows[0], b_ref[rows[1], :, t * TILE : (t + 1) * TILE], preferred_element_type=f32)
        hi, lo = split2(lax.rsqrt(square))
        hi_ref[j, t] = hi
        lo_ref[j, t] = lo

    even, odd = (eh_ref, el_ref), (oh_ref, ol_ref)
    mul = functools.partial(multiply_tile, chunk_ref, q_ref, acc_ref)

    def both(done, source, js, new, target, jt):
        rows = rows_of(new)
        for t in range(TILES):
            mul(done, *source, js, t)
            evaluate_tile(rows, *target, jt, t)

    rows = rows_of(0)
    for t in range(TILES):
        evaluate_tile(rows, *even, 0, t)

    def pair(j):
        both(2 * j, even, j, 2 * j + 1, odd, j)
        both(2 * j + 1, odd, j, 2 * j + 2, even, j + 1)

    pairs = (count - 1) >> 1
    in_steps(pairs, pair)

    @pl.when((count & 1) == 0)
    def _():
        both(2 * pairs, even, pairs, 2 * pairs + 1, odd, pairs)
        for t in range(TILES):
            mul(2 * pairs + 1, *odd, pairs, t)

    @pl.when((count & 1) == 1)
    def _():
        for t in range(TILES):
            mul(2 * pairs, *even, pairs, t)

    write_sums(acc_ref, out_ref)


def second_kernel(chunk_ref, count_ref, far_ref, recv_ref, ih_ref, il_ref, eh_ref, el_ref, oh_ref, ol_ref, out_ref, q_ref, wide_ref, acc_ref):
    charge_blocks(lambda k: recv_ref[k], ih_ref, il_ref, far_ref, q_ref, wide_ref)
    acc_ref[...] = jnp.zeros_like(acc_ref)
    count = count_ref[0]
    mul = functools.partial(multiply_tile, chunk_ref, q_ref, acc_ref)

    def pair(j):
        for t in range(TILES):
            mul(2 * j, eh_ref, el_ref, j, t)
            mul(2 * j + 1, oh_ref, ol_ref, j, t)

    in_steps(count >> 1, pair)

    @pl.when((count & 1) == 1)
    def _():
        for t in range(TILES):
            mul(count - 1, eh_ref, el_ref, count >> 1, t)

    write_sums(acc_ref, out_ref)


def update_kernel(scale, last, recv_ref, held_ref, current_ref, new_ref, other_ref):
    parts = [recv_ref[k] for k in range(PLANE)]
    while len(parts) > 1:
        parts = [parts[i] + parts[i + 1] for i in range(0, len(parts), 2)]
    live = held_ref[2]
    residual = live * (held_ref[0] - scale * parts[0])
    new = live * (current_ref[...] + held_ref[1] * residual / (1.0 + jnp.abs(residual)))
    new_ref[...] = new
    if last:
        other_ref[...] = residual
    else:
        for k in range(NZ):
            other_ref[k] = new


VM = pl.BlockSpec(memory_space=pltpu.VMEM)
SM = pl.BlockSpec(memory_space=pltpu.SMEM)
HB = pl.BlockSpec(memory_space=pltpu.HBM)


def sds(shape, dtype=f32):
    return jax.ShapeDtypeStruct(shape, dtype)


def body(leaf_centers, source_coords, target_points, charges, boundary_data, step_sizes, valid_count, near_lists):
    plane = ("y", "x", "core")
    params = pltpu.CompilerParams(vmem_limit_bytes=12 * 2**20)
    small = pltpu.CompilerParams(vmem_limit_bytes=4 * 2**20)
    hbm = functools.partial(pltpu.with_memory_space_constraint, memory_space=pltpu.HBM)
    zsend, tsend, current = pl.pallas_call(
        prologue_kernel,
        out_shape=(sds((3 * NZ, 4, 128)), sds((PLANE, 4, 128)), sds((8, 128))),
        in_specs=[SM, HB, HB, HB],
        out_specs=(VM,) * 3,
        scratch_shapes=[pltpu.VMEM((3, 128), f32), pltpu.VMEM((3, 128), f32), pltpu.SemaphoreType.DMA((3,))],
        compiler_params=small,
        name="prologue",
    )(valid_count, hbm(charges), hbm(source_coords), hbm(target_points))
    recv = lax.all_to_all(zsend, "z", 0, 0, tiled=True)
    recv, tsend = lax.optimization_barrier((recv, tsend))
    targets = lax.all_to_all(tsend, plane, 0, 0, tiled=True)
    interp = sds((NZ * 32, 128), bf16)
    a, ih, il, q, held, far, chunks, count = pl.pallas_call(
        setup_kernel,
        out_shape=(
            sds((ZERO_BLOCK * 128, 128), bf16),
            interp,
            interp,
            sds((ZERO_BLOCK + 1, 16, 128), bf16),
            sds((3, 8, 128)),
            sds((NY, FAR_SLOTS), jnp.int32),
            sds((CHUNK_SLOTS,), jnp.int32),
            sds((1,), jnp.int32),
        ),
        in_specs=[SM, HB, HB, HB, HB, VM],
        out_specs=(VM,) * 5 + (SM,) * 3,
        scratch_shapes=[
            pltpu.VMEM((5, 16, 128), f32),
            pltpu.VMEM((544, 128), bf16),
            pltpu.SMEM((3, NZ * NY * MEMBERS), f32),
            pltpu.SMEM((NEAR, NY * NZ), jnp.int32),
            pltpu.SMEM((8,), f32),
            pltpu.SemaphoreType.DMA((4,)),
        ],
        compiler_params=params,
        cost_estimate=pl.CostEstimate(flops=10**9, bytes_accessed=12 * 10**6, transcendentals=0),
        name="setup",
    )(valid_count, hbm(step_sizes), hbm(leaf_centers), hbm(near_lists.T), hbm(boundary_data), recv)
    scale = 1.0 / math.sqrt(NY * NZ * MEMBERS * 128)
    half = pltpu.VMEM((PAIRS, TILES, 256, TILE), bf16)
    sums, *kernels = pl.pallas_call(
        first_kernel,
        out_shape=(sds((PLANE, 8, 128)), half, half, half, half),
        in_specs=[SM, SM, VM, VM, VM],
        out_specs=(VM,) * 5,
        scratch_shapes=[pltpu.VMEM((NY, DEPTH, MEMBERS * 128), bf16), pltpu.VMEM((NY * 16, MEMBERS * 128), f32)],
        compiler_params=params,
        name="first",
    )(chunks, count, targets, a, q)

    def update(sums, current, last):
        return pl.pallas_call(
            functools.partial(update_kernel, scale, last),
            out_shape=(sds((8, 128)), sds((8, 128) if last else (NZ, 8, 128))),
            in_specs=[VM, VM, VM],
            out_specs=(VM, VM),
            compiler_params=small,
            name="update",
        )(lax.all_to_all(sums, plane, 0, 0, tiled=True), held, current)

    current, zsend = update(sums, current, False)
    recv = lax.all_to_all(zsend, "z", 0, 0, tiled=True)
    sums = pl.pallas_call(
        second_kernel,
        out_shape=sds((PLANE, 8, 128)),
        in_specs=[SM, SM, SM] + [VM] * 7,
        out_specs=VM,
        scratch_shapes=[
            pltpu.VMEM((ZERO_BLOCK + 1, 16, 128), bf16),
            pltpu.VMEM((5, 16, 128), f32),
            pltpu.VMEM((NY * 16, MEMBERS * 128), f32),
        ],
        compiler_params=params,
        name="second",
    )(chunks, count, far, recv, ih, il, *kernels)
    current, residual = update(sums, current, True)
    return (current, residual)


def solution(mesh):
    grid = Mesh(mesh.devices.reshape(NY, NZ, NX, NC), ("y", "z", "x", "core"))
    split = P(None, ("y", "z", "x", "core"))
    in_specs = (P(), split, split, split, split, P(), P(("y", "z", "x", "core")), P())
    return jax.shard_map(body, mesh=grid, in_specs=in_specs, out_specs=(split, split), check_vma=False)
```

```python
import functools
import math

import jax
import jax.numpy as jnp
import numpy as np
from jax import lax
from jax.experimental import pallas as pl
from jax.experimental.pallas import tpu as pltpu
from jax.sharding import Mesh
from jax.sharding import PartitionSpec as P

HALF_SIDE = 0.08
SOFTENING = 0.0025
NY, NZ, NX, NC = 4, 16, 4, 2
MEMBERS = NX * NC
PLANE = NY * MEMBERS
NEAR = 26
DEPTH = 48
FAR = NZ
ZERO_BLOCK = FAR + 4 * NY
FAR_SLOTS = 16
CHUNK_OWNER = 80
CHUNK_SLOTS = 128
PAIRS = 17
TILE = 256
TILES = MEMBERS * 128 // TILE
bf16, f32 = jnp.bfloat16, jnp.float32


def cheby_nodes(number):
    return np.cos(np.pi * (2 * np.arange(number) + 1) / (2 * number))


def pick(index, values):
    out = jnp.full(index.shape, float(values[0]), f32)
    for k in range(1, len(values)):
        out = jnp.where(index == k, float(values[k]), out)
    return out


def iota(shape, dim):
    return lax.broadcasted_iota(jnp.int32, shape, dim)


def split3(v):
    h = v.astype(bf16).astype(f32)
    r = v - h
    m = r.astype(bf16).astype(f32)
    low = (r - m).astype(bf16).astype(f32)
    return h, m, low


def split2(v):
    h = v.astype(bf16)
    return h, (v - h.astype(f32)).astype(bf16)


def source_rows(pts):
    row = iota(pts.shape, 0)
    s = jnp.where(row < 3, pts - 0.5, 0.0)
    norm = jnp.sum(s * s, axis=0, keepdims=True) + SOFTENING
    return jnp.where(row < 3, -2.0 * s, jnp.where(row == 3, norm, jnp.where(row == 4, 1.0, 0.0)))


def target_rows(pts):
    t = pts - 0.5
    return jnp.concatenate([t, jnp.sum(t * t, axis=0, keepdims=True)], 0)


def column3(a, b, c, shape):
    row = iota(shape, 0)
    return jnp.where(row == 0, a, jnp.where(row == 1, b, jnp.where(row == 2, c, 0.0)))


def here():
    member = lax.axis_index("x") * NC + lax.axis_index("core")
    return lax.axis_index("y"), lax.axis_index("z"), member


def a_block(rows):
    h, m, low = split3(rows)
    return jnp.concatenate([h, h, m, m, h, low], 0).T.astype(bf16)


def interp_tables():
    p = iota((32, 128), 0)
    parts = (p >> 4, (p >> 2) & 3, p & 3)
    tables = []
    for index, number in zip(parts, (2, 4, 4)):
        nodes = cheby_nodes(number)
        others = [[nodes[i] for i in range(number) if i != k] for k in range(number)]
        roots = [pick(index, [others[k][j] for k in range(number)]) for j in range(number - 1)]
        scale = pick(index, [1.0 / np.prod([nodes[k] - o for o in others[k]]) for k in range(number)])
        tables.append((roots, scale))
    return tables


def make_lists(y, z, near_ref, far_ref, chunk_ref, count_ref):
    total = jnp.int32(0)
    for other in range(NY):
        bits = jnp.where(y == other, 1 << z, 0)
        for j in range(NEAR):
            cluster = near_ref[j, other * NZ + z]
            bits = bits | jnp.where((cluster >> 4) == y, 1 << (cluster & 15), 0)
        near_count = jnp.int32(0)
        for k in range(NZ):
            far_ref[other, k] = NZ
        for k in range(NZ):
            mine = (bits >> k) & 1
            chunk_ref[total + near_count] = k
            far_ref[other, k - near_count] = jnp.where(mine > 0, NZ, k)
            near_count = near_count + mine
        far_blocks = (NZ + 3 - near_count) >> 2
        start = total + near_count
        for k in range(4):
            chunk_ref[start + k] = FAR + other * 4 + k
        end = start + far_blocks
        chunk_ref[end] = ZERO_BLOCK
        for k in range(8):
            chunk_ref[CHUNK_OWNER + (total >> 1) + k] = other
        total = ((end + 1) >> 1) << 1
    count_ref[0] = total >> 1


def prologue_kernel(count_ref, charges_hbm, coords_hbm, targets_hbm, zsend_ref, tsend_ref, current_ref, coords_ref, targets_ref, sem):
    moves = ((charges_hbm, current_ref), (coords_hbm, coords_ref), (targets_hbm, targets_ref))
    copies = [pltpu.make_async_copy(source, target, sem.at[k]) for k, (source, target) in enumerate(moves)]
    for copy in copies:
        copy.start()
    for copy in copies:
        copy.wait()
    current = current_ref[...] * (iota((8, 128), 1) < count_ref[0]).astype(f32)
    current_ref[...] = current
    coords = jnp.concatenate([coords_ref[...], jnp.zeros((1, 128), f32)], 0)
    for k in range(NZ):
        zsend_ref[3 * k] = current[0:4]
        zsend_ref[3 * k + 1] = current[4:8]
        zsend_ref[3 * k + 2] = coords
    rows = target_rows(targets_ref[...])
    for k in range(PLANE):
        tsend_ref[k] = rows


def charge_blocks(charges, ih_ref, il_ref, far_ref, q_ref, wide_ref):
    nt = (((1,), (1,)), ((), ()))
    group = iota((16, 128), 1) >> 5
    for block in range(4):
        rows = []
        for k in range(4 * block, 4 * block + 4):
            hi, lo = split2(charges(k))
            q = jnp.concatenate([hi.astype(f32), lo.astype(f32)], 0).astype(bf16)
            q_ref[k] = q
            rows.append(q)
        rows = jnp.concatenate(rows, 0)
        part = slice(block * 128, (block + 1) * 128)
        both = lax.dot_general(rows, ih_ref[part], nt, preferred_element_type=f32)
        both = both + lax.dot_general(rows, il_ref[part], nt, preferred_element_type=f32)
        own = both[0:16]
        for k in range(1, 4):
            own = jnp.where(group == k, both[16 * k : 16 * k + 16], own)
        wide = own[0:8] + own[8:16]
        hi = wide.astype(bf16).astype(f32)
        wide_ref[block] = jnp.concatenate([hi, wide - hi], 0)
    wide_ref[4] = jnp.zeros((16, 128), f32)
    q_ref[ZERO_BLOCK] = jnp.zeros((16, 128), bf16)
    for other in range(NY):
        for block in range(4):
            out = None
            for k in range(4):
                leaf = far_ref[other, block * 4 + k]
                moved = pltpu.roll(wide_ref[leaf >> 2], ((4 + k - leaf) & 3) * 32, 1)
                out = moved if out is None else jnp.where(group == k, moved, out)
            q_ref[FAR + other * 4 + block] = out.astype(bf16)


def setup_kernel(
    count_ref, steps_hbm, centers_hbm, near_hbm, boundary_hbm, recv_ref,
    a_ref, ih_ref, il_ref, q_ref, held_ref, far_ref, chunk_ref, chunks_ref,
    wide_ref, proxy_ref, centers_ref, near_ref, steps_ref, sem,
):
    y, z, member = here()
    moves = ((near_hbm, near_ref), (centers_hbm, centers_ref), (boundary_hbm, held_ref.at[0]), (steps_hbm, steps_ref))
    copies = [pltpu.make_async_copy(source, target, sem.at[k]) for k, (source, target) in enumerate(moves)]
    for copy in copies:
        copy.start()
    tables = interp_tables()
    for k in range(NZ):
        rows = recv_ref[3 * k + 2]
        value = None
        for axis, (roots, scale) in enumerate(tables):
            u = jnp.broadcast_to(rows[axis : axis + 1], (32, 128))
            line = scale
            for root in roots:
                line = line * (u - root)
            value = line if value is None else value * line
        hi, lo = split2(value)
        ih_ref[k * 32 : (k + 1) * 32] = hi
        il_ref[k * 32 : (k + 1) * 32] = lo
    lane = iota((8, 128), 1)
    row = iota((8, 128), 0)
    p = lane & 31
    offset = jnp.where(
        row == 0,
        pick(p >> 4, cheby_nodes(2)),
        jnp.where(row == 1, pick((p >> 2) & 3, cheby_nodes(4)), jnp.where(row == 2, pick(p & 3, cheby_nodes(4)), 0.0)),
    )
    held_ref[2] = (lane < count_ref[0]).astype(f32)
    for copy in copies:
        copy.wait()
    steps = jnp.zeros((8, 128), f32)
    for k in range(8):
        steps = jnp.where(row == k, steps_ref[k], steps)
    held_ref[1] = steps
    make_lists(y, z, near_ref, far_ref, chunk_ref, chunks_ref)
    for block in range(4):
        center = jnp.zeros((8, 128), f32)
        for k in range(4):
            place = block * 4 + k
            leaf = (y * NZ + place) * MEMBERS + member
            column = column3(centers_ref[0, leaf], centers_ref[1, leaf], centers_ref[2, leaf], (8, 128))
            points = column + HALF_SIDE * jnp.concatenate([recv_ref[3 * place + 2], jnp.zeros((4, 128), f32)], 0)
            a_ref[place * 128 : (place + 1) * 128, :DEPTH] = a_block(source_rows(points))
            center = jnp.where((lane >> 5) == k, column, center)
        proxy_ref[block * 128 : (block + 1) * 128, :DEPTH] = a_block(source_rows(center + HALF_SIDE * offset))
    proxy_ref[512:544, :DEPTH] = proxy_ref[0:32, :DEPTH]
    for other in range(NY):
        for k in range(NZ):
            base = (FAR + other * 4) * 128 + k * 32
            a_ref[base : base + 32] = proxy_ref[pl.ds(pl.multiple_of(far_ref[other, k] * 32, 32), 32)]
    charge_blocks(lambda k: jnp.concatenate([recv_ref[3 * k], recv_ref[3 * k + 1]], 0), ih_ref, il_ref, far_ref, q_ref, wide_ref)


def multiply_tile(chunk_ref, q_ref, acc_ref, i, hi_ref, lo_ref, j, t):
    q = jnp.concatenate([q_ref[chunk_ref[2 * i + k]] for k in range(2)], 1)
    rows = pl.ds(pl.multiple_of(chunk_ref[CHUNK_OWNER + i] * 16, 16), 16)
    cols = slice(t * TILE, (t + 1) * TILE)
    both = jnp.concatenate([hi_ref[j, t], lo_ref[j, t]], 0)
    acc_ref[rows, cols] = acc_ref[rows, cols] + jnp.dot(jnp.concatenate([q, q], 1), both, preferred_element_type=f32)


def in_steps(number, work, most=4):
    def many(j, carry):
        for k in range(most):
            work(most * j + k)
        return carry

    lax.fori_loop(0, number // most, many, 0)
    size = most // 2
    while size:

        @pl.when((number & size) == size)
        def _(size=size):
            start = number // (2 * size) * (2 * size)
            for k in range(size):
                work(start + k)

        size //= 2


def write_sums(acc_ref, out_ref):
    for other in range(NY):
        total = acc_ref[other * 16 : other * 16 + 8] + acc_ref[other * 16 + 8 : other * 16 + 16]
        for k in range(MEMBERS):
            out_ref[other * MEMBERS + k] = total[:, k * 128 : (k + 1) * 128]


def first_kernel(chunk_ref, count_ref, tgt_ref, a_ref, q_ref, out_ref, eh_ref, el_ref, oh_ref, ol_ref, b_ref, acc_ref):
    for other in range(NY):
        got = jnp.concatenate([tgt_ref[other * MEMBERS + k] for k in range(MEMBERS)], 1)
        one, none = jnp.ones((1, MEMBERS * 128), f32), jnp.zeros((3, MEMBERS * 128), f32)
        h, m, low = split3(jnp.concatenate([got[0:3], one, got[3:4], none], 0))
        b_ref[other] = jnp.concatenate([h, m, h, m, low, h], 0).astype(bf16)
    acc_ref[...] = jnp.zeros_like(acc_ref)
    count = count_ref[0]

    def rows_of(i):
        blocks = [chunk_ref[2 * i + k] for k in range(2)]
        starts = [pl.multiple_of(jnp.where(n == ZERO_BLOCK, 0, n) * 128, 128) for n in blocks]
        return jnp.concatenate([a_ref[pl.ds(n, 128), :DEPTH] for n in starts], 0), chunk_ref[CHUNK_OWNER + i]

    def evaluate_tile(rows, hi_ref, lo_ref, j, t):
        square = jnp.dot(rows[0], b_ref[rows[1], :, t * TILE : (t + 1) * TILE], preferred_element_type=f32)
        hi, lo = split2(lax.rsqrt(square))
        hi_ref[j, t] = hi
        lo_ref[j, t] = lo

    even, odd = (eh_ref, el_ref), (oh_ref, ol_ref)
    mul = functools.partial(multiply_tile, chunk_ref, q_ref, acc_ref)

    def both(done, source, js, new, target, jt):
        rows = rows_of(new)
        for t in range(TILES):
            mul(done, *source, js, t)
            evaluate_tile(rows, *target, jt, t)

    rows = rows_of(0)
    for t in range(TILES):
        evaluate_tile(rows, *even, 0, t)

    def pair(j):
        both(2 * j, even, j, 2 * j + 1, odd, j)
        both(2 * j + 1, odd, j, 2 * j + 2, even, j + 1)

    pairs = (count - 1) >> 1
    in_steps(pairs, pair)

    @pl.when((count & 1) == 0)
    def _():
        both(2 * pairs, even, pairs, 2 * pairs + 1, odd, pairs)
        for t in range(TILES):
            mul(2 * pairs + 1, *odd, pairs, t)

    @pl.when((count & 1) == 1)
    def _():
        for t in range(TILES):
            mul(2 * pairs, *even, pairs, t)

    write_sums(acc_ref, out_ref)


def second_kernel(chunk_ref, count_ref, far_ref, recv_ref, ih_ref, il_ref, eh_ref, el_ref, oh_ref, ol_ref, out_ref, q_ref, wide_ref, acc_ref):
    charge_blocks(lambda k: recv_ref[k], ih_ref, il_ref, far_ref, q_ref, wide_ref)
    acc_ref[...] = jnp.zeros_like(acc_ref)
    count = count_ref[0]
    mul = functools.partial(multiply_tile, chunk_ref, q_ref, acc_ref)

    def pair(j):
        for t in range(TILES):
            mul(2 * j, eh_ref, el_ref, j, t)
            mul(2 * j + 1, oh_ref, ol_ref, j, t)

    in_steps(count >> 1, pair, 8)

    @pl.when((count & 1) == 1)
    def _():
        for t in range(TILES):
            mul(count - 1, eh_ref, el_ref, count >> 1, t)

    write_sums(acc_ref, out_ref)


def update_kernel(scale, last, recv_ref, held_ref, current_ref, new_ref, other_ref):
    parts = [recv_ref[k] for k in range(PLANE)]
    while len(parts) > 1:
        parts = [parts[i] + parts[i + 1] for i in range(0, len(parts), 2)]
    live = held_ref[2]
    residual = live * (held_ref[0] - scale * parts[0])
    new = live * (current_ref[...] + held_ref[1] * residual / (1.0 + jnp.abs(residual)))
    new_ref[...] = new
    if last:
        other_ref[...] = residual
    else:
        for k in range(NZ):
            other_ref[k] = new


VM = pl.BlockSpec(memory_space=pltpu.VMEM)
SM = pl.BlockSpec(memory_space=pltpu.SMEM)
HB = pl.BlockSpec(memory_space=pltpu.HBM)


def sds(shape, dtype=f32):
    return jax.ShapeDtypeStruct(shape, dtype)


def body(leaf_centers, source_coords, target_points, charges, boundary_data, step_sizes, valid_count, near_lists):
    plane = ("y", "x", "core")
    params = pltpu.CompilerParams(vmem_limit_bytes=12 * 2**20)
    small = pltpu.CompilerParams(vmem_limit_bytes=4 * 2**20)
    hbm = functools.partial(pltpu.with_memory_space_constraint, memory_space=pltpu.HBM)
    zsend, tsend, current = pl.pallas_call(
        prologue_kernel,
        out_shape=(sds((3 * NZ, 4, 128)), sds((PLANE, 4, 128)), sds((8, 128))),
        in_specs=[SM, HB, HB, HB],
        out_specs=(VM,) * 3,
        scratch_shapes=[pltpu.VMEM((3, 128), f32), pltpu.VMEM((3, 128), f32), pltpu.SemaphoreType.DMA((3,))],
        compiler_params=small,
        name="prologue",
    )(valid_count, hbm(charges), hbm(source_coords), hbm(target_points))
    recv = lax.all_to_all(zsend, "z", 0, 0, tiled=True)
    recv, tsend = lax.optimization_barrier((recv, tsend))
    targets = lax.all_to_all(tsend, plane, 0, 0, tiled=True)
    interp = sds((NZ * 32, 128), bf16)
    a, ih, il, q, held, far, chunks, count = pl.pallas_call(
        setup_kernel,
        out_shape=(
            sds((ZERO_BLOCK * 128, 128), bf16),
            interp,
            interp,
            sds((ZERO_BLOCK + 1, 16, 128), bf16),
            sds((3, 8, 128)),
            sds((NY, FAR_SLOTS), jnp.int32),
            sds((CHUNK_SLOTS,), jnp.int32),
            sds((1,), jnp.int32),
        ),
        in_specs=[SM, HB, HB, HB, HB, VM],
        out_specs=(VM,) * 5 + (SM,) * 3,
        scratch_shapes=[
            pltpu.VMEM((5, 16, 128), f32),
            pltpu.VMEM((544, 128), bf16),
            pltpu.SMEM((3, NZ * NY * MEMBERS), f32),
            pltpu.SMEM((NEAR, NY * NZ), jnp.int32),
            pltpu.SMEM((8,), f32),
            pltpu.SemaphoreType.DMA((4,)),
        ],
        compiler_params=params,
        cost_estimate=pl.CostEstimate(flops=10**9, bytes_accessed=12 * 10**6, transcendentals=0),
        name="setup",
    )(valid_count, hbm(step_sizes), hbm(leaf_centers), hbm(near_lists.T), hbm(boundary_data), recv)
    scale = 1.0 / math.sqrt(NY * NZ * MEMBERS * 128)
    half = pltpu.VMEM((PAIRS, TILES, 256, TILE), bf16)
    sums, *kernels = pl.pallas_call(
        first_kernel,
        out_shape=(sds((PLANE, 8, 128)), half, half, half, half),
        in_specs=[SM, SM, VM, VM, VM],
        out_specs=(VM,) * 5,
        scratch_shapes=[pltpu.VMEM((NY, DEPTH, MEMBERS * 128), bf16), pltpu.VMEM((NY * 16, MEMBERS * 128), f32)],
        compiler_params=params,
        name="first",
    )(chunks, count, targets, a, q)

    def update(sums, current, last):
        return pl.pallas_call(
            functools.partial(update_kernel, scale, last),
            out_shape=(sds((8, 128)), sds((8, 128) if last else (NZ, 8, 128))),
            in_specs=[VM, VM, VM],
            out_specs=(VM, VM),
            compiler_params=small,
            name="update",
        )(lax.all_to_all(sums, plane, 0, 0, tiled=True), held, current)

    current, zsend = update(sums, current, False)
    recv = lax.all_to_all(zsend, "z", 0, 0, tiled=True)
    sums = pl.pallas_call(
        second_kernel,
        out_shape=sds((PLANE, 8, 128)),
        in_specs=[SM, SM, SM] + [VM] * 7,
        out_specs=VM,
        scratch_shapes=[
            pltpu.VMEM((ZERO_BLOCK + 1, 16, 128), bf16),
            pltpu.VMEM((5, 16, 128), f32),
            pltpu.VMEM((NY * 16, MEMBERS * 128), f32),
        ],
        compiler_params=params,
        name="second",
    )(chunks, count, far, recv, ih, il, *kernels)
    current, residual = update(sums, current, True)
    return (current, residual)


def solution(mesh):
    grid = Mesh(mesh.devices.reshape(NY, NZ, NX, NC), ("y", "z", "x", "core"))
    split = P(None, ("y", "z", "x", "core"))
    in_specs = (P(), split, split, split, split, P(), P(("y", "z", "x", "core")), P())
    return jax.shard_map(body, mesh=grid, in_specs=in_specs, out_specs=(split, split), check_vma=False)
```
